128 devices in a mesh: coil: 4 (over z), slab: 32 (over x, y, core).
Axes of the slice: x: 4, y: 4, z: 4, core: 2. Of those that a mesh axis runs over, the one named last changes fastest.
Arguments:
- image: float32 [2, 256, 256, 128], P(None, 'slab'), may hold values from -6 to 6
- sensitivity: bfloat16 [16, 2, 256, 256, 128], P('coil', None, 'slab'), may hold values from -5 to 5
- blocks: bfloat16 [32, 24, 128, 512], P('slab'), may hold values from -0.25 to 0.25
- samples: bfloat16 [32, 24, 128, 16, 2, 128], P('slab', None, None, 'coil'), may hold values from -6 to 6
- offsets: int32 [32, 24], P('slab'), may hold values from 0 to 192
- counts: int32 [32], P('slab'), may hold values from 1 to 24, as said below
- auxiliary: float32 [2, 256, 256, 128], P(None, 'slab', 'coil'), may hold values from -4 to 4
- scaled_dual: float32 [2, 256, 256, 128], P(None, 'slab', 'coil'), may hold values from -3 to 3
Outputs:
- image_next: float32 [2, 256, 256, 128], P(None, 'slab', 'coil')
- auxiliary_next: float32 [2, 256, 256, 128], P(None, 'slab', 'coil')
- dual_next: float32 [2, 256, 256, 128], P(None, 'slab', 'coil')
The draws below stay inside these ranges and needn't reach their ends.
Inputs may be any that keep to these rules, and one draw needn't show every extreme that they name: Each tile's live groups are its first counts slots; some tile holds 24 live groups.
All inputs are finite; a program needn't handle non-finite values.
Results may differ from the reference program's by a relative error of at most 0.014.
Values may be sent and summed in bfloat16 or wider, within the bound.
No kernel may reach another device: no remote copies, remote signals or barrier semaphores. Data moves between devices by JAX's collectives and lax.ppermute only.
A program may use at most 128 MiB of HBM per device.

```python
import math
import jax
import jax.numpy as jnp
from jax import lax

X = 256
Y = 256
Z = 128
C = 16
WIN = 64
P_SIZE = 128
CH = 24
TILES = 32
KYD = 8
CELLS = 512


def draw_counts(key, part):
    tile = jnp.arange(TILES, dtype=jnp.int32)
    spread = jnp.abs(2 * tile + 1 - TILES)
    profile = jnp.maximum(1, CH * (TILES - spread) // TILES)
    factor = jax.random.randint(jax.random.fold_in(key, 11), (TILES,), 2, 5)
    loads = jnp.clip(profile * factor // 4, 1, CH)
    return jnp.where(tile == TILES // 2, CH, loads).astype(jnp.int32)


def touch_ends(values, rng, smallest, high):
    longest = values.shape.index(max(values.shape))
    spots = []
    for shift in (0, 1):
        where = [jax.random.randint(jax.random.fold_in(rng, axis), (), 0, length) for axis, length in enumerate(values.shape)]
        where[longest] = (where[longest] + shift) % values.shape[longest]
        spots.append(tuple(where))
    return values.at[spots[0]].set(smallest).at[spots[1]].set(high)


def steps_of(stream_key, shape, pieces, low, largest):
    def one(axis_at, blocks):
        steps = jax.random.uniform(jax.random.fold_in(jax.random.fold_in(stream_key, 6), axis_at), (blocks,), jnp.float32, low / len(pieces), largest / len(pieces))
        return jnp.repeat(jnp.exp(steps), shape[axis_at] // blocks).reshape((-1,) + (1,) * (len(shape) - axis_at - 1))

    level = one(*pieces[0])
    for cut in pieces[1:]:
        level = level * one(*cut)
    return level


def scatter_about(own_key, shape, width, most, shards=(), kind=jnp.bfloat16):
    entries = width * jax.random.normal(own_key, shape, jnp.float32)
    if shards:
        entries = entries * steps_of(own_key, shape, shards, -0.22, 0.18)
    return jnp.clip(entries, -most, most).astype(kind)


def setup_inputs(seed: int = 0) -> dict:
    arg_keys = jax.random.split(jax.random.key(seed), 9)
    return {
        "image": scatter_about(arg_keys[0], (2, X, Y, Z), 1.0, 6.0, ((1, 32),), jnp.float32),
        "sensitivity": scatter_about(arg_keys[1], (C, 2, X, Y, Z), 0.7, 5.0, ((0, 4), (2, 32))),
        "blocks": scatter_about(arg_keys[2], (TILES, CH, P_SIZE, CELLS), CELLS ** -0.5, 0.25, ((0, 32),)),
        "samples": scatter_about(arg_keys[3], (TILES, CH, P_SIZE, C, 2, Z), 1.0, 6.0, ((0, 32), (3, 4))),
        "offsets": touch_ends(jax.random.randint(arg_keys[4], (TILES, CH), 0, X - WIN + 1), jax.random.fold_in(arg_keys[4], 1), 0, X - WIN).astype(jnp.int32),
        "counts": draw_counts(jax.random.fold_in(arg_keys[8], 71), 0),
        "auxiliary": scatter_about(arg_keys[6], (2, X, Y, Z), 0.5, 4.0, ((1, 32), (2, 4)), jnp.float32),
        "scaled_dual": scatter_about(arg_keys[7], (2, X, Y, Z), 0.3, 3.0, ((1, 32), (2, 4)), jnp.float32),
    }


step_size = 0.5
penalty = 1.0
threshold = 0.3

def tables(length):
    index = jnp.arange(length, dtype=jnp.int32)
    product = index[:, None] * index[None, :] % length
    angle = product.astype(jnp.float32) * (2.0 * math.pi / length)
    factor = 1.0 / math.sqrt(length)
    return ((jnp.cos(angle) * factor).astype(jnp.bfloat16), (-jnp.sin(angle) * factor).astype(jnp.bfloat16))

def complex_apply(form, table_re, table_im, real, imag, inverse):

    def apply(table, values):
        return jnp.einsum(form, table.astype(jnp.float32), values.astype(jnp.float32), precision=lax.Precision.HIGHEST)
    if inverse:
        return (apply(table_re, real) + apply(table_im, imag), apply(table_re, imag) - apply(table_im, real))
    return (apply(table_re, real) - apply(table_im, imag), apply(table_im, real) + apply(table_re, imag))

def haar(values):
    parts, rows, cols, depth = values.shape
    blocked = values.reshape(parts, rows // 2, 2, cols // 2, 2, depth)
    first = blocked[:, :, 0, :, 0]
    second = blocked[:, :, 0, :, 1]
    third = blocked[:, :, 1, :, 0]
    fourth = blocked[:, :, 1, :, 1]
    upper = jnp.stack([(first + second + third + fourth) * 0.5, (first - second + third - fourth) * 0.5], axis=3)
    lower = jnp.stack([(first + second - third - fourth) * 0.5, (first - second - third + fourth) * 0.5], axis=3)
    return jnp.stack([upper, lower], axis=2).reshape(parts, rows, cols, depth)

def admm_update(current, gradient, auxiliary, scaled_dual):
    target = haar(auxiliary - scaled_dual)
    image_next = current - step_size * (gradient + penalty * (current - target))
    coeffs = haar(image_next) + scaled_dual
    magnitude = jnp.sqrt(coeffs[0] * coeffs[0] + coeffs[1] * coeffs[1])
    factor = jnp.maximum(1.0 - threshold / jnp.maximum(magnitude, threshold), 0.0)
    auxiliary_next = coeffs * factor
    return (image_next, auxiliary_next, coeffs - auxiliary_next)

def reference(image, sensitivity, blocks, samples, offsets, counts, auxiliary, scaled_dual):
    y_re, y_im = tables(Y)
    x_re, x_im = tables(X)

    def coil_kspace(coil_index):
        sens_re = sensitivity[coil_index, 0].astype(jnp.float32)
        sens_im = sensitivity[coil_index, 1].astype(jnp.float32)
        coil_re = (sens_re * image[0] - sens_im * image[1]).astype(jnp.bfloat16)
        coil_im = (sens_re * image[1] + sens_im * image[0]).astype(jnp.bfloat16)
        half_re, half_im = complex_apply('kn,xnz->xkz', y_re, y_im, coil_re, coil_im, False)
        half_re = half_re.astype(jnp.bfloat16)
        half_im = half_im.astype(jnp.bfloat16)
        out_re, out_im = complex_apply('kn,nyz->kyz', x_re, x_im, half_re, half_im, False)
        return jnp.stack([out_re, out_im]).astype(jnp.bfloat16)
    kspace = lax.map(coil_kspace, jnp.arange(C, dtype=jnp.int32))
    kspace = jnp.transpose(kspace, (2, 3, 0, 1, 4))
    columns = C * 2 * Z

    def grid_tile(tile):
        local = lax.dynamic_slice_in_dim(kspace, tile * KYD, KYD, 1)

        def grid_step(slot, total):
            start = offsets[tile, slot]
            window = lax.dynamic_slice_in_dim(local, start, WIN, 0).reshape(CELLS, columns)
            block = blocks[tile, slot]
            predicted = jnp.dot(block, window, preferred_element_type=jnp.float32)
            misfit = (predicted - samples[tile, slot].reshape(P_SIZE, columns).astype(jnp.float32)).astype(jnp.bfloat16)
            update = jnp.dot(block.T, misfit, preferred_element_type=jnp.float32).reshape(WIN, KYD, C, 2, Z)
            current = lax.dynamic_slice_in_dim(total, start, WIN, 0)
            return lax.dynamic_update_slice_in_dim(total, current + update, start, 0)
        total = lax.fori_loop(0, counts[tile], grid_step, jnp.zeros((X, KYD, C, 2, Z), jnp.float32))
        return total.astype(jnp.bfloat16)
    gridded = lax.map(grid_tile, jnp.arange(TILES, dtype=jnp.int32))
    gridded = jnp.transpose(gridded, (1, 0, 2, 3, 4, 5)).reshape(X, Y, C, 2, Z)

    def combine(total, coil_index):
        piece = lax.dynamic_index_in_dim(gridded, coil_index, 2, keepdims=False)
        back_re, back_im = complex_apply('kn,kyz->nyz', x_re, x_im, piece[:, :, 0], piece[:, :, 1], True)
        back_re = back_re.astype(jnp.bfloat16)
        back_im = back_im.astype(jnp.bfloat16)
        adj_re, adj_im = complex_apply('kn,xkz->xnz', y_re, y_im, back_re, back_im, True)
        adj_re = adj_re.astype(jnp.bfloat16).astype(jnp.float32)
        adj_im = adj_im.astype(jnp.bfloat16).astype(jnp.float32)
        sens_re = sensitivity[coil_index, 0].astype(jnp.float32)
        sens_im = sensitivity[coil_index, 1].astype(jnp.float32)
        term = jnp.stack([sens_re * adj_re + sens_im * adj_im, sens_re * adj_im - sens_im * adj_re])
        return (total + term, 0)
    gradient, unused = lax.scan(combine, jnp.zeros((2, X, Y, Z), jnp.float32), jnp.arange(C, dtype=jnp.int32))
    return admm_update(image, gradient, auxiliary, scaled_dual)
```

```python
import math

import jax
import jax.numpy as jnp
import numpy as np
import ml_dtypes
from jax import lax
from jax.experimental import pallas as pl
from jax.experimental.pallas import tpu as pltpu
from jax.sharding import PartitionSpec as P

N = 256
Z = 128
WIN = 64
P_SIZE = 128
CH = 24
KYD = 8
TILES = 32
CELLS = WIN * KYD
ROWS = N * KYD
NCOIL = 4

step_size = 0.5
penalty = 1.0
threshold = 0.3

BF = jnp.bfloat16
F32 = jnp.float32


def dft_parts():
    index = np.arange(N)
    angle = (index[:, None] * index[None, :] % N).astype(np.float32) * np.float32(2.0 * math.pi / N)
    factor = np.float32(1.0 / math.sqrt(N))
    re = (np.cos(angle) * factor).astype(ml_dtypes.bfloat16)
    im = (-np.sin(angle) * factor).astype(ml_dtypes.bfloat16)
    return re, im


def real_tables():
    re, im = dft_parts()
    along_y = np.stack(
        [np.concatenate([re, -im], 1), np.concatenate([im, re], 1)], 1
    ).reshape(2 * N, 2 * N)
    re_c = re.reshape(N, TILES, KYD)
    im_c = im.reshape(N, TILES, KYD)
    along_x = np.stack(
        [np.stack([re_c, -im_c], 2), np.stack([im_c, re_c], 2)], 0
    ).reshape(2 * N, 2 * N)
    return along_y, along_x


def coil_kernel(table_ref, sens_ref, image_ref, out_ref, spread):
    step = pl.program_id(0)
    parts = []
    for i in range(2):
        s_re = sens_ref[0, 0, i].astype(F32)
        s_im = sens_ref[0, 1, i].astype(F32)
        m_re = image_ref[0, i]
        m_im = image_ref[1, i]
        c_re = (s_re * m_re - s_im * m_im).astype(BF)
        c_im = (s_re * m_im + s_im * m_re).astype(BF)
        parts.append(jnp.concatenate([c_re, c_im], 0))
    data = jnp.concatenate(parts, 1)
    result = jnp.dot(table_ref[...], data, preferred_element_type=F32)
    for i in range(2):
        spread[pl.ds(2 * step + i, 2 * N, stride=KYD), :] = result[:, i * Z : (i + 1) * Z]

    @pl.when(step == 3)
    def _():
        out_ref[...] = spread[...].astype(BF)


def coil_forward(coil, table, sensitivity, image):
    return pl.pallas_call(
        coil_kernel,
        out_shape=jax.ShapeDtypeStruct((TILES * 128, Z), BF),
        grid=(4,),
        in_specs=[
            pl.BlockSpec((2 * N, 2 * N), lambda i: (0, 0)),
            pl.BlockSpec((1, 2, 2, N, Z), lambda i: (coil, 0, i, 0, 0)),
            pl.BlockSpec((2, 2, N, Z), lambda i: (0, i, 0, 0)),
        ],
        out_specs=pl.BlockSpec((TILES * 128, Z), lambda i: (0, 0)),
        scratch_shapes=[pltpu.VMEM((TILES * 128, Z), F32)],
        compiler_params=pltpu.CompilerParams(vmem_limit_bytes=32 << 20),
        name=f"coil_forward_{coil}",
    )(table, sensitivity, image)


def grid_kernel(
    coil,
    offsets_ref,
    counts_ref,
    piece_ref,
    forward_ref,
    inverse_ref,
    blocks_hbm,
    turned_hbm,
    samples_hbm,
    out_ref,
    blocks,
    turned,
    samples,
    cells,
    window,
    total,
    sems,
):
    count = counts_ref[0]

    def copies(j):
        return (
            pltpu.make_async_copy(blocks_hbm.at[j], blocks.at[j], sems.at[0, j]),
            pltpu.make_async_copy(turned_hbm.at[j], turned.at[j], sems.at[1, j]),
            pltpu.make_async_copy(samples_hbm.at[coil, j], samples.at[j], sems.at[2, j]),
        )

    def start(j, carry):
        for copy in copies(j):
            copy.start()
        return carry

    lax.fori_loop(0, count, start, 0)

    for pair in range(KYD // 2):
        data = jnp.concatenate(
            [piece_ref[:, 2 * pair + i].reshape(2 * N, Z) for i in range(2)], 1
        )
        result = jnp.dot(forward_ref[...], data, preferred_element_type=F32)
        for i in range(2):
            for part in range(2):
                cells[part, pl.ds(2 * pair + i, N, stride=KYD), :] = result[
                    part * N : (part + 1) * N, i * Z : (i + 1) * Z
                ]
    for part in range(2):
        cells[part, ROWS : ROWS + KYD, :] = jnp.zeros((KYD, Z), F32)
        window[0, :, part * Z : (part + 1) * Z] = cells[part, 0:ROWS, :].astype(BF)
        window[1, :, part * Z : (part + 1) * Z] = cells[part, KYD : ROWS + KYD, :].astype(BF)
    total[...] = jnp.zeros_like(total)

    def group(j, carry):
        for copy in copies(j):
            copy.wait()
        first = offsets_ref[0, j]
        row = pl.multiple_of((first // 2) * (2 * KYD), 2 * KYD)
        view = window[first % 2, pl.ds(row, CELLS), :]
        predicted = jnp.dot(blocks[j], view, preferred_element_type=F32)
        misfit = (predicted - samples[j].astype(F32)).astype(BF)
        update = jnp.dot(turned[j], misfit, preferred_element_type=F32)
        spot = pl.ds(pl.multiple_of(first * KYD, KYD), CELLS)
        for part in range(2):
            total[part, spot, :] = total[part, spot, :] + update[:, part * Z : (part + 1) * Z]
        return carry

    lax.fori_loop(0, count, group, 0)

    for pair in range(KYD // 2):
        sides = []
        for i in range(2):
            ky = 2 * pair + i
            sides.append(
                jnp.concatenate(
                    [
                        total[part, pl.ds(ky, N, stride=KYD), :].astype(BF)
                        for part in range(2)
                    ],
                    0,
                )
            )
        data = jnp.concatenate(sides, 1)
        result = jnp.dot(inverse_ref[...], data, preferred_element_type=F32).astype(BF)
        for i in range(2):
            out_ref[:, 2 * pair + i] = result[:, i * Z : (i + 1) * Z].reshape(TILES, 16, Z)


def grid_tile(coil, offsets, counts, piece, forward, inverse, blocks, turned, samples):
    vmem = pl.BlockSpec(memory_space=pltpu.VMEM)
    smem = pl.BlockSpec(memory_space=pltpu.SMEM)
    hbm = pl.BlockSpec(memory_space=pl.ANY)

    def kernel(*refs):
        grid_kernel(coil, *refs)

    return pl.pallas_call(
        kernel,
        out_shape=jax.ShapeDtypeStruct((TILES, KYD, 16, Z), BF),
        in_specs=[smem, smem, vmem, vmem, vmem, hbm, hbm, hbm],
        out_specs=vmem,
        scratch_shapes=[
            pltpu.VMEM((CH, P_SIZE, CELLS), BF),
            pltpu.VMEM((CH, CELLS, P_SIZE), BF),
            pltpu.VMEM((CH, P_SIZE, 2 * Z), BF),
            pltpu.VMEM((2, ROWS + KYD, Z), F32),
            pltpu.VMEM((2, ROWS, 2 * Z), BF),
            pltpu.VMEM((2, ROWS, Z), F32),
            pltpu.SemaphoreType.DMA((3, CH)),
        ],
        compiler_params=pltpu.CompilerParams(vmem_limit_bytes=48 << 20),
        name=f"grid_tile_{coil}",
    )(offsets, counts, piece, forward, inverse, blocks, turned, samples)


def gradient_kernel(first, last, table_ref, piece_ref, sens_ref, *rest):
    if first:
        (out_ref, spread) = rest
    else:
        (before_ref, out_ref, spread) = rest
    step = pl.program_id(0)

    @pl.when(step == 0)
    def _():
        spread[...] = piece_ref[...].astype(F32)

    data = jnp.concatenate(
        [spread[pl.ds(2 * step + i, 2 * N, stride=KYD), :].astype(BF) for i in range(2)], 1
    )
    result = jnp.dot(table_ref[...], data, preferred_element_type=F32).astype(BF).astype(F32)
    for i in range(2):
        a_re = result[:N, i * Z : (i + 1) * Z]
        a_im = result[N:, i * Z : (i + 1) * Z]
        s_re = sens_ref[0, 0, i].astype(F32)
        s_im = sens_ref[0, 1, i].astype(F32)
        g_re = s_re * a_re + s_im * a_im
        g_im = s_re * a_im - s_im * a_re
        if not first:
            g_re = g_re + before_ref[0, i]
            g_im = g_im + before_ref[1, i]
        if last:
            out_ref[:, 0, i] = g_re.astype(BF).reshape(NCOIL, N // NCOIL, Z)
            out_ref[:, 1, i] = g_im.astype(BF).reshape(NCOIL, N // NCOIL, Z)
        else:
            out_ref[0, i] = g_re
            out_ref[1, i] = g_im


def gradient_step(coil, table, piece, sensitivity, before):
    first = before is None
    last = coil == NCOIL - 1
    whole = pl.BlockSpec((2, 2, N, Z), lambda i: (0, i, 0, 0))
    if last:
        out_shape = jax.ShapeDtypeStruct((NCOIL, 2, KYD, N // NCOIL, Z), BF)
        out_spec = pl.BlockSpec((NCOIL, 2, 2, N // NCOIL, Z), lambda i: (0, 0, i, 0, 0))
    else:
        out_shape = jax.ShapeDtypeStruct((2, KYD, N, Z), F32)
        out_spec = whole

    def kernel(*refs):
        gradient_kernel(first, last, *refs)

    return pl.pallas_call(
        kernel,
        out_shape=out_shape,
        grid=(4,),
        in_specs=[
            pl.BlockSpec((2 * N, 2 * N), lambda i: (0, 0)),
            pl.BlockSpec((TILES * 128, Z), lambda i: (0, 0)),
            pl.BlockSpec((1, 2, 2, N, Z), lambda i: (coil, 0, i, 0, 0)),
        ]
        + ([] if first else [whole]),
        out_specs=out_spec,
        scratch_shapes=[pltpu.VMEM((TILES * 128, Z), F32)],
        compiler_params=pltpu.CompilerParams(vmem_limit_bytes=32 << 20),
        name=f"gradient_{coil}",
    )(*([table, piece, sensitivity] + ([] if first else [before])))


def haar_rows(top, low):
    add = (top + low) * 0.5
    sub = (top - low) * 0.5
    cols = top.shape[0]
    odd = lax.broadcasted_iota(jnp.int32, top.shape, 0) % 2 == 1

    def pairs(v):
        ahead = pltpu.roll(v, cols - 1, 0)
        behind = pltpu.roll(v, 1, 0)
        return jnp.where(odd, behind - v, v + ahead)

    return pairs(add), pairs(sub)


def target_kernel(image_ref, aux_ref, dual_ref, out_ref):
    for part in range(2):
        for m in range(KYD // 2):
            rows = haar_rows(
                aux_ref[part, 2 * m] - dual_ref[part, 2 * m],
                aux_ref[part, 2 * m + 1] - dual_ref[part, 2 * m + 1],
            )
            for i in range(2):
                current = image_ref[part, 2 * m + i]
                out_ref[part, 2 * m + i] = current - step_size * penalty * (current - rows[i])


def target_step(position, image, auxiliary, scaled_dual):
    vmem = pl.BlockSpec((2, KYD, N // NCOIL, Z), lambda i, s: (0, 0, 0, 0))
    return pl.pallas_call(
        lambda s, *refs: target_kernel(*refs),
        out_shape=jax.ShapeDtypeStruct(auxiliary.shape, F32),
        grid_spec=pltpu.PrefetchScalarGridSpec(
            num_scalar_prefetch=1,
            grid=(1,),
            in_specs=[
                pl.BlockSpec((2, KYD, N // NCOIL, Z), lambda i, s: (0, 0, s[0], 0)),
                vmem,
                vmem,
            ],
            out_specs=vmem,
        ),
        name="target",
    )(position, image, auxiliary, scaled_dual)


def update_kernel(base_ref, pieces_ref, dual_ref, image_out, aux_out, dual_out):
    for m in range(KYD // 2):
        coeffs = []
        for part in range(2):
            rows = []
            for i in range(2):
                x = 2 * m + i
                gradient = pieces_ref[0, part, x].astype(F32)
                for k in range(1, NCOIL):
                    gradient = gradient + pieces_ref[k, part, x].astype(F32)
                value = base_ref[part, x] - step_size * gradient
                image_out[part, x] = value
                rows.append(value)
            top, low = haar_rows(*rows)
            coeffs.append((top + dual_ref[part, 2 * m], low + dual_ref[part, 2 * m + 1]))
        for i in range(2):
            x = 2 * m + i
            c_re = coeffs[0][i]
            c_im = coeffs[1][i]
            magnitude = jnp.sqrt(c_re * c_re + c_im * c_im)
            factor = jnp.maximum(1.0 - threshold / jnp.maximum(magnitude, threshold), 0.0)
            for part, c in enumerate((c_re, c_im)):
                kept = c * factor
                aux_out[part, x] = kept
                dual_out[part, x] = c - kept


def update_step(base, pieces, scaled_dual):
    vmem = pl.BlockSpec(memory_space=pltpu.VMEM)
    shape = jax.ShapeDtypeStruct(scaled_dual.shape, F32)
    return pl.pallas_call(
        update_kernel,
        out_shape=(shape, shape, shape),
        in_specs=[vmem, vmem, vmem],
        out_specs=(vmem, vmem, vmem),
        name="update",
    )(base, pieces, scaled_dual)


def body(image, sensitivity, blocks, samples, offsets, counts, auxiliary, scaled_dual):
    along_y, along_x = real_tables()
    y_forward = jnp.asarray(along_y)
    y_inverse = jnp.asarray(np.ascontiguousarray(along_y.T))
    x_forward = jnp.asarray(along_x)
    x_inverse = jnp.asarray(np.ascontiguousarray(along_x.T))

    turned = jnp.swapaxes(blocks[0], 1, 2)
    by_coil = jnp.transpose(samples[0], (2, 0, 1, 3, 4)).reshape(NCOIL, CH, P_SIZE, 2 * Z)

    pieces = []
    for coil in range(NCOIL):
        half = coil_forward(coil, y_forward, sensitivity, image).reshape(TILES, KYD, 16, Z)
        pieces.append(lax.all_to_all(half, "slab", 0, 0, tiled=True))
    position = lax.axis_index("coil").reshape(1)
    base = target_step(position, image, auxiliary, scaled_dual)
    backs = []
    for coil in range(NCOIL):
        back = grid_tile(
            coil, offsets, counts, pieces[coil], x_forward, x_inverse, blocks[0], turned, by_coil
        )
        backs.append(lax.all_to_all(back, "slab", 0, 0, tiled=True))
    total = None
    for coil in range(NCOIL):
        total = gradient_step(coil, y_inverse, backs[coil].reshape(TILES * 128, Z), sensitivity, total)
    shares = lax.all_to_all(total, "coil", 0, 0, tiled=True)
    return update_step(base, shares, scaled_dual)


def solution(mesh):
    return jax.shard_map(
        body,
        mesh=mesh,
        in_specs=(
            P(None, "slab", None, None),
            P("coil", None, "slab", None, None),
            P("slab", None, None, None),
            P("slab", None, None, "coil", None, None),
            P("slab", None),
            P("slab"),
            P(None, "slab", "coil", None),
            P(None, "slab", "coil", None),
        ),
        out_specs=(
            P(None, "slab", "coil", None),
            P(None, "slab", "coil", None),
            P(None, "slab", "coil", None),
        ),
        check_vma=False,
    )
```

```python
import math

import jax
import jax.numpy as jnp
import numpy as np
import ml_dtypes
from jax import lax
from jax.experimental import pallas as pl
from jax.experimental.pallas import tpu as pltpu
from jax.sharding import PartitionSpec as P

N = 256
Z = 128
WIN = 64
P_SIZE = 128
CH = 24
KYD = 8
TILES = 32
CELLS = WIN * KYD
ROWS = N * KYD
NCOIL = 4
PER = 2

step_size = 0.5
penalty = 1.0
threshold = 0.3

BF = jnp.bfloat16
F32 = jnp.float32


def dft_parts():
    index = np.arange(N)
    angle = (index[:, None] * index[None, :] % N).astype(np.float32) * np.float32(2.0 * math.pi / N)
    factor = np.float32(1.0 / math.sqrt(N))
    re = (np.cos(angle) * factor).astype(ml_dtypes.bfloat16)
    im = (-np.sin(angle) * factor).astype(ml_dtypes.bfloat16)
    return re, im


def real_tables():
    re, im = dft_parts()
    along_y = np.stack(
        [np.concatenate([re, -im], 1), np.concatenate([im, re], 1)], 1
    ).reshape(2 * N, 2 * N)
    re_c = re.reshape(N, TILES, KYD)
    im_c = im.reshape(N, TILES, KYD)
    along_x = np.stack(
        [np.stack([re_c, -im_c], 2), np.stack([im_c, re_c], 2)], 0
    ).reshape(2 * N, 2 * N)
    return along_y, along_x


def hbm(shape, dtype):
    return pltpu.HBM(shape, dtype)


def in_hbm(x):
    return pltpu.with_memory_space_constraint(x, pltpu.HBM)


def coil_kernel(table_ref, sens_ref, image_ref, out_ref, spread):
    step = pl.program_id(1)
    parts = []
    for i in range(2):
        s_re = sens_ref[0, 0, i].astype(F32)
        s_im = sens_ref[0, 1, i].astype(F32)
        m_re = image_ref[0, i]
        m_im = image_ref[1, i]
        c_re = (s_re * m_re - s_im * m_im).astype(BF)
        c_im = (s_re * m_im + s_im * m_re).astype(BF)
        parts.append(jnp.concatenate([c_re, c_im], 0))
    data = jnp.concatenate(parts, 1)
    result = jnp.dot(table_ref[...], data, preferred_element_type=F32)
    for i in range(2):
        spread[pl.ds(2 * step + i, 2 * N, stride=KYD), :] = result[:, i * Z : (i + 1) * Z]

    @pl.when(step == 3)
    def _():
        out_ref[:, 0] = spread[...].astype(BF).reshape(TILES, 128, Z)


def coil_forward(chunk, table, sensitivity, image):
    first = chunk * PER
    return pl.pallas_call(
        coil_kernel,
        out_shape=hbm((TILES, PER, 128, Z), BF),
        grid=(PER, 4),
        in_specs=[
            pl.BlockSpec((2 * N, 2 * N), lambda c, i: (0, 0)),
            pl.BlockSpec((1, 2, 2, N, Z), lambda c, i: (first + c, 0, i, 0, 0)),
            pl.BlockSpec((2, 2, N, Z), lambda c, i: (0, i, 0, 0)),
        ],
        out_specs=pl.BlockSpec((TILES, 1, 128, Z), lambda c, i: (0, c, 0, 0)),
        scratch_shapes=[pltpu.VMEM((TILES * 128, Z), F32)],
        compiler_params=pltpu.CompilerParams(vmem_limit_bytes=32 << 20),
        name=f"coil_forward_{chunk}",
    )(table, sensitivity, image)


def samples_kernel(counts_ref, samples_ref, out_ref, spread):
    @pl.when(pl.program_id(0) < counts_ref[0])
    def _():
        spread[...] = samples_ref[0].astype(F32).reshape(P_SIZE * 8, Z)
        for coil in range(NCOIL):
            for part in range(2):
                out_ref[coil, 0, :, part * Z : (part + 1) * Z] = spread[
                    pl.ds(2 * coil + part, P_SIZE, stride=8), :
                ].astype(BF)


def samples_by_coil(counts, samples):
    last = lambda i, n: jnp.minimum(i, n[0] - 1)
    return pl.pallas_call(
        samples_kernel,
        out_shape=hbm((NCOIL, CH, P_SIZE, 2 * Z), BF),
        grid_spec=pltpu.PrefetchScalarGridSpec(
            num_scalar_prefetch=1,
            grid=(CH,),
            in_specs=[pl.BlockSpec((1, P_SIZE, 8, Z), lambda i, n: (last(i, n), 0, 0, 0))],
            out_specs=pl.BlockSpec((NCOIL, 1, P_SIZE, 2 * Z), lambda i, n: (0, last(i, n), 0, 0)),
            scratch_shapes=[pltpu.VMEM((P_SIZE * 8, Z), F32)],
        ),
        name="samples_by_coil",
    )(counts, samples)


def grid_kernel(
    chunk,
    offsets_ref,
    counts_ref,
    piece_ref,
    forward_ref,
    inverse_ref,
    blocks_hbm,
    turned_hbm,
    samples_hbm,
    out_ref,
    blocks,
    turned,
    samples,
    cells,
    window,
    total,
    sems,
):
    count = counts_ref[0]

    def copies(j):
        return [
            pltpu.make_async_copy(blocks_hbm.at[j], blocks.at[j], sems.at[0, j]),
            pltpu.make_async_copy(turned_hbm.at[j], turned.at[j], sems.at[1, j]),
        ] + [
            pltpu.make_async_copy(
                samples_hbm.at[chunk * PER + c, j],
                samples.at[j, :, pl.ds(2 * Z * c, 2 * Z)],
                sems.at[2 + c, j],
            )
            for c in range(PER)
        ]

    def start(j, carry):
        for copy in copies(j):
            copy.start()
        return carry

    lax.fori_loop(0, count, start, 0)

    for ky in range(KYD):
        data = jnp.concatenate(
            [piece_ref[:, c, ky].reshape(2 * N, Z) for c in range(PER)], 1
        )
        result = jnp.dot(forward_ref[...], data, preferred_element_type=F32)
        for c in range(PER):
            for part in range(2):
                cells[2 * c + part, pl.ds(ky, N, stride=KYD), :] = result[
                    part * N : (part + 1) * N, c * Z : (c + 1) * Z
                ]
    for s in range(2 * PER):
        lanes = slice(s * Z, (s + 1) * Z)
        cells[s, ROWS : ROWS + KYD, :] = jnp.zeros((KYD, Z), F32)
        window[0, :, lanes] = cells[s, 0:ROWS, :].astype(BF)
        window[1, :, lanes] = cells[s, KYD : ROWS + KYD, :].astype(BF)
    total[...] = jnp.zeros_like(total)

    def arrive(j):
        for copy in copies(j):
            copy.wait()

    def predict(j):
        first = offsets_ref[0, j]
        row = pl.multiple_of((first // 2) * (2 * KYD), 2 * KYD)
        view = window[first % 2, pl.ds(row, CELLS), :]
        predicted = jnp.dot(blocks[j], view, preferred_element_type=F32)
        return (predicted - samples[j].astype(F32)).astype(BF)

    def add_back(j, misfit):
        update = jnp.dot(turned[j], misfit, preferred_element_type=F32)
        spot = pl.ds(pl.multiple_of(offsets_ref[0, j] * KYD, KYD), CELLS)
        for s in range(2 * PER):
            total[s, spot, :] = total[s, spot, :] + update[:, s * Z : (s + 1) * Z]

    arrive(0)
    samples[0] = predict(0)

    def group(j, carry):
        arrive(j)
        before = samples[j - 1]
        misfit = predict(j)
        add_back(j - 1, before)
        samples[j] = misfit
        return carry

    lax.fori_loop(1, count, group, 0)
    add_back(count - 1, samples[count - 1])

    for ky in range(KYD):
        data = jnp.concatenate(
            [
                jnp.concatenate(
                    [
                        total[2 * c + part, pl.ds(ky, N, stride=KYD), :].astype(BF)
                        for part in range(2)
                    ],
                    0,
                )
                for c in range(PER)
            ],
            1,
        )
        result = jnp.dot(inverse_ref[...], data, preferred_element_type=F32).astype(BF)
        for c in range(PER):
            out_ref[:, c, ky] = result[:, c * Z : (c + 1) * Z].reshape(TILES, 16, Z)


def grid_tile(chunk, offsets, counts, piece, forward, inverse, blocks, turned, samples):
    vmem = pl.BlockSpec(memory_space=pltpu.VMEM)
    smem = pl.BlockSpec(memory_space=pltpu.SMEM)
    far = pl.BlockSpec(memory_space=pltpu.HBM)

    def kernel(*refs):
        grid_kernel(chunk, *refs)

    return pl.pallas_call(
        kernel,
        out_shape=jax.ShapeDtypeStruct((TILES, PER, KYD, 16, Z), BF),
        in_specs=[smem, smem, vmem, vmem, vmem, far, far, far],
        out_specs=vmem,
        scratch_shapes=[
            pltpu.VMEM((CH, P_SIZE, CELLS), BF),
            pltpu.VMEM((CH, CELLS, P_SIZE), BF),
            pltpu.VMEM((CH, P_SIZE, 2 * Z * PER), BF),
            pltpu.VMEM((2 * PER, ROWS + KYD, Z), F32),
            pltpu.VMEM((2, ROWS, 2 * Z * PER), BF),
            pltpu.VMEM((2 * PER, ROWS, Z), F32),
            pltpu.SemaphoreType.DMA((2 + PER, CH)),
        ],
        compiler_params=pltpu.CompilerParams(vmem_limit_bytes=48 << 20),
        name=f"grid_tile_{chunk}",
    )(offsets, counts, piece, forward, inverse, blocks, turned, samples)


def gradient_kernel(first, last, table_ref, piece_ref, sens_ref, *rest):
    if first:
        (out_ref, spread) = rest
    else:
        (before_ref, out_ref, spread) = rest
    step = pl.program_id(0)

    @pl.when(step == 0)
    def _():
        for c in range(PER):
            spread[c] = piece_ref[:, c].astype(F32).reshape(TILES * 128, Z)

    data = jnp.concatenate(
        [
            spread[c, pl.ds(2 * step + i, 2 * N, stride=KYD), :].astype(BF)
            for c in range(PER)
            for i in range(2)
        ],
        1,
    )
    result = jnp.dot(table_ref[...], data, preferred_element_type=F32).astype(BF).astype(F32)
    for i in range(2):
        g_re = None if first else before_ref[0, i]
        g_im = None if first else before_ref[1, i]
        for c in range(PER):
            lanes = slice((2 * c + i) * Z, (2 * c + i + 1) * Z)
            a_re = result[:N, lanes]
            a_im = result[N:, lanes]
            s_re = sens_ref[c, 0, i].astype(F32)
            s_im = sens_ref[c, 1, i].astype(F32)
            t_re = s_re * a_re + s_im * a_im
            t_im = s_re * a_im - s_im * a_re
            g_re = t_re if g_re is None else g_re + t_re
            g_im = t_im if g_im is None else g_im + t_im
        if last:
            out_ref[:, 0, i] = g_re.astype(BF).reshape(NCOIL, N // NCOIL, Z)
            out_ref[:, 1, i] = g_im.astype(BF).reshape(NCOIL, N // NCOIL, Z)
        else:
            out_ref[0, i] = g_re
            out_ref[1, i] = g_im


def gradient_step(chunk, table, piece, sensitivity, before):
    first = before is None
    last = chunk == NCOIL // PER - 1
    whole = pl.BlockSpec((2, 2, N, Z), lambda i: (0, i, 0, 0))
    if last:
        out_shape = hbm((NCOIL, 2, KYD, N // NCOIL, Z), BF)
        out_spec = pl.BlockSpec((NCOIL, 2, 2, N // NCOIL, Z), lambda i: (0, 0, i, 0, 0))
    else:
        out_shape = hbm((2, KYD, N, Z), F32)
        out_spec = whole

    def kernel(*refs):
        gradient_kernel(first, last, *refs)

    return pl.pallas_call(
        kernel,
        out_shape=out_shape,
        grid=(4,),
        in_specs=[
            pl.BlockSpec((2 * N, 2 * N), lambda i: (0, 0)),
            pl.BlockSpec((TILES, PER, 128, Z), lambda i: (0, 0, 0, 0)),
            pl.BlockSpec((PER, 2, 2, N, Z), lambda i: (chunk, 0, i, 0, 0)),
        ]
        + ([] if first else [whole]),
        out_specs=out_spec,
        scratch_shapes=[pltpu.VMEM((PER, TILES * 128, Z), F32)],
        compiler_params=pltpu.CompilerParams(vmem_limit_bytes=32 << 20),
        name=f"gradient_{chunk}",
    )(*([table, piece, sensitivity] + ([] if first else [before])))


def haar_rows(top, low):
    add = (top + low) * 0.5
    sub = (top - low) * 0.5
    cols = top.shape[0]
    odd = lax.broadcasted_iota(jnp.int32, top.shape, 0) % 2 == 1

    def pairs(v):
        ahead = pltpu.roll(v, cols - 1, 0)
        behind = pltpu.roll(v, 1, 0)
        return jnp.where(odd, behind - v, v + ahead)

    return pairs(add), pairs(sub)


def target_kernel(image_ref, aux_ref, dual_ref, out_ref):
    for part in range(2):
        rows = haar_rows(
            aux_ref[part, 0] - dual_ref[part, 0],
            aux_ref[part, 1] - dual_ref[part, 1],
        )
        for i in range(2):
            current = image_ref[part, i]
            out_ref[part, i] = current - step_size * penalty * (current - rows[i])


def target_step(position, image, auxiliary, scaled_dual):
    pair = pl.BlockSpec((2, 2, N // NCOIL, Z), lambda i, s: (0, i, 0, 0))
    return pl.pallas_call(
        lambda s, *refs: target_kernel(*refs),
        out_shape=hbm(auxiliary.shape, F32),
        grid_spec=pltpu.PrefetchScalarGridSpec(
            num_scalar_prefetch=1,
            grid=(KYD // 2,),
            in_specs=[
                pl.BlockSpec((2, 2, N // NCOIL, Z), lambda i, s: (0, i, s[0], 0)),
                pair,
                pair,
            ],
            out_specs=pair,
        ),
        name="target",
    )(position, image, auxiliary, scaled_dual)


def update_kernel(base_ref, pieces_ref, dual_ref, image_out, aux_out, dual_out):
    coeffs = []
    for part in range(2):
        rows = []
        for x in range(2):
            gradient = pieces_ref[0, part, x].astype(F32)
            for k in range(1, NCOIL):
                gradient = gradient + pieces_ref[k, part, x].astype(F32)
            value = base_ref[part, x] - step_size * gradient
            image_out[part, x] = value
            rows.append(value)
        top, low = haar_rows(*rows)
        coeffs.append((top + dual_ref[part, 0], low + dual_ref[part, 1]))
    for x in range(2):
        c_re = coeffs[0][x]
        c_im = coeffs[1][x]
        magnitude = jnp.sqrt(c_re * c_re + c_im * c_im)
        factor = jnp.maximum(1.0 - threshold / jnp.maximum(magnitude, threshold), 0.0)
        for part, c in enumerate((c_re, c_im)):
            kept = c * factor
            aux_out[part, x] = kept
            dual_out[part, x] = c - kept


def update_step(base, pieces, scaled_dual):
    pair = pl.BlockSpec((2, 2, N // NCOIL, Z), lambda i: (0, i, 0, 0))
    shape = hbm(scaled_dual.shape, F32)
    return pl.pallas_call(
        update_kernel,
        out_shape=(shape, shape, shape),
        grid=(KYD // 2,),
        in_specs=[
            pair,
            pl.BlockSpec((NCOIL, 2, 2, N // NCOIL, Z), lambda i: (0, 0, i, 0, 0)),
            pair,
        ],
        out_specs=(pair, pair, pair),
        name="update",
    )(base, pieces, scaled_dual)


def body(image, sensitivity, blocks, samples, offsets, counts, auxiliary, scaled_dual):
    along_y, along_x = real_tables()
    y_forward, x_forward = lax.optimization_barrier((jnp.asarray(along_y), jnp.asarray(along_x)))
    y_inverse = y_forward.T
    x_inverse = x_forward.T

    image, sensitivity, auxiliary, scaled_dual = (
        in_hbm(v) for v in (image, sensitivity, auxiliary, scaled_dual)
    )
    turned = jnp.swapaxes(blocks[0], 1, 2)
    by_coil = samples_by_coil(counts, in_hbm(samples.reshape(CH, P_SIZE, 2 * NCOIL, Z)))

    chunks = range(NCOIL // PER)
    pieces = []
    for chunk in chunks:
        half = coil_forward(chunk, in_hbm(y_forward), sensitivity, image)
        piece = lax.all_to_all(half, "slab", 0, 0, tiled=True)
        pieces.append(piece.reshape(TILES, PER, KYD, 16, Z))
    position = lax.axis_index("coil").reshape(1)
    base = target_step(position, image, auxiliary, scaled_dual)
    backs = []
    for chunk in chunks:
        back = grid_tile(
            chunk, offsets, counts, pieces[chunk], x_forward, x_inverse, blocks[0], turned, by_coil
        )
        backs.append(lax.all_to_all(back, "slab", 0, 0, tiled=True))
    total = None
    for chunk in chunks:
        piece = in_hbm(backs[chunk].reshape(TILES, PER, 128, Z))
        total = gradient_step(chunk, in_hbm(y_inverse), piece, sensitivity, total)
    shares = in_hbm(lax.all_to_all(total, "coil", 0, 0, tiled=True))
    return update_step(base, shares, scaled_dual)


def solution(mesh):
    return jax.shard_map(
        body,
        mesh=mesh,
        in_specs=(
            P(None, "slab", None, None),
            P("coil", None, "slab", None, None),
            P("slab", None, None, None),
            P("slab", None, None, "coil", None, None),
            P("slab", None),
            P("slab"),
            P(None, "slab", "coil", None),
            P(None, "slab", "coil", None),
        ),
        out_specs=(
            P(None, "slab", "coil", None),
            P(None, "slab", "coil", None),
            P(None, "slab", "coil", None),
        ),
        check_vma=False,
    )
```

```python
import math

import jax
import jax.numpy as jnp
import numpy as np
import ml_dtypes
from jax import lax
from jax.experimental import pallas as pl
from jax.experimental.pallas import tpu as pltpu
from jax.sharding import PartitionSpec as P

N = 256
Z = 128
WIN = 64
P_SIZE = 128
CH = 24
KYD = 8
TILES = 32
CELLS = WIN * KYD
ROWS = N * KYD
NCOIL = 4
PER = 2

step_size = 0.5
penalty = 1.0
threshold = 0.3

BF = jnp.bfloat16
F32 = jnp.float32


def dft_parts():
    index = np.arange(N)
    angle = (index[:, None] * index[None, :] % N).astype(np.float32) * np.float32(2.0 * math.pi / N)
    factor = np.float32(1.0 / math.sqrt(N))
    re = (np.cos(angle) * factor).astype(ml_dtypes.bfloat16)
    im = (-np.sin(angle) * factor).astype(ml_dtypes.bfloat16)
    return re, im


def real_tables():
    re, im = dft_parts()
    along_y = np.stack(
        [np.concatenate([re, -im], 1), np.concatenate([im, re], 1)], 1
    ).reshape(2 * N, 2 * N)
    re_c = re.reshape(N, TILES, KYD)
    im_c = im.reshape(N, TILES, KYD)
    along_x = np.stack(
        [np.stack([re_c, -im_c], 2), np.stack([im_c, re_c], 2)], 0
    ).reshape(2 * N, 2 * N)
    return along_y, along_x


def hbm(shape, dtype):
    return pltpu.HBM(shape, dtype)


def in_hbm(x):
    return pltpu.with_memory_space_constraint(x, pltpu.HBM)


VMEM = pl.BlockSpec(memory_space=pltpu.VMEM)
SMEM = pl.BlockSpec(memory_space=pltpu.SMEM)
HBM = pl.BlockSpec(memory_space=pltpu.HBM)
DMA = pltpu.SemaphoreType.DMA


def coil_kernel(
    chunk, table_hbm, sens_hbm, image_hbm, out_hbm, table, sens, image, spread, out, sems, done
):
    def copies(step):
        rows = pl.ds(2 * step, 2)
        return [
            pltpu.make_async_copy(image_hbm.at[:, rows], image.at[:, rows], sems.at[PER, step])
        ] + [
            pltpu.make_async_copy(
                sens_hbm.at[chunk * PER + c, :, rows], sens.at[c, :, rows], sems.at[c, step]
            )
            for c in range(PER)
        ]

    whole = pltpu.make_async_copy(table_hbm, table, done.at[PER])
    whole.start()
    pending = [copies(step) for step in range(4)]
    for step in range(4):
        for copy in pending[step][:2]:
            copy.start()
    for step in range(4):
        for copy in pending[step][2:]:
            copy.start()
    whole.wait()

    def leave(c):
        return pltpu.make_async_copy(out.at[:, c], out_hbm.at[:, c], done.at[c])

    def one_coil(c, carry):
        for step in range(4):

            @pl.when(c == 0)
            def _():
                pending[step][0].wait()

            arrival = pltpu.make_async_copy(
                sens_hbm.at[chunk * PER + c, :, pl.ds(2 * step, 2)],
                sens.at[c, :, pl.ds(2 * step, 2)],
                sems.at[c, step],
            )
            arrival.wait()
            parts = []
            for x in (2 * step, 2 * step + 1):
                s_re = sens[c, 0, x].astype(F32)
                s_im = sens[c, 1, x].astype(F32)
                m_re = image[0, x]
                m_im = image[1, x]
                c_re = (s_re * m_re - s_im * m_im).astype(BF)
                c_im = (s_re * m_im + s_im * m_re).astype(BF)
                parts.append(jnp.concatenate([c_re, c_im], 0))
            data = jnp.concatenate(parts, 1)
            result = jnp.dot(table[...], data, preferred_element_type=F32)
            for i in range(2):
                spread[pl.ds(2 * step + i, 2 * N, stride=KYD), :] = result[:, i * Z : (i + 1) * Z]
        out[:, c] = spread[...].astype(BF).reshape(TILES, 128, Z)
        leave(c).start()
        return carry

    lax.fori_loop(0, PER, one_coil, 0)
    for c in range(PER):
        leave(c).wait()


def coil_forward(chunk, table, sensitivity, image):
    def kernel(*refs):
        coil_kernel(chunk, *refs)

    return pl.pallas_call(
        kernel,
        out_shape=hbm((TILES, PER, 128, Z), BF),
        in_specs=[HBM, HBM, HBM],
        out_specs=HBM,
        scratch_shapes=[
            pltpu.VMEM((2 * N, 2 * N), BF),
            pltpu.VMEM((PER, 2, KYD, N, Z), BF),
            pltpu.VMEM((2, KYD, N, Z), F32),
            pltpu.VMEM((TILES * 128, Z), F32),
            pltpu.VMEM((TILES, PER, 128, Z), BF),
            DMA((PER + 1, 4)),
            DMA((PER + 1,)),
        ],
        compiler_params=pltpu.CompilerParams(vmem_limit_bytes=18 << 20),
        name=f"coil_forward_{chunk}",
    )(table, sensitivity, image)


def samples_kernel(counts_ref, samples_hbm, out_hbm, samples, spread, out, arrive, leave):
    count = counts_ref[0]

    def into(j):
        return pltpu.make_async_copy(samples_hbm.at[j], samples.at[j], arrive.at[j])

    def back(j):
        return pltpu.make_async_copy(out.at[:, j], out_hbm.at[:, j], leave.at[j])

    def start(j, carry):
        into(j).start()
        return carry

    def group(j, carry):
        into(j).wait()
        slot = j % 2
        spread[slot] = samples[j].astype(F32).reshape(P_SIZE * 8, Z)
        for coil in range(NCOIL):
            for part in range(2):
                out[coil, j, :, part * Z : (part + 1) * Z] = spread[
                    slot, pl.ds(2 * coil + part, P_SIZE, stride=8), :
                ].astype(BF)
        back(j).start()
        return carry

    def finish(j, carry):
        back(j).wait()
        return carry

    lax.fori_loop(0, count, start, 0)
    lax.fori_loop(0, count, group, 0)
    lax.fori_loop(0, count, finish, 0)


def samples_by_coil(counts, samples):
    return pl.pallas_call(
        samples_kernel,
        out_shape=hbm((NCOIL, CH, P_SIZE, 2 * Z), BF),
        in_specs=[SMEM, HBM],
        out_specs=HBM,
        scratch_shapes=[
            pltpu.VMEM((CH, P_SIZE, 8, Z), BF),
            pltpu.VMEM((2, P_SIZE * 8, Z), F32),
            pltpu.VMEM((NCOIL, CH, P_SIZE, 2 * Z), BF),
            DMA((CH,)),
            DMA((CH,)),
        ],
        compiler_params=pltpu.CompilerParams(vmem_limit_bytes=18 << 20),
        name="samples_by_coil",
    )(counts, samples)


def grid_kernel(
    chunk,
    offsets_ref,
    counts_ref,
    piece_hbm,
    forward_ref,
    inverse_ref,
    blocks_hbm,
    turned_hbm,
    samples_hbm,
    out_hbm,
    piece,
    blocks,
    turned,
    samples,
    window,
    total,
    out,
    sems,
    leave,
):
    count = counts_ref[0]
    arrival = pltpu.make_async_copy(piece_hbm, piece, leave.at[PER])
    arrival.start()

    def copies(j):
        return [
            pltpu.make_async_copy(blocks_hbm.at[j], blocks.at[j], sems.at[0, j]),
            pltpu.make_async_copy(turned_hbm.at[j], turned.at[j], sems.at[1, j]),
        ] + [
            pltpu.make_async_copy(
                samples_hbm.at[chunk * PER + c, j],
                samples.at[j, :, pl.ds(2 * Z * c, 2 * Z)],
                sems.at[2 + c, j],
            )
            for c in range(PER)
        ]

    def start(j, carry):
        for copy in copies(j):
            copy.start()
        return carry

    lax.fori_loop(0, count, start, 0)

    arrival.wait()

    def forward_row(ky, carry):
        data = jnp.concatenate(
            [piece[:, c, ky].reshape(2 * N, Z) for c in range(PER)], 1
        )
        result = jnp.dot(forward_ref[...], data, preferred_element_type=F32)
        for c in range(PER):
            for part in range(2):
                total[2 * c + part, pl.ds(ky, N, stride=KYD), :] = result[
                    part * N : (part + 1) * N, c * Z : (c + 1) * Z
                ]
        return carry

    lax.fori_loop(0, KYD, forward_row, 0)
    for s in range(2 * PER):
        lanes = slice(s * Z, (s + 1) * Z)
        total[s, ROWS : ROWS + KYD, :] = jnp.zeros((KYD, Z), F32)
        window[0, :, lanes] = total[s, 0:ROWS, :].astype(BF)
        window[1, :, lanes] = total[s, KYD : ROWS + KYD, :].astype(BF)
    total[...] = jnp.zeros_like(total)

    def arrive(j):
        for copy in copies(j):
            copy.wait()

    def predict(j):
        first = offsets_ref[0, j]
        row = pl.multiple_of((first // 2) * (2 * KYD), 2 * KYD)
        view = window[first % 2, pl.ds(row, CELLS), :]
        predicted = jnp.dot(blocks[j], view, preferred_element_type=F32)
        return (predicted - samples[j].astype(F32)).astype(BF)

    def add_back(j, misfit):
        update = jnp.dot(turned[j], misfit, preferred_element_type=F32)
        spot = pl.ds(pl.multiple_of(offsets_ref[0, j] * KYD, KYD), CELLS)
        for s in range(2 * PER):
            total[s, spot, :] = total[s, spot, :] + update[:, s * Z : (s + 1) * Z]

    arrive(0)
    samples[0] = predict(0)

    def group(j, carry):
        arrive(j)
        before = samples[j - 1]
        misfit = predict(j)
        add_back(j - 1, before)
        samples[j] = misfit
        return carry

    lax.fori_loop(1, count, group, 0)
    add_back(count - 1, samples[count - 1])

    leaving = []
    for c in range(PER):

        def inverse_rows(pair, carry):
            data = jnp.concatenate(
                [
                    jnp.concatenate(
                        [
                            total[2 * c + part, pl.ds(2 * pair + i, N, stride=KYD), :].astype(BF)
                            for part in range(2)
                        ],
                        0,
                    )
                    for i in range(2)
                ],
                1,
            )
            result = jnp.dot(inverse_ref[...], data, preferred_element_type=F32).astype(BF)
            for i in range(2):
                out[:, c, 2 * pair + i] = result[:, i * Z : (i + 1) * Z].reshape(TILES, 16, Z)
            return carry

        lax.fori_loop(0, KYD // 2, inverse_rows, 0)
        copy = pltpu.make_async_copy(out.at[:, c], out_hbm.at[:, c], leave.at[c])
        copy.start()
        leaving.append(copy)
    for copy in leaving:
        copy.wait()


def grid_tile(chunk, offsets, counts, piece, forward, inverse, blocks, turned, samples):
    def kernel(*refs):
        grid_kernel(chunk, *refs)

    return pl.pallas_call(
        kernel,
        out_shape=hbm((TILES, PER, KYD, 16, Z), BF),
        in_specs=[SMEM, SMEM, HBM, VMEM, VMEM, HBM, HBM, HBM],
        out_specs=HBM,
        scratch_shapes=[
            pltpu.VMEM((TILES, PER, KYD, 16, Z), BF),
            pltpu.VMEM((CH, P_SIZE, CELLS), BF),
            pltpu.VMEM((CH, CELLS, P_SIZE), BF),
            pltpu.VMEM((CH, P_SIZE, 2 * Z * PER), BF),
            pltpu.VMEM((2, ROWS, 2 * Z * PER), BF),
            pltpu.VMEM((2 * PER, ROWS + KYD, Z), F32),
            pltpu.VMEM((TILES, PER, KYD, 16, Z), BF),
            DMA((2 + PER, CH)),
            DMA((PER + 1,)),
        ],
        compiler_params=pltpu.CompilerParams(vmem_limit_bytes=30 << 20),
        name=f"grid_tile_{chunk}",
    )(offsets, counts, piece, forward, inverse, blocks, turned, samples)


def gradient_kernel(chunk, table_ref, piece_hbm, sens_hbm, *rest):
    first = chunk == 0
    last = chunk == NCOIL // PER - 1
    rest = list(rest)
    before_ref = None if first else rest.pop(0)
    out_ref = rest.pop(0)
    piece, sens, spread, sems, arrive = rest[:5]
    if last:
        out, leave = rest[5:]
    half = TILES // 2

    def sens_copy(step):
        rows = pl.ds(2 * step, 2)
        return pltpu.make_async_copy(
            sens_hbm.at[pl.ds(chunk * PER, PER), :, rows], sens.at[:, :, rows], sems.at[step]
        )

    def leave_copy(step):
        rows = pl.ds(2 * step, 2)
        return pltpu.make_async_copy(out.at[:, :, rows], out_ref.at[:, :, rows], leave.at[step])

    arrivals = []
    for c in range(PER):
        for h in range(2):
            tiles = pl.ds(h * half, half)
            copy = pltpu.make_async_copy(
                piece_hbm.at[tiles, c], piece.at[tiles, c], arrive.at[c, h]
            )
            copy.start()
            arrivals.append((c, h, copy))
    for step in range(4):
        sens_copy(step).start()
    for c, h, copy in arrivals:
        copy.wait()
        spread[c, h * half * 128 : (h + 1) * half * 128, :] = (
            piece[h * half : (h + 1) * half, c].astype(F32).reshape(half * 128, Z)
        )

    def rows_pair(step, carry):
        sens_copy(step).wait()
        for i in range(2):
            x = 2 * step + i
            data = jnp.concatenate(
                [spread[c, pl.ds(x, 2 * N, stride=KYD), :].astype(BF) for c in range(PER)], 1
            )
            result = jnp.dot(table_ref[...], data, preferred_element_type=F32)
            result = result.astype(BF).astype(F32)
            g_re = None if first else before_ref[0, x]
            g_im = None if first else before_ref[1, x]
            for c in range(PER):
                lanes = slice(c * Z, (c + 1) * Z)
                a_re = result[:N, lanes]
                a_im = result[N:, lanes]
                s_re = sens[c, 0, x].astype(F32)
                s_im = sens[c, 1, x].astype(F32)
                t_re = s_re * a_re + s_im * a_im
                t_im = s_re * a_im - s_im * a_re
                g_re = t_re if g_re is None else g_re + t_re
                g_im = t_im if g_im is None else g_im + t_im
            if last:
                out[:, 0, x] = g_re.astype(BF).reshape(NCOIL, N // NCOIL, Z)
                out[:, 1, x] = g_im.astype(BF).reshape(NCOIL, N // NCOIL, Z)
            else:
                out_ref[0, x] = g_re
                out_ref[1, x] = g_im
        if last:
            leave_copy(step).start()
        return carry

    lax.fori_loop(0, 4, rows_pair, 0)
    if last:
        for step in range(4):
            leave_copy(step).wait()


def gradient_step(chunk, table, piece, sensitivity, before):
    first = chunk == 0
    last = chunk == NCOIL // PER - 1

    def kernel(*refs):
        gradient_kernel(chunk, *refs)

    shares = (NCOIL, 2, KYD, N // NCOIL, Z)
    return pl.pallas_call(
        kernel,
        out_shape=hbm(shares, BF) if last else jax.ShapeDtypeStruct((2, KYD, N, Z), F32),
        in_specs=[VMEM, HBM, HBM] + ([] if first else [VMEM]),
        out_specs=HBM if last else VMEM,
        scratch_shapes=[
            pltpu.VMEM((TILES, PER, 128, Z), BF),
            pltpu.VMEM((PER, 2, KYD, N, Z), BF),
            pltpu.VMEM((PER, TILES * 128, Z), F32),
            DMA((4,)),
            DMA((PER, 2)),
        ]
        + ([pltpu.VMEM(shares, BF), DMA((4,))] if last else []),
        compiler_params=pltpu.CompilerParams(vmem_limit_bytes=18 << 20),
        name=f"gradient_{chunk}",
    )(*([table, piece, sensitivity] + ([] if first else [before])))


def haar_rows(top, low):
    add = (top + low) * 0.5
    sub = (top - low) * 0.5
    cols = top.shape[0]
    odd = lax.broadcasted_iota(jnp.int32, top.shape, 0) % 2 == 1

    def pairs(v):
        ahead = pltpu.roll(v, cols - 1, 0)
        behind = pltpu.roll(v, 1, 0)
        return jnp.where(odd, behind - v, v + ahead)

    return pairs(add), pairs(sub)


def target_kernel(position_ref, image_hbm, aux_ref, dual_ref, out_ref, image, sem):
    share = N // NCOIL
    columns = pl.ds(pl.multiple_of(position_ref[0] * share, share), share)
    copy = pltpu.make_async_copy(image_hbm.at[:, :, columns], image, sem)
    copy.start()
    copy.wait()
    for m in range(KYD // 2):
        for part in range(2):
            rows = haar_rows(
                *(aux_ref[part, 2 * m + i] - dual_ref[part, 2 * m + i] for i in range(2))
            )
            for i in range(2):
                current = image[part, 2 * m + i]
                out_ref[part, 2 * m + i] = current - step_size * penalty * (current - rows[i])


def target_step(position, image, auxiliary, scaled_dual):
    return pl.pallas_call(
        target_kernel,
        out_shape=jax.ShapeDtypeStruct(auxiliary.shape, F32),
        in_specs=[SMEM, HBM, VMEM, VMEM],
        out_specs=VMEM,
        scratch_shapes=[pltpu.VMEM(auxiliary.shape, F32), DMA],
        compiler_params=pltpu.CompilerParams(vmem_limit_bytes=6 << 20),
        name="target",
    )(position, image, auxiliary, scaled_dual)


def update_kernel(
    base_ref, pieces_ref, dual_ref, image_hbm, aux_hbm, dual_hbm, image, aux, dual, sems
):
    leaving = []
    for m in range(KYD // 2):
        coeffs = []
        for part in range(2):
            rows = []
            for x in (2 * m, 2 * m + 1):
                gradient = pieces_ref[0, part, x].astype(F32)
                for k in range(1, NCOIL):
                    gradient = gradient + pieces_ref[k, part, x].astype(F32)
                value = base_ref[part, x] - step_size * gradient
                image[part, x] = value
                rows.append(value)
            top, low = haar_rows(*rows)
            coeffs.append((top + dual_ref[part, 2 * m], low + dual_ref[part, 2 * m + 1]))
        for i in range(2):
            c_re = coeffs[0][i]
            c_im = coeffs[1][i]
            magnitude = jnp.sqrt(c_re * c_re + c_im * c_im)
            factor = jnp.maximum(1.0 - threshold / jnp.maximum(magnitude, threshold), 0.0)
            for part, value in enumerate((c_re, c_im)):
                kept = value * factor
                aux[part, 2 * m + i] = kept
                dual[part, 2 * m + i] = value - kept
        pair = pl.ds(2 * m, 2)
        for k, (near, far) in enumerate(((image, image_hbm), (aux, aux_hbm), (dual, dual_hbm))):
            copy = pltpu.make_async_copy(near.at[:, pair], far.at[:, pair], sems.at[k, m])
            copy.start()
            leaving.append(copy)
    for copy in leaving:
        copy.wait()


def update_step(base, pieces, scaled_dual):
    shape = hbm(scaled_dual.shape, F32)
    return pl.pallas_call(
        update_kernel,
        out_shape=(shape, shape, shape),
        in_specs=[VMEM, VMEM, VMEM],
        out_specs=(HBM, HBM, HBM),
        scratch_shapes=[pltpu.VMEM(scaled_dual.shape, F32)] * 3 + [DMA((3, KYD // 2))],
        compiler_params=pltpu.CompilerParams(vmem_limit_bytes=8 << 20),
        name="update",
    )(base, pieces, scaled_dual)


def body(image, sensitivity, blocks, samples, offsets, counts, auxiliary, scaled_dual):
    along_y, along_x = real_tables()
    y_forward, x_forward = jnp.asarray(along_y), jnp.asarray(along_x)
    y_kept, x_kept = lax.optimization_barrier((y_forward, x_forward))
    y_inverse = y_kept.T
    x_inverse = x_kept.T

    image, sensitivity = in_hbm(image), in_hbm(sensitivity)
    y_forward = in_hbm(y_forward)
    turned = jnp.swapaxes(blocks[0], 1, 2)
    by_coil = samples_by_coil(counts, in_hbm(samples.reshape(CH, P_SIZE, 2 * NCOIL, Z)))

    chunks = range(NCOIL // PER)
    pieces = []
    for chunk in chunks:
        half = coil_forward(chunk, y_forward, sensitivity, image)
        if chunk == 1:
            half, turned, by_coil, y_inverse, x_inverse = lax.optimization_barrier(
                (half, turned, by_coil, y_inverse, x_inverse)
            )
        piece = lax.all_to_all(half, "slab", 0, 0, tiled=True)
        pieces.append(piece.reshape(TILES, PER, KYD, 16, Z))
    position = lax.axis_index("coil").reshape(1)
    base = target_step(position, image, auxiliary, scaled_dual)
    backs = []
    for chunk in chunks:
        back = grid_tile(
            chunk,
            offsets,
            counts,
            in_hbm(pieces[chunk]),
            x_forward,
            x_inverse,
            in_hbm(blocks[0]),
            in_hbm(turned),
            in_hbm(by_coil),
        )
        backs.append(lax.all_to_all(back, "slab", 0, 0, tiled=True))
    total = None
    for chunk in chunks:
        piece = in_hbm(backs[chunk].reshape(TILES, PER, 128, Z))
        total = gradient_step(chunk, y_inverse, piece, sensitivity, total)
    shares = lax.all_to_all(total, "coil", 0, 0, tiled=True)
    return update_step(base, shares, scaled_dual)


def solution(mesh):
    return jax.shard_map(
        body,
        mesh=mesh,
        in_specs=(
            P(None, "slab", None, None),
            P("coil", None, "slab", None, None),
            P("slab", None, None, None),
            P("slab", None, None, "coil", None, None),
            P("slab", None),
            P("slab"),
            P(None, "slab", "coil", None),
            P(None, "slab", "coil", None),
        ),
        out_specs=(
            P(None, "slab", "coil", None),
            P(None, "slab", "coil", None),
            P(None, "slab", "coil", None),
        ),
        check_vma=False,
    )
```

```python
import math

import jax
import jax.numpy as jnp
import numpy as np
import ml_dtypes
from jax import lax
from jax.experimental import pallas as pl
from jax.experimental.pallas import tpu as pltpu
from jax.sharding import PartitionSpec as P

N = 256
Z = 128
WIN = 64
P_SIZE = 128
CH = 24
KYD = 8
TILES = 32
CELLS = WIN * KYD
ROWS = N * KYD
NCOIL = 4
PER = 2

step_size = 0.5
penalty = 1.0
threshold = 0.3

BF = jnp.bfloat16
F32 = jnp.float32


def dft_parts():
    index = np.arange(N)
    angle = (index[:, None] * index[None, :] % N).astype(np.float32) * np.float32(2.0 * math.pi / N)
    factor = np.float32(1.0 / math.sqrt(N))
    re = (np.cos(angle) * factor).astype(ml_dtypes.bfloat16)
    im = (-np.sin(angle) * factor).astype(ml_dtypes.bfloat16)
    return re, im


def real_tables():
    re, im = dft_parts()
    along_y = np.stack(
        [np.concatenate([re, -im], 1), np.concatenate([im, re], 1)], 1
    ).reshape(2 * N, 2 * N)
    re_c = re.reshape(N, TILES, KYD)
    im_c = im.reshape(N, TILES, KYD)
    along_x = np.stack(
        [np.stack([re_c, -im_c], 2), np.stack([im_c, re_c], 2)], 0
    ).reshape(2 * N, 2 * N)
    return along_y, along_x


def hbm(shape, dtype):
    return pltpu.HBM(shape, dtype)


def in_hbm(x):
    return pltpu.with_memory_space_constraint(x, pltpu.HBM)


VMEM = pl.BlockSpec(memory_space=pltpu.VMEM)
SMEM = pl.BlockSpec(memory_space=pltpu.SMEM)
HBM = pl.BlockSpec(memory_space=pltpu.HBM)
DMA = pltpu.SemaphoreType.DMA


def coil_kernel(
    chunk, table_hbm, sens_hbm, image_hbm, out_hbm, table, sens, image, spread, out, sems, leave
):
    stages = 2
    span = KYD // stages
    group = TILES // stages

    def sens_copy(c, stage):
        rows = pl.ds(stage * span, span)
        return pltpu.make_async_copy(
            sens_hbm.at[chunk * PER + c, :, rows], sens.at[c, :, rows], sems.at[c, stage]
        )

    def image_copy(stage):
        rows = pl.ds(stage * span, span)
        return pltpu.make_async_copy(image_hbm.at[:, rows], image.at[:, rows], sems.at[PER, stage])

    def leave_copy(c, stage):
        tiles = pl.ds(stage * group, group)
        return pltpu.make_async_copy(out.at[tiles, c], out_hbm.at[tiles, c], leave.at[c, stage])

    whole = pltpu.make_async_copy(table_hbm, table, leave.at[PER, 0])
    whole.start()
    for stage in range(stages):
        image_copy(stage).start()
        sens_copy(0, stage).start()
    for c in range(1, PER):
        for stage in range(stages):
            sens_copy(c, stage).start()
    whole.wait()

    def one_coil(c, arrive):
        for stage in range(stages):
            arrive(c, stage)
            for pair in range(span // 2):
                first = stage * span + 2 * pair
                parts = []
                for x in (first, first + 1):
                    s_re = sens[c, 0, x].astype(F32)
                    s_im = sens[c, 1, x].astype(F32)
                    m_re = image[0, x]
                    m_im = image[1, x]
                    c_re = (s_re * m_re - s_im * m_im).astype(BF)
                    c_im = (s_re * m_im + s_im * m_re).astype(BF)
                    parts.append(jnp.concatenate([c_re, c_im], 0))
                data = jnp.concatenate(parts, 1)
                result = jnp.dot(table[...], data, preferred_element_type=F32)
                for i in range(2):
                    spread[c, pl.ds(first + i, 2 * N, stride=KYD), :] = result[
                        :, i * Z : (i + 1) * Z
                    ]
        for stage in range(stages):
            rows = slice(stage * group * 128, (stage + 1) * group * 128)
            out[stage * group : (stage + 1) * group, c] = (
                spread[c, rows].astype(BF).reshape(group, 128, Z)
            )
            leave_copy(c, stage).start()

    def arrive_staged(c, stage):
        if c == 0:
            image_copy(stage).wait()
        sens_copy(c, stage).wait()

    if chunk == 0:
        for c in range(PER):
            one_coil(c, arrive_staged)
    else:
        for stage in range(stages):
            for c in range(PER):
                arrive_staged(c, stage)

        def rolled(c, carry):
            one_coil(c, lambda c, stage: None)
            return carry

        lax.fori_loop(0, PER, rolled, 0)
    for c in range(PER):
        for stage in range(stages):
            leave_copy(c, stage).wait()


def coil_forward(chunk, table, sensitivity, image):
    def kernel(*refs):
        coil_kernel(chunk, *refs)

    return pl.pallas_call(
        kernel,
        out_shape=hbm((TILES, PER, 128, Z), BF),
        in_specs=[HBM, HBM, HBM],
        out_specs=HBM,
        scratch_shapes=[
            pltpu.VMEM((2 * N, 2 * N), BF),
            pltpu.VMEM((PER, 2, KYD, N, Z), BF),
            pltpu.VMEM((2, KYD, N, Z), F32),
            pltpu.VMEM((PER, TILES * 128, Z), F32),
            pltpu.VMEM((TILES, PER, 128, Z), BF),
            DMA((PER + 1, 2)),
            DMA((PER + 1, 2)),
        ],
        compiler_params=pltpu.CompilerParams(vmem_limit_bytes=18 << 20),
        name=f"coil_forward_{chunk}",
    )(table, sensitivity, image)


def samples_kernel(counts_ref, samples_hbm, out_hbm, samples, spread, out, arrive, leave):
    count = counts_ref[0]

    def into(j):
        return pltpu.make_async_copy(samples_hbm.at[j], samples.at[j], arrive.at[j])

    def back(j):
        return pltpu.make_async_copy(out.at[:, j], out_hbm.at[:, j], leave.at[j])

    def start(j, carry):
        into(j).start()
        return carry

    def group(j, carry):
        into(j).wait()
        slot = j % 2
        spread[slot] = samples[j].astype(F32).reshape(P_SIZE * 8, Z)
        for coil in range(NCOIL):
            for part in range(2):
                out[coil, j, :, part * Z : (part + 1) * Z] = spread[
                    slot, pl.ds(2 * coil + part, P_SIZE, stride=8), :
                ].astype(BF)
        back(j).start()
        return carry

    def finish(j, carry):
        back(j).wait()
        return carry

    lax.fori_loop(0, count, start, 0)
    lax.fori_loop(0, count, group, 0)
    lax.fori_loop(0, count, finish, 0)


def samples_by_coil(counts, samples):
    return pl.pallas_call(
        samples_kernel,
        out_shape=hbm((NCOIL, CH, P_SIZE, 2 * Z), BF),
        in_specs=[SMEM, HBM],
        out_specs=HBM,
        scratch_shapes=[
            pltpu.VMEM((CH, P_SIZE, 8, Z), BF),
            pltpu.VMEM((2, P_SIZE * 8, Z), F32),
            pltpu.VMEM((NCOIL, CH, P_SIZE, 2 * Z), BF),
            DMA((CH,)),
            DMA((CH,)),
        ],
        compiler_params=pltpu.CompilerParams(vmem_limit_bytes=18 << 20),
        name="samples_by_coil",
    )(counts, samples)


def grid_kernel(
    chunk,
    offsets_ref,
    counts_ref,
    piece_hbm,
    forward_ref,
    inverse_ref,
    blocks_hbm,
    turned_hbm,
    samples_hbm,
    out_hbm,
    piece,
    blocks,
    turned,
    samples,
    window,
    total,
    out,
    sems,
    leave,
):
    count = counts_ref[0]
    if chunk == 0:
        arrival = pltpu.make_async_copy(piece_hbm, piece, leave.at[PER])
        arrival.start()
    else:
        piece = piece_hbm

    def copies(j):
        return [
            pltpu.make_async_copy(blocks_hbm.at[j], blocks.at[j], sems.at[0, j]),
            pltpu.make_async_copy(turned_hbm.at[j], turned.at[j], sems.at[1, j]),
        ] + [
            pltpu.make_async_copy(
                samples_hbm.at[chunk * PER + c, j],
                samples.at[j, :, pl.ds(2 * Z * c, 2 * Z)],
                sems.at[2 + c, j],
            )
            for c in range(PER)
        ]

    def start(j, carry):
        for copy in copies(j):
            copy.start()
        return carry

    lax.fori_loop(0, count, start, 0)

    if chunk == 0:
        arrival.wait()

    def forward_row(ky, carry):
        data = jnp.concatenate(
            [piece[:, c, ky].reshape(2 * N, Z) for c in range(PER)], 1
        )
        result = jnp.dot(forward_ref[...], data, preferred_element_type=F32)
        for c in range(PER):
            for part in range(2):
                total[2 * c + part, pl.ds(ky, N, stride=KYD), :] = result[
                    part * N : (part + 1) * N, c * Z : (c + 1) * Z
                ]
        return carry

    lax.fori_loop(0, KYD, forward_row, 0)
    for s in range(2 * PER):
        lanes = slice(s * Z, (s + 1) * Z)
        total[s, ROWS : ROWS + KYD, :] = jnp.zeros((KYD, Z), F32)
        window[0, :, lanes] = total[s, 0:ROWS, :].astype(BF)
        window[1, :, lanes] = total[s, KYD : ROWS + KYD, :].astype(BF)
    total[...] = jnp.zeros_like(total)

    def arrive(j):
        for copy in copies(j):
            copy.wait()

    def predict(j):
        first = offsets_ref[0, j]
        row = pl.multiple_of((first // 2) * (2 * KYD), 2 * KYD)
        view = window[first % 2, pl.ds(row, CELLS), :]
        predicted = jnp.dot(blocks[j], view, preferred_element_type=F32)
        return (predicted - samples[j].astype(F32)).astype(BF)

    def add_back(j, misfit):
        update = jnp.dot(turned[j], misfit, preferred_element_type=F32)
        spot = pl.ds(pl.multiple_of(offsets_ref[0, j] * KYD, KYD), CELLS)
        for s in range(2 * PER):
            total[s, spot, :] = total[s, spot, :] + update[:, s * Z : (s + 1) * Z]

    arrive(0)
    samples[0] = predict(0)

    def group(j, carry):
        arrive(j)
        before = samples[j - 1]
        misfit = predict(j)
        add_back(j - 1, before)
        samples[j] = misfit
        return carry

    lax.fori_loop(1, count, group, 0)
    add_back(count - 1, samples[count - 1])

    leaving = []
    for c in range(PER):

        def inverse_rows(pair, carry):
            data = jnp.concatenate(
                [
                    jnp.concatenate(
                        [
                            total[2 * c + part, pl.ds(2 * pair + i, N, stride=KYD), :].astype(BF)
                            for part in range(2)
                        ],
                        0,
                    )
                    for i in range(2)
                ],
                1,
            )
            result = jnp.dot(inverse_ref[...], data, preferred_element_type=F32).astype(BF)
            for i in range(2):
                out[:, c, 2 * pair + i] = result[:, i * Z : (i + 1) * Z].reshape(TILES, 16, Z)
            return carry

        lax.fori_loop(0, KYD // 2, inverse_rows, 0)
        copy = pltpu.make_async_copy(out.at[:, c], out_hbm.at[:, c], leave.at[c])
        copy.start()
        leaving.append(copy)
    for copy in leaving:
        copy.wait()


def grid_tile(chunk, offsets, counts, piece, forward, inverse, blocks, turned, samples):
    def kernel(*refs):
        grid_kernel(chunk, *refs)

    return pl.pallas_call(
        kernel,
        out_shape=hbm((TILES, PER, KYD, 16, Z), BF),
        in_specs=[SMEM, SMEM, HBM if chunk == 0 else VMEM, VMEM, VMEM, HBM, HBM, HBM],
        out_specs=HBM,
        scratch_shapes=[
            pltpu.VMEM((TILES, PER, KYD, 16, Z) if chunk == 0 else (16, Z), BF),
            pltpu.VMEM((CH, P_SIZE, CELLS), BF),
            pltpu.VMEM((CH, CELLS, P_SIZE), BF),
            pltpu.VMEM((CH, P_SIZE, 2 * Z * PER), BF),
            pltpu.VMEM((2, ROWS, 2 * Z * PER), BF),
            pltpu.VMEM((2 * PER, ROWS + KYD, Z), F32),
            pltpu.VMEM((TILES, PER, KYD, 16, Z), BF),
            DMA((2 + PER, CH)),
            DMA((PER + 1,)),
        ],
        compiler_params=pltpu.CompilerParams(vmem_limit_bytes=30 << 20),
        name=f"grid_tile_{chunk}",
    )(offsets, counts, piece, forward, inverse, blocks, turned, samples)


def combine(adjoint, sens, x, before):
    g_re, g_im = before
    for c in range(PER):
        lanes = slice(c * Z, (c + 1) * Z)
        a_re = adjoint[:N, lanes]
        a_im = adjoint[N:, lanes]
        s_re = sens[c, 0, x].astype(F32)
        s_im = sens[c, 1, x].astype(F32)
        t_re = s_re * a_re + s_im * a_im
        t_im = s_re * a_im - s_im * a_re
        g_re = t_re if g_re is None else g_re + t_re
        g_im = t_im if g_im is None else g_im + t_im
    return g_re, g_im


def adjoint_row(table_ref, spread, x):
    data = jnp.concatenate(
        [spread[c, pl.ds(x, 2 * N, stride=KYD), :].astype(BF) for c in range(PER)], 1
    )
    return jnp.dot(table_ref[...], data, preferred_element_type=F32).astype(BF).astype(F32)


def gradient_first_kernel(table_ref, piece_hbm, sens_hbm, out_ref, piece, sens, spread, sems):
    copies = [
        pltpu.make_async_copy(piece_hbm, piece, sems.at[0]),
        pltpu.make_async_copy(sens_hbm.at[pl.ds(0, PER)], sens, sems.at[1]),
    ]
    for copy in copies:
        copy.start()
    copies[0].wait()
    for c in range(PER):
        spread[c] = piece[:, c].astype(F32).reshape(TILES * 128, Z)
    copies[1].wait()

    def row(x, carry):
        g_re, g_im = combine(adjoint_row(table_ref, spread, x), sens, x, (None, None))
        out_ref[0, x] = g_re
        out_ref[1, x] = g_im
        return carry

    lax.fori_loop(0, KYD, row, 0)


def gradient_first(table, piece, sensitivity):
    return pl.pallas_call(
        gradient_first_kernel,
        out_shape=jax.ShapeDtypeStruct((2, KYD, N, Z), F32),
        in_specs=[VMEM, HBM, HBM],
        out_specs=VMEM,
        scratch_shapes=[
            pltpu.VMEM((TILES, PER, 128, Z), BF),
            pltpu.VMEM((PER, 2, KYD, N, Z), BF),
            pltpu.VMEM((PER, TILES * 128, Z), F32),
            DMA((2,)),
        ],
        compiler_params=pltpu.CompilerParams(vmem_limit_bytes=18 << 20),
        name="gradient_first",
    )(table, piece, sensitivity)


def gradient_last_kernel(position_ref, table_ref, piece_hbm, sens_hbm, before_ref, *rest):
    shares = rest[:NCOIL]
    piece, sens, spread, out, arrive, sems = rest[NCOIL:]
    position = position_ref[0]
    span = KYD // 2

    def sens_copy(stage):
        rows = pl.ds(stage * span, span)
        return pltpu.make_async_copy(
            sens_hbm.at[pl.ds(PER, PER), :, rows], sens.at[:, :, rows], arrive.at[stage]
        )

    def leave(k, stage):
        rows = pl.ds(stage * span, span)
        target = lax.rem(position + k, NCOIL)
        return pltpu.make_async_copy(
            out.at[target, :, rows], shares[k].at[:, rows], sems.at[k, stage]
        )

    arrivals = [
        pltpu.make_async_copy(piece_hbm.at[:, c], piece.at[:, c], arrive.at[2 + c])
        for c in range(PER)
    ]
    for copy in arrivals:
        copy.start()
    for stage in range(2):
        sens_copy(stage).start()
    for c in range(PER):
        arrivals[c].wait()
        spread[c] = piece[:, c].astype(F32).reshape(TILES * 128, Z)
    for stage in range(2):
        sens_copy(stage).wait()
        for x in range(stage * span, (stage + 1) * span):
            g_re, g_im = combine(
                adjoint_row(table_ref, spread, x), sens, x, (before_ref[0, x], before_ref[1, x])
            )
            out[:, 0, x] = g_re.astype(BF).reshape(NCOIL, N // NCOIL, Z)
            out[:, 1, x] = g_im.astype(BF).reshape(NCOIL, N // NCOIL, Z)
        for k in range(NCOIL):
            leave(k, stage).start()
    for stage in range(2):
        for k in range(NCOIL):
            leave(k, stage).wait()


def gradient_last(position, table, piece, sens, before):
    share = (2, KYD, N // NCOIL, Z)
    return pl.pallas_call(
        gradient_last_kernel,
        out_shape=(hbm(share, BF),) * NCOIL,
        in_specs=[SMEM, VMEM, HBM, HBM, VMEM],
        out_specs=(HBM,) * NCOIL,
        scratch_shapes=[
            pltpu.VMEM((TILES, PER, 128, Z), BF),
            pltpu.VMEM((PER, 2, KYD, N, Z), BF),
            pltpu.VMEM((PER, TILES * 128, Z), F32),
            pltpu.VMEM((NCOIL,) + share, BF),
            DMA((2 + PER,)),
            DMA((NCOIL, 2)),
        ],
        compiler_params=pltpu.CompilerParams(vmem_limit_bytes=16 << 20),
        name="gradient_last",
    )(position, table, piece, sens, before)


def haar_rows(top, low):
    add = (top + low) * 0.5
    sub = (top - low) * 0.5
    cols = top.shape[0]
    odd = lax.broadcasted_iota(jnp.int32, top.shape, 0) % 2 == 1

    def pairs(v):
        ahead = pltpu.roll(v, cols - 1, 0)
        behind = pltpu.roll(v, 1, 0)
        return jnp.where(odd, behind - v, v + ahead)

    return pairs(add), pairs(sub)


def target_kernel(position_ref, image_hbm, aux_ref, dual_ref, out_ref, image, sem):
    share = N // NCOIL
    columns = pl.ds(pl.multiple_of(position_ref[0] * share, share), share)
    copy = pltpu.make_async_copy(image_hbm.at[:, :, columns], image, sem)
    copy.start()
    copy.wait()
    for m in range(KYD // 2):
        for part in range(2):
            rows = haar_rows(
                *(aux_ref[part, 2 * m + i] - dual_ref[part, 2 * m + i] for i in range(2))
            )
            for i in range(2):
                current = image[part, 2 * m + i]
                out_ref[part, 2 * m + i] = current - step_size * penalty * (current - rows[i])


def target_step(position, image, auxiliary, scaled_dual):
    return pl.pallas_call(
        target_kernel,
        out_shape=jax.ShapeDtypeStruct(auxiliary.shape, F32),
        in_specs=[SMEM, HBM, VMEM, VMEM],
        out_specs=VMEM,
        scratch_shapes=[pltpu.VMEM(auxiliary.shape, F32), DMA],
        compiler_params=pltpu.CompilerParams(vmem_limit_bytes=6 << 20),
        name="target",
    )(position, image, auxiliary, scaled_dual)


def update_kernel(
    base_ref, s0, s1, s2, s3, dual_ref, image_hbm, aux_hbm, dual_hbm, image, aux, dual, sems
):
    leaving = []
    for m in range(KYD // 2):
        coeffs = []
        for part in range(2):
            rows = []
            for x in (2 * m, 2 * m + 1):
                gradient = s0[part, x].astype(F32)
                for share in (s1, s2, s3):
                    gradient = gradient + share[part, x].astype(F32)
                value = base_ref[part, x] - step_size * gradient
                image[part, x] = value
                rows.append(value)
            top, low = haar_rows(*rows)
            coeffs.append((top + dual_ref[part, 2 * m], low + dual_ref[part, 2 * m + 1]))
        for i in range(2):
            c_re = coeffs[0][i]
            c_im = coeffs[1][i]
            magnitude = jnp.sqrt(c_re * c_re + c_im * c_im)
            factor = jnp.maximum(1.0 - threshold / jnp.maximum(magnitude, threshold), 0.0)
            for part, value in enumerate((c_re, c_im)):
                kept = value * factor
                aux[part, 2 * m + i] = kept
                dual[part, 2 * m + i] = value - kept
        pair = pl.ds(2 * m, 2)
        for k, (near, far) in enumerate(((image, image_hbm), (aux, aux_hbm), (dual, dual_hbm))):
            copy = pltpu.make_async_copy(near.at[:, pair], far.at[:, pair], sems.at[k, m])
            copy.start()
            leaving.append(copy)
    for copy in leaving:
        copy.wait()


def update_step(base, shares, scaled_dual):
    shape = hbm(scaled_dual.shape, F32)
    return pl.pallas_call(
        update_kernel,
        out_shape=(shape, shape, shape),
        in_specs=[VMEM] * (NCOIL + 2),
        out_specs=(HBM, HBM, HBM),
        scratch_shapes=[pltpu.VMEM(scaled_dual.shape, F32)] * 3 + [DMA((3, KYD // 2))],
        compiler_params=pltpu.CompilerParams(vmem_limit_bytes=8 << 20),
        name="update",
    )(base, *shares, scaled_dual)


def body(image, sensitivity, blocks, samples, offsets, counts, auxiliary, scaled_dual):
    along_y, along_x = real_tables()
    y_forward, x_forward = jnp.asarray(along_y), jnp.asarray(along_x)
    y_kept, x_kept = lax.optimization_barrier((y_forward, x_forward))
    y_inverse = y_kept.T
    x_inverse = x_kept.T

    image, sensitivity = in_hbm(image), in_hbm(sensitivity)
    y_forward = in_hbm(y_forward)
    turned = jnp.swapaxes(blocks[0], 1, 2)
    by_coil = samples_by_coil(counts, in_hbm(samples.reshape(CH, P_SIZE, 2 * NCOIL, Z)))

    chunks = range(NCOIL // PER)
    pieces = []
    for chunk in chunks:
        half = coil_forward(chunk, y_forward, sensitivity, image)
        if chunk == 1:
            half, turned, by_coil, y_inverse, x_inverse = lax.optimization_barrier(
                (half, turned, by_coil, y_inverse, x_inverse)
            )
        piece = lax.all_to_all(half, "slab", 0, 0, tiled=True)
        pieces.append(piece.reshape(TILES, PER, KYD, 16, Z))
    position = lax.axis_index("coil").reshape(1)
    base = target_step(position, image, auxiliary, scaled_dual)
    backs = []
    for chunk in chunks:
        back = grid_tile(
            chunk,
            offsets,
            counts,
            in_hbm(pieces[chunk]) if chunk == 0 else pieces[chunk],
            x_forward,
            x_inverse,
            in_hbm(blocks[0]),
            in_hbm(turned),
            in_hbm(by_coil),
        )
        backs.append(lax.all_to_all(back, "slab", 0, 0, tiled=True))
    first, last = (back.reshape(TILES, PER, 128, Z) for back in backs)
    before = gradient_first(y_inverse, in_hbm(first), sensitivity)
    own, *others = gradient_last(position, y_inverse, in_hbm(last), sensitivity, before)
    shares = [own]
    for k in (2, 1, 3):
        ring = [(i, (i + k) % NCOIL) for i in range(NCOIL)]
        shares.append(lax.ppermute(others[k - 1], "coil", ring))
    return update_step(base, shares, scaled_dual)


def solution(mesh):
    return jax.shard_map(
        body,
        mesh=mesh,
        in_specs=(
            P(None, "slab", None, None),
            P("coil", None, "slab", None, None),
            P("slab", None, None, None),
            P("slab", None, None, "coil", None, None),
            P("slab", None),
            P("slab"),
            P(None, "slab", "coil", None),
            P(None, "slab", "coil", None),
        ),
        out_specs=(
            P(None, "slab", "coil", None),
            P(None, "slab", "coil", None),
            P(None, "slab", "coil", None),
        ),
        check_vma=False,
    )
```

```python
import math

import jax
import jax.numpy as jnp
import numpy as np
import ml_dtypes
from jax import lax
from jax.experimental import pallas as pl
from jax.experimental.pallas import tpu as pltpu
from jax.sharding import PartitionSpec as P

N = 256
Z = 128
WIN = 64
P_SIZE = 128
CH = 24
KYD = 8
TILES = 32
CELLS = WIN * KYD
ROWS = N * KYD
NCOIL = 4
PER = 2

step_size = 0.5
penalty = 1.0
threshold = 0.3

BF = jnp.bfloat16
F32 = jnp.float32


def dft_parts():
    index = np.arange(N)
    angle = (index[:, None] * index[None, :] % N).astype(np.float32) * np.float32(2.0 * math.pi / N)
    factor = np.float32(1.0 / math.sqrt(N))
    re = (np.cos(angle) * factor).astype(ml_dtypes.bfloat16)
    im = (-np.sin(angle) * factor).astype(ml_dtypes.bfloat16)
    return re, im


def real_tables():
    re, im = dft_parts()
    along_y = np.stack(
        [np.concatenate([re, -im], 1), np.concatenate([im, re], 1)], 1
    ).reshape(2 * N, 2 * N)
    along_x = np.concatenate([np.concatenate([re, -im], 1), np.concatenate([im, re], 1)], 0)
    return along_y, along_x


def hbm(shape, dtype):
    return pltpu.HBM(shape, dtype)


def in_hbm(x):
    return pltpu.with_memory_space_constraint(x, pltpu.HBM)


VMEM = pl.BlockSpec(memory_space=pltpu.VMEM)
SMEM = pl.BlockSpec(memory_space=pltpu.SMEM)
HBM = pl.BlockSpec(memory_space=pltpu.HBM)
DMA = pltpu.SemaphoreType.DMA


def coil_kernel(chunk, table_hbm, sens_hbm, image_hbm, out_hbm, table, sens, image, out, sems, leave):
    stages = 2
    span = KYD // stages

    def sens_copy(c, stage):
        rows = pl.ds(stage * span, span)
        return pltpu.make_async_copy(
            sens_hbm.at[chunk * PER + c, :, rows], sens.at[c, :, rows], sems.at[c, stage]
        )

    def image_copy(stage):
        rows = pl.ds(stage * span, span)
        return pltpu.make_async_copy(image_hbm.at[:, rows], image.at[:, rows], sems.at[PER, stage])

    def leave_copy(c, stage):
        rows = pl.ds(stage * span, span)
        return pltpu.make_async_copy(out.at[:, c, rows], out_hbm.at[:, c, rows], leave.at[c, stage])

    whole = pltpu.make_async_copy(table_hbm, table, leave.at[PER, 0])
    whole.start()
    for stage in range(stages):
        image_copy(stage).start()
        sens_copy(0, stage).start()
    for c in range(1, PER):
        for stage in range(stages):
            sens_copy(c, stage).start()
    whole.wait()

    def one_coil(c, arrive):
        for stage in range(stages):
            arrive(c, stage)
            for pair in range(span // 2):
                first = stage * span + 2 * pair
                parts = []
                for x in (first, first + 1):
                    s_re = sens[c, 0, x].astype(F32)
                    s_im = sens[c, 1, x].astype(F32)
                    m_re = image[0, x]
                    m_im = image[1, x]
                    c_re = (s_re * m_re - s_im * m_im).astype(BF)
                    c_im = (s_re * m_im + s_im * m_re).astype(BF)
                    parts.append(jnp.concatenate([c_re, c_im], 0))
                data = jnp.concatenate(parts, 1)
                result = jnp.dot(table[...], data, preferred_element_type=F32).astype(BF)
                for i in range(2):
                    out[:, c, first + i] = result[:, i * Z : (i + 1) * Z].reshape(TILES, 16, Z)
            leave_copy(c, stage).start()

    def arrive_staged(c, stage):
        if c == 0:
            image_copy(stage).wait()
        sens_copy(c, stage).wait()

    if chunk == 0:
        for c in range(PER):
            one_coil(c, arrive_staged)
    else:
        for stage in range(stages):
            for c in range(PER):
                arrive_staged(c, stage)

        def rolled(c, carry):
            one_coil(c, lambda c, stage: None)
            return carry

        lax.fori_loop(0, PER, rolled, 0)
    for c in range(PER):
        for stage in range(stages):
            leave_copy(c, stage).wait()


def coil_forward(chunk, table, sensitivity, image):
    def kernel(*refs):
        coil_kernel(chunk, *refs)

    return pl.pallas_call(
        kernel,
        out_shape=hbm((TILES, PER, KYD, 16, Z), BF),
        in_specs=[HBM, HBM, HBM],
        out_specs=HBM,
        scratch_shapes=[
            pltpu.VMEM((2 * N, 2 * N), BF),
            pltpu.VMEM((PER, 2, KYD, N, Z), BF),
            pltpu.VMEM((2, KYD, N, Z), F32),
            pltpu.VMEM((TILES, PER, KYD, 16, Z), BF),
            DMA((PER + 1, 2)),
            DMA((PER + 1, 2)),
        ],
        compiler_params=pltpu.CompilerParams(vmem_limit_bytes=14 << 20),
        name=f"coil_forward_{chunk}",
    )(table, sensitivity, image)


def samples_kernel(counts_ref, samples_hbm, out_hbm, samples, spread, out, arrive, leave):
    count = counts_ref[0]

    def into(j):
        return pltpu.make_async_copy(samples_hbm.at[j], samples.at[j], arrive.at[j])

    def back(j):
        return pltpu.make_async_copy(out.at[:, j], out_hbm.at[:, j], leave.at[j])

    def start(j, carry):
        into(j).start()
        return carry

    def group(j, carry):
        into(j).wait()
        slot = j % 2
        spread[slot] = samples[j].astype(F32).reshape(P_SIZE * 8, Z)
        for coil in range(NCOIL):
            for part in range(2):
                out[coil, j, :, part * Z : (part + 1) * Z] = spread[
                    slot, pl.ds(2 * coil + part, P_SIZE, stride=8), :
                ].astype(BF)
        back(j).start()
        return carry

    def finish(j, carry):
        back(j).wait()
        return carry

    lax.fori_loop(0, count, start, 0)
    lax.fori_loop(0, count, group, 0)
    lax.fori_loop(0, count, finish, 0)


def samples_by_coil(counts, samples):
    return pl.pallas_call(
        samples_kernel,
        out_shape=hbm((NCOIL, CH, P_SIZE, 2 * Z), BF),
        in_specs=[SMEM, HBM],
        out_specs=HBM,
        scratch_shapes=[
            pltpu.VMEM((CH, P_SIZE, 8, Z), BF),
            pltpu.VMEM((2, P_SIZE * 8, Z), F32),
            pltpu.VMEM((NCOIL, CH, P_SIZE, 2 * Z), BF),
            DMA((CH,)),
            DMA((CH,)),
        ],
        compiler_params=pltpu.CompilerParams(vmem_limit_bytes=18 << 20),
        name="samples_by_coil",
    )(counts, samples)


def grid_kernel(
    chunk,
    offsets_ref,
    counts_ref,
    piece_hbm,
    forward_ref,
    inverse_ref,
    blocks_hbm,
    turned_hbm,
    samples_hbm,
    out_hbm,
    piece,
    blocks,
    turned,
    samples,
    window,
    total,
    spread,
    out,
    sems,
    leave,
):
    count = counts_ref[0]
    if chunk == 0:
        arrival = pltpu.make_async_copy(piece_hbm, piece, leave.at[PER])
        arrival.start()
    else:
        piece = piece_hbm

    def copies(j):
        return [
            pltpu.make_async_copy(blocks_hbm.at[j], blocks.at[j], sems.at[0, j]),
            pltpu.make_async_copy(turned_hbm.at[j], turned.at[j], sems.at[1, j]),
        ] + [
            pltpu.make_async_copy(
                samples_hbm.at[chunk * PER + c, j],
                samples.at[j, :, pl.ds(2 * Z * c, 2 * Z)],
                sems.at[2 + c, j],
            )
            for c in range(PER)
        ]

    def start(j, carry):
        for copy in copies(j):
            copy.start()
        return carry

    lax.fori_loop(0, count, start, 0)

    if chunk == 0:
        arrival.wait()

    for c in range(PER):
        spread[c] = piece[:, c].astype(F32).reshape(ROWS * 2, Z)

    def forward_row(ky, carry):
        data = jnp.concatenate(
            [
                jnp.concatenate(
                    [
                        spread[c, pl.ds(2 * ky + part, N, stride=2 * KYD), :].astype(BF)
                        for part in range(2)
                    ],
                    0,
                )
                for c in range(PER)
            ],
            1,
        )
        result = jnp.dot(forward_ref[...], data, preferred_element_type=F32)
        for c in range(PER):
            for part in range(2):
                total[2 * c + part, pl.ds(ky, N, stride=KYD), :] = result[
                    part * N : (part + 1) * N, c * Z : (c + 1) * Z
                ]
        return carry

    lax.fori_loop(0, KYD, forward_row, 0)
    for s in range(2 * PER):
        lanes = slice(s * Z, (s + 1) * Z)
        total[s, ROWS : ROWS + KYD, :] = jnp.zeros((KYD, Z), F32)
        window[0, :, lanes] = total[s, 0:ROWS, :].astype(BF)
        window[1, :, lanes] = total[s, KYD : ROWS + KYD, :].astype(BF)
    total[...] = jnp.zeros_like(total)

    def arrive(j):
        for copy in copies(j):
            copy.wait()

    def predict(j):
        first = offsets_ref[0, j]
        row = pl.multiple_of((first // 2) * (2 * KYD), 2 * KYD)
        view = window[first % 2, pl.ds(row, CELLS), :]
        predicted = jnp.dot(blocks[j], view, preferred_element_type=F32)
        return (predicted - samples[j].astype(F32)).astype(BF)

    def add_back(j, misfit):
        update = jnp.dot(turned[j], misfit, preferred_element_type=F32)
        spot = pl.ds(pl.multiple_of(offsets_ref[0, j] * KYD, KYD), CELLS)
        for s in range(2 * PER):
            total[s, spot, :] = total[s, spot, :] + update[:, s * Z : (s + 1) * Z]

    arrive(0)
    samples[0] = predict(0)

    def group(j, carry):
        arrive(j)
        before = samples[j - 1]
        misfit = predict(j)
        add_back(j - 1, before)
        samples[j] = misfit
        return carry

    lax.fori_loop(1, count, group, 0)
    add_back(count - 1, samples[count - 1])

    leaving = []
    for c in range(PER):

        def inverse_rows(pair, carry):
            data = jnp.concatenate(
                [
                    jnp.concatenate(
                        [
                            total[2 * c + part, pl.ds(2 * pair + i, N, stride=KYD), :].astype(BF)
                            for part in range(2)
                        ],
                        0,
                    )
                    for i in range(2)
                ],
                1,
            )
            result = jnp.dot(inverse_ref[...], data, preferred_element_type=F32)
            for i in range(2):
                for part in range(2):
                    spread[c, pl.ds(2 * (2 * pair + i) + part, N, stride=2 * KYD), :] = result[
                        part * N : (part + 1) * N, i * Z : (i + 1) * Z
                    ]
            return carry

        lax.fori_loop(0, KYD // 2, inverse_rows, 0)
        out[:, c] = spread[c].astype(BF).reshape(TILES, KYD, 16, Z)
        copy = pltpu.make_async_copy(out.at[:, c], out_hbm.at[:, c], leave.at[c])
        copy.start()
        leaving.append(copy)
    for copy in leaving:
        copy.wait()


def grid_tile(chunk, offsets, counts, piece, forward, inverse, blocks, turned, samples):
    def kernel(*refs):
        grid_kernel(chunk, *refs)

    return pl.pallas_call(
        kernel,
        out_shape=hbm((TILES, PER, KYD, 16, Z), BF),
        in_specs=[SMEM, SMEM, HBM if chunk == 0 else VMEM, VMEM, VMEM, HBM, HBM, HBM],
        out_specs=HBM,
        scratch_shapes=[
            pltpu.VMEM((TILES, PER, KYD, 16, Z) if chunk == 0 else (16, Z), BF),
            pltpu.VMEM((CH, P_SIZE, CELLS), BF),
            pltpu.VMEM((CH, CELLS, P_SIZE), BF),
            pltpu.VMEM((CH, P_SIZE, 2 * Z * PER), BF),
            pltpu.VMEM((2, ROWS, 2 * Z * PER), BF),
            pltpu.VMEM((2 * PER, ROWS + KYD, Z), F32),
            pltpu.VMEM((PER, 2 * ROWS, Z), F32),
            pltpu.VMEM((TILES, PER, KYD, 16, Z), BF),
            DMA((2 + PER, CH)),
            DMA((PER + 1,)),
        ],
        compiler_params=pltpu.CompilerParams(vmem_limit_bytes=34 << 20),
        name=f"grid_tile_{chunk}",
    )(offsets, counts, piece, forward, inverse, blocks, turned, samples)


def combine(adjoint, sens, x, before):
    g_re, g_im = before
    for c in range(PER):
        lanes = slice(c * Z, (c + 1) * Z)
        a_re = adjoint[:N, lanes]
        a_im = adjoint[N:, lanes]
        s_re = sens[c, 0, x].astype(F32)
        s_im = sens[c, 1, x].astype(F32)
        t_re = s_re * a_re + s_im * a_im
        t_im = s_re * a_im - s_im * a_re
        g_re = t_re if g_re is None else g_re + t_re
        g_im = t_im if g_im is None else g_im + t_im
    return g_re, g_im


def adjoint_row(table_ref, piece, x):
    data = jnp.concatenate([piece[:, c, x].reshape(2 * N, Z) for c in range(PER)], 1)
    return jnp.dot(table_ref[...], data, preferred_element_type=F32).astype(BF).astype(F32)


def gradient_first_kernel(table_ref, piece_hbm, sens_hbm, out_ref, piece, sens, sems):
    copies = [
        pltpu.make_async_copy(piece_hbm, piece, sems.at[0]),
        pltpu.make_async_copy(sens_hbm.at[pl.ds(0, PER)], sens, sems.at[1]),
    ]
    for copy in copies:
        copy.start()
    for copy in copies:
        copy.wait()

    def row(x, carry):
        g_re, g_im = combine(adjoint_row(table_ref, piece, x), sens, x, (None, None))
        out_ref[0, x] = g_re
        out_ref[1, x] = g_im
        return carry

    lax.fori_loop(0, KYD, row, 0)


def gradient_first(table, piece, sensitivity):
    return pl.pallas_call(
        gradient_first_kernel,
        out_shape=jax.ShapeDtypeStruct((2, KYD, N, Z), F32),
        in_specs=[VMEM, HBM, HBM],
        out_specs=VMEM,
        scratch_shapes=[
            pltpu.VMEM((TILES, PER, KYD, 16, Z), BF),
            pltpu.VMEM((PER, 2, KYD, N, Z), BF),
            DMA((2,)),
        ],
        compiler_params=pltpu.CompilerParams(vmem_limit_bytes=12 << 20),
        name="gradient_first",
    )(table, piece, sensitivity)


def gradient_last_kernel(position_ref, table_ref, piece_hbm, sens_hbm, before_ref, *rest):
    near_send, far_send, mine, near_keep, far_keep = rest[:5]
    piece, sens, out, arrive, sems = rest[5:]
    me = position_ref[0]
    near = me + 1 - 2 * lax.rem(me, 2)
    far = NCOIL - 1 - me
    across = NCOIL - 1 - near
    span = KYD // 2

    def arrivals(stage):
        rows = pl.ds(stage * span, span)
        return (
            pltpu.make_async_copy(
                piece_hbm.at[:, :, rows], piece.at[:, :, rows], arrive.at[0, stage]
            ),
            pltpu.make_async_copy(
                sens_hbm.at[pl.ds(PER, PER), :, rows], sens.at[:, :, rows], arrive.at[1, stage]
            ),
        )

    def departures(stage):
        rows = pl.ds(stage * span, span)
        first, keep = ((near, far), (far, near))[stage]
        send, kept = ((near_send, near_keep), (far_send, far_keep))[stage]
        pairs = (
            (first, send.at[0]),
            (across, send.at[1]),
            (keep, kept),
            (me, mine.at[:, rows]),
        )
        return [
            pltpu.make_async_copy(out.at[target, :, rows], place, sems.at[stage, k])
            for k, (target, place) in enumerate(pairs)
        ]

    for stage in range(2):
        for copy in arrivals(stage):
            copy.start()
    leaving = []
    for stage in range(2):
        for copy in arrivals(stage):
            copy.wait()
        for x in range(stage * span, (stage + 1) * span):
            g_re, g_im = combine(
                adjoint_row(table_ref, piece, x), sens, x, (before_ref[0, x], before_ref[1, x])
            )
            out[:, 0, x] = g_re.astype(BF).reshape(NCOIL, N // NCOIL, Z)
            out[:, 1, x] = g_im.astype(BF).reshape(NCOIL, N // NCOIL, Z)
        for copy in departures(stage):
            copy.start()
            leaving.append(copy)
    for copy in leaving:
        copy.wait()


def gradient_last(position, table, piece, sens, before):
    share = (2, KYD, N // NCOIL, Z)
    half = (2, KYD // 2, N // NCOIL, Z)
    shapes = ((2,) + half, (2,) + half, share, half, half)
    return pl.pallas_call(
        gradient_last_kernel,
        out_shape=tuple(hbm(shape, BF) for shape in shapes),
        in_specs=[SMEM, VMEM, HBM, HBM, VMEM],
        out_specs=(HBM,) * 5,
        scratch_shapes=[
            pltpu.VMEM((TILES, PER, KYD, 16, Z), BF),
            pltpu.VMEM((PER, 2, KYD, N, Z), BF),
            pltpu.VMEM((NCOIL,) + share, BF),
            DMA((2, 2)),
            DMA((2, 4)),
        ],
        compiler_params=pltpu.CompilerParams(vmem_limit_bytes=12 << 20),
        name="gradient_last",
    )(position, table, piece, sens, before)


def sum_over_planes(near_send, far_send, mine, near_keep, far_keep):
    near = [(i, i ^ 1) for i in range(NCOIL)]
    far = [(i, NCOIL - 1 - i) for i in range(NCOIL)]
    near_got = lax.ppermute(near_send, "coil", near)
    far_got = lax.ppermute(far_send, "coil", far)
    near_pass = (near_keep.astype(F32) + near_got[1].astype(F32)).astype(BF)
    far_pass = (far_keep.astype(F32) + far_got[1].astype(F32)).astype(BF)
    return (
        mine,
        near_got,
        far_got,
        lax.ppermute(near_pass, "coil", far),
        lax.ppermute(far_pass, "coil", near),
    )


def haar_rows(top, low):
    add = (top + low) * 0.5
    sub = (top - low) * 0.5
    cols = top.shape[0]
    odd = lax.broadcasted_iota(jnp.int32, top.shape, 0) % 2 == 1

    def pairs(v):
        ahead = pltpu.roll(v, cols - 1, 0)
        behind = pltpu.roll(v, 1, 0)
        return jnp.where(odd, behind - v, v + ahead)

    return pairs(add), pairs(sub)


def target_kernel(position_ref, image_hbm, aux_ref, dual_ref, out_ref, image, sem):
    share = N // NCOIL
    columns = pl.ds(pl.multiple_of(position_ref[0] * share, share), share)
    copy = pltpu.make_async_copy(image_hbm.at[:, :, columns], image, sem)
    copy.start()
    copy.wait()
    for m in range(KYD // 2):
        for part in range(2):
            rows = haar_rows(
                *(aux_ref[part, 2 * m + i] - dual_ref[part, 2 * m + i] for i in range(2))
            )
            for i in range(2):
                current = image[part, 2 * m + i]
                out_ref[part, 2 * m + i] = current - step_size * penalty * (current - rows[i])


def target_step(position, image, auxiliary, scaled_dual):
    return pl.pallas_call(
        target_kernel,
        out_shape=jax.ShapeDtypeStruct(auxiliary.shape, F32),
        in_specs=[SMEM, HBM, VMEM, VMEM],
        out_specs=VMEM,
        scratch_shapes=[pltpu.VMEM(auxiliary.shape, F32), DMA],
        compiler_params=pltpu.CompilerParams(vmem_limit_bytes=6 << 20),
        name="target",
    )(position, image, auxiliary, scaled_dual)


def update_kernel(
    base_ref,
    mine,
    near,
    far,
    near_last,
    far_last,
    dual_ref,
    image_hbm,
    aux_hbm,
    dual_hbm,
    image,
    aux,
    dual,
    sems,
):
    span = KYD // 2
    leaving = []
    for m in range(KYD // 2):
        coeffs = []
        for part in range(2):
            rows = []
            for x in (2 * m, 2 * m + 1):
                first, second = ((near, near_last), (far, far_last))[x // span]
                gradient = (
                    mine[part, x].astype(F32)
                    + first[0, part, x % span].astype(F32)
                    + second[part, x % span].astype(F32)
                )
                value = base_ref[part, x] - step_size * gradient
                image[part, x] = value
                rows.append(value)
            top, low = haar_rows(*rows)
            coeffs.append((top + dual_ref[part, 2 * m], low + dual_ref[part, 2 * m + 1]))
        for i in range(2):
            c_re = coeffs[0][i]
            c_im = coeffs[1][i]
            magnitude = jnp.sqrt(c_re * c_re + c_im * c_im)
            factor = jnp.maximum(1.0 - threshold / jnp.maximum(magnitude, threshold), 0.0)
            for part, value in enumerate((c_re, c_im)):
                kept = value * factor
                aux[part, 2 * m + i] = kept
                dual[part, 2 * m + i] = value - kept
        pair = pl.ds(2 * m, 2)
        for k, (held, place) in enumerate(((image, image_hbm), (aux, aux_hbm), (dual, dual_hbm))):
            copy = pltpu.make_async_copy(held.at[:, pair], place.at[:, pair], sems.at[k, m])
            copy.start()
            leaving.append(copy)
    for copy in leaving:
        copy.wait()


def update_step(base, shares, scaled_dual):
    shape = hbm(scaled_dual.shape, F32)
    return pl.pallas_call(
        update_kernel,
        out_shape=(shape, shape, shape),
        in_specs=[VMEM] * 7,
        out_specs=(HBM, HBM, HBM),
        scratch_shapes=[pltpu.VMEM(scaled_dual.shape, F32)] * 3 + [DMA((3, KYD // 2))],
        compiler_params=pltpu.CompilerParams(vmem_limit_bytes=8 << 20),
        name="update",
    )(base, *shares, scaled_dual)


def body(image, sensitivity, blocks, samples, offsets, counts, auxiliary, scaled_dual):
    along_y, along_x = real_tables()
    y_forward, x_forward = jnp.asarray(along_y), jnp.asarray(along_x)
    y_kept, x_kept = lax.optimization_barrier((y_forward, x_forward))
    y_inverse = y_kept.T
    x_inverse = x_kept.T

    image, sensitivity = in_hbm(image), in_hbm(sensitivity)
    y_forward = in_hbm(y_forward)
    turned = jnp.swapaxes(blocks[0], 1, 2)
    by_coil = samples_by_coil(counts, in_hbm(samples.reshape(CH, P_SIZE, 2 * NCOIL, Z)))

    chunks = range(NCOIL // PER)
    pieces = []
    for chunk in chunks:
        half = coil_forward(chunk, y_forward, sensitivity, image)
        if chunk == 1:
            half, turned, by_coil, y_inverse, x_inverse = lax.optimization_barrier(
                (half, turned, by_coil, y_inverse, x_inverse)
            )
        piece = lax.all_to_all(half, "slab", 0, 0, tiled=True)
        pieces.append(piece)
    position = lax.axis_index("coil").reshape(1)
    base = target_step(position, image, auxiliary, scaled_dual)
    backs = []
    for chunk in chunks:
        back = grid_tile(
            chunk,
            offsets,
            counts,
            in_hbm(pieces[chunk]) if chunk == 0 else pieces[chunk],
            x_forward,
            x_inverse,
            in_hbm(blocks[0]),
            in_hbm(turned),
            in_hbm(by_coil),
        )
        backs.append(lax.all_to_all(back, "slab", 0, 0, tiled=True))
    first, last = backs
    before = gradient_first(y_inverse, in_hbm(first), sensitivity)
    shares = gradient_last(position, y_inverse, in_hbm(last), sensitivity, before)
    return update_step(base, sum_over_planes(*shares), scaled_dual)


def solution(mesh):
    return jax.shard_map(
        body,
        mesh=mesh,
        in_specs=(
            P(None, "slab", None, None),
            P("coil", None, "slab", None, None),
            P("slab", None, None, None),
            P("slab", None, None, "coil", None, None),
            P("slab", None),
            P("slab"),
            P(None, "slab", "coil", None),
            P(None, "slab", "coil", None),
        ),
        out_specs=(
            P(None, "slab", "coil", None),
            P(None, "slab", "coil", None),
            P(None, "slab", "coil", None),
        ),
        check_vma=False,
    )
```

```python
import math

import jax
import jax.numpy as jnp
import numpy as np
import ml_dtypes
from jax import lax
from jax.experimental import pallas as pl
from jax.experimental.pallas import tpu as pltpu
from jax.sharding import PartitionSpec as P

N = 256
Z = 128
WIN = 64
P_SIZE = 128
CH = 24
KYD = 8
TILES = 32
CELLS = WIN * KYD
ROWS = N * KYD
NCOIL = 4
PER = 2

step_size = 0.5
penalty = 1.0
threshold = 0.3

BF = jnp.bfloat16
F32 = jnp.float32


def dft_parts():
    index = np.arange(N)
    angle = (index[:, None] * index[None, :] % N).astype(np.float32) * np.float32(2.0 * math.pi / N)
    factor = np.float32(1.0 / math.sqrt(N))
    re = (np.cos(angle) * factor).astype(ml_dtypes.bfloat16)
    im = (-np.sin(angle) * factor).astype(ml_dtypes.bfloat16)
    return re, im


def real_tables():
    re, im = dft_parts()
    along_y = np.stack(
        [np.concatenate([re, -im], 1), np.concatenate([im, re], 1)], 1
    ).reshape(2 * N, 2 * N)
    along_x = np.concatenate([np.concatenate([re, -im], 1), np.concatenate([im, re], 1)], 0)
    return along_y, along_x


def hbm(shape, dtype):
    return pltpu.HBM(shape, dtype)


def in_hbm(x):
    return pltpu.with_memory_space_constraint(x, pltpu.HBM)


VMEM = pl.BlockSpec(memory_space=pltpu.VMEM)
SMEM = pl.BlockSpec(memory_space=pltpu.SMEM)
HBM = pl.BlockSpec(memory_space=pltpu.HBM)
DMA = pltpu.SemaphoreType.DMA


def coil_kernel(chunk, table_hbm, sens_hbm, image_hbm, out_hbm, table, sens, image, out, sems, leave):
    stages = 2
    span = KYD // stages

    def sens_copy(c, stage):
        rows = pl.ds(stage * span, span)
        return pltpu.make_async_copy(
            sens_hbm.at[chunk * PER + c, :, rows], sens.at[c, :, rows], sems.at[c, stage]
        )

    def image_copy(stage):
        rows = pl.ds(stage * span, span)
        return pltpu.make_async_copy(image_hbm.at[:, rows], image.at[:, rows], sems.at[PER, stage])

    def leave_copy(c, stage):
        rows = pl.ds(stage * span, span)
        return pltpu.make_async_copy(out.at[:, c, rows], out_hbm.at[:, c, rows], leave.at[c, stage])

    whole = pltpu.make_async_copy(table_hbm, table, leave.at[PER, 0])
    whole.start()
    for stage in range(stages):
        image_copy(stage).start()
        sens_copy(0, stage).start()
    for c in range(1, PER):
        for stage in range(stages):
            sens_copy(c, stage).start()
    whole.wait()

    def one_coil(c, arrive):
        for stage in range(stages):
            arrive(c, stage)
            for pair in range(span // 2):
                first = stage * span + 2 * pair
                parts = []
                for x in (first, first + 1):
                    s_re = sens[c, 0, x].astype(F32)
                    s_im = sens[c, 1, x].astype(F32)
                    m_re = image[0, x]
                    m_im = image[1, x]
                    c_re = (s_re * m_re - s_im * m_im).astype(BF)
                    c_im = (s_re * m_im + s_im * m_re).astype(BF)
                    parts.append(jnp.concatenate([c_re, c_im], 0))
                data = jnp.concatenate(parts, 1)
                result = jnp.dot(table[...], data, preferred_element_type=F32).astype(BF)
                for i in range(2):
                    out[:, c, first + i] = result[:, i * Z : (i + 1) * Z].reshape(TILES, 16, Z)
            leave_copy(c, stage).start()

    def arrive_staged(c, stage):
        if c == 0:
            image_copy(stage).wait()
        sens_copy(c, stage).wait()

    if chunk == 0:
        for c in range(PER):
            one_coil(c, arrive_staged)
    else:
        for stage in range(stages):
            for c in range(PER):
                arrive_staged(c, stage)

        def rolled(c, carry):
            one_coil(c, lambda c, stage: None)
            return carry

        lax.fori_loop(0, PER, rolled, 0)
    for c in range(PER):
        for stage in range(stages):
            leave_copy(c, stage).wait()


def coil_forward(chunk, table, sensitivity, image):
    def kernel(*refs):
        coil_kernel(chunk, *refs)

    return pl.pallas_call(
        kernel,
        out_shape=hbm((TILES, PER, KYD, 16, Z), BF),
        in_specs=[HBM, HBM, HBM],
        out_specs=HBM,
        scratch_shapes=[
            pltpu.VMEM((2 * N, 2 * N), BF),
            pltpu.VMEM((PER, 2, KYD, N, Z), BF),
            pltpu.VMEM((2, KYD, N, Z), F32),
            pltpu.VMEM((TILES, PER, KYD, 16, Z), BF),
            DMA((PER + 1, 2)),
            DMA((PER + 1, 2)),
        ],
        compiler_params=pltpu.CompilerParams(vmem_limit_bytes=14 << 20),
        name=f"coil_forward_{chunk}",
    )(table, sensitivity, image)


def samples_kernel(counts_ref, samples_hbm, out_hbm, samples, spread, out, arrive, leave):
    count = counts_ref[0]

    def into(j):
        return pltpu.make_async_copy(samples_hbm.at[j], samples.at[j], arrive.at[j])

    def back(j):
        return pltpu.make_async_copy(out.at[:, j], out_hbm.at[:, j], leave.at[j])

    def start(j, carry):
        into(j).start()
        return carry

    def group(j, carry):
        into(j).wait()
        slot = j % 2
        spread[slot] = samples[j].astype(F32).reshape(P_SIZE * 8, Z)
        for coil in range(NCOIL):
            for part in range(2):
                out[coil, j, :, part * Z : (part + 1) * Z] = spread[
                    slot, pl.ds(2 * coil + part, P_SIZE, stride=8), :
                ].astype(BF)
        back(j).start()
        return carry

    def finish(j, carry):
        back(j).wait()
        return carry

    lax.fori_loop(0, count, start, 0)
    lax.fori_loop(0, count, group, 0)
    lax.fori_loop(0, count, finish, 0)


def samples_by_coil(counts, samples):
    return pl.pallas_call(
        samples_kernel,
        out_shape=hbm((NCOIL, CH, P_SIZE, 2 * Z), BF),
        in_specs=[SMEM, HBM],
        out_specs=HBM,
        scratch_shapes=[
            pltpu.VMEM((CH, P_SIZE, 8, Z), BF),
            pltpu.VMEM((2, P_SIZE * 8, Z), F32),
            pltpu.VMEM((NCOIL, CH, P_SIZE, 2 * Z), BF),
            DMA((CH,)),
            DMA((CH,)),
        ],
        compiler_params=pltpu.CompilerParams(vmem_limit_bytes=18 << 20),
        name="samples_by_coil",
    )(counts, samples)


def grid_kernel(
    chunk,
    offsets_ref,
    counts_ref,
    piece_hbm,
    forward_ref,
    inverse_ref,
    blocks_hbm,
    turned_hbm,
    samples_hbm,
    out_hbm,
    piece,
    blocks,
    turned,
    samples,
    window,
    total,
    spread,
    out,
    sems,
    leave,
):
    count = counts_ref[0]
    if chunk == 0:
        arrival = pltpu.make_async_copy(piece_hbm, piece, leave.at[PER])
        arrival.start()
    else:
        piece = piece_hbm

    def copies(j):
        return [
            pltpu.make_async_copy(blocks_hbm.at[j], blocks.at[j], sems.at[0, j]),
            pltpu.make_async_copy(turned_hbm.at[j], turned.at[j], sems.at[1, j]),
        ] + [
            pltpu.make_async_copy(
                samples_hbm.at[chunk * PER + c, j],
                samples.at[j, :, pl.ds(2 * Z * c, 2 * Z)],
                sems.at[2 + c, j],
            )
            for c in range(PER)
        ]

    def start(j, carry):
        for copy in copies(j):
            copy.start()
        return carry

    lax.fori_loop(0, count, start, 0)

    if chunk == 0:
        arrival.wait()

    for c in range(PER):
        spread[c] = piece[:, c].astype(F32).reshape(ROWS * 2, Z)

    def forward_row(ky, carry):
        data = jnp.concatenate(
            [
                jnp.concatenate(
                    [
                        spread[c, pl.ds(2 * ky + part, N, stride=2 * KYD), :].astype(BF)
                        for part in range(2)
                    ],
                    0,
                )
                for c in range(PER)
            ],
            1,
        )
        result = jnp.dot(forward_ref[...], data, preferred_element_type=F32)
        for c in range(PER):
            for part in range(2):
                total[2 * c + part, pl.ds(ky, N, stride=KYD), :] = result[
                    part * N : (part + 1) * N, c * Z : (c + 1) * Z
                ]
        return carry

    lax.fori_loop(0, KYD, forward_row, 0)
    for s in range(2 * PER):
        lanes = slice(s * Z, (s + 1) * Z)
        total[s, ROWS : ROWS + KYD, :] = jnp.zeros((KYD, Z), F32)
        window[0, :, lanes] = total[s, 0:ROWS, :].astype(BF)
        window[1, :, lanes] = total[s, KYD : ROWS + KYD, :].astype(BF)
    total[...] = jnp.zeros_like(total)

    def arrive(j):
        for copy in copies(j):
            copy.wait()

    def predict(j):
        first = offsets_ref[0, j]
        row = pl.multiple_of((first // 2) * (2 * KYD), 2 * KYD)
        view = window[first % 2, pl.ds(row, CELLS), :]
        predicted = jnp.dot(blocks[j], view, preferred_element_type=F32)
        return (predicted - samples[j].astype(F32)).astype(BF)

    def add_back(j, misfit):
        update = jnp.dot(turned[j], misfit, preferred_element_type=F32)
        spot = pl.ds(pl.multiple_of(offsets_ref[0, j] * KYD, KYD), CELLS)
        for s in range(2 * PER):
            total[s, spot, :] = total[s, spot, :] + update[:, s * Z : (s + 1) * Z]

    arrive(0)
    samples[0] = predict(0)

    def group(j, carry):
        arrive(j)
        before = samples[j - 1]
        misfit = predict(j)
        add_back(j - 1, before)
        samples[j] = misfit
        return carry

    lax.fori_loop(1, count, group, 0)
    add_back(count - 1, samples[count - 1])

    leaving = []
    for c in range(PER):

        def inverse_rows(pair, carry):
            data = jnp.concatenate(
                [
                    jnp.concatenate(
                        [
                            total[2 * c + part, pl.ds(2 * pair + i, N, stride=KYD), :].astype(BF)
                            for part in range(2)
                        ],
                        0,
                    )
                    for i in range(2)
                ],
                1,
            )
            result = jnp.dot(inverse_ref[...], data, preferred_element_type=F32)
            for i in range(2):
                for part in range(2):
                    spread[c, pl.ds(2 * (2 * pair + i) + part, N, stride=2 * KYD), :] = result[
                        part * N : (part + 1) * N, i * Z : (i + 1) * Z
                    ]
            return carry

        lax.fori_loop(0, KYD // 2, inverse_rows, 0)
        out[:, c] = spread[c].astype(BF).reshape(TILES, KYD, 16, Z)
        copy = pltpu.make_async_copy(out.at[:, c], out_hbm.at[:, c], leave.at[c])
        copy.start()
        leaving.append(copy)
    for copy in leaving:
        copy.wait()


def grid_tile(chunk, offsets, counts, piece, forward, inverse, blocks, turned, samples):
    def kernel(*refs):
        grid_kernel(chunk, *refs)

    return pl.pallas_call(
        kernel,
        out_shape=hbm((TILES, PER, KYD, 16, Z), BF),
        in_specs=[SMEM, SMEM, HBM if chunk == 0 else VMEM, VMEM, VMEM, HBM, HBM, HBM],
        out_specs=HBM,
        scratch_shapes=[
            pltpu.VMEM((TILES, PER, KYD, 16, Z) if chunk == 0 else (16, Z), BF),
            pltpu.VMEM((CH, P_SIZE, CELLS), BF),
            pltpu.VMEM((CH, CELLS, P_SIZE), BF),
            pltpu.VMEM((CH, P_SIZE, 2 * Z * PER), BF),
            pltpu.VMEM((2, ROWS, 2 * Z * PER), BF),
            pltpu.VMEM((2 * PER, ROWS + KYD, Z), F32),
            pltpu.VMEM((PER, 2 * ROWS, Z), F32),
            pltpu.VMEM((TILES, PER, KYD, 16, Z), BF),
            DMA((2 + PER, CH)),
            DMA((PER + 1,)),
        ],
        compiler_params=pltpu.CompilerParams(vmem_limit_bytes=34 << 20),
        name=f"grid_tile_{chunk}",
    )(offsets, counts, piece, forward, inverse, blocks, turned, samples)


def combine(adjoint, sens, x, before):
    g_re, g_im = before
    for c in range(PER):
        lanes = slice(c * Z, (c + 1) * Z)
        a_re = adjoint[:N, lanes]
        a_im = adjoint[N:, lanes]
        s_re = sens[c, 0, x].astype(F32)
        s_im = sens[c, 1, x].astype(F32)
        t_re = s_re * a_re + s_im * a_im
        t_im = s_re * a_im - s_im * a_re
        g_re = t_re if g_re is None else g_re + t_re
        g_im = t_im if g_im is None else g_im + t_im
    return g_re, g_im


def adjoint_row(table_ref, piece, x):
    data = jnp.concatenate([piece[:, c, x].reshape(2 * N, Z) for c in range(PER)], 1)
    return jnp.dot(table_ref[...], data, preferred_element_type=F32).astype(BF).astype(F32)


def gradient_first_kernel(table_ref, piece_hbm, sens_hbm, out_ref, piece, sens, sems):
    copies = [
        pltpu.make_async_copy(piece_hbm, piece, sems.at[0]),
        pltpu.make_async_copy(sens_hbm.at[pl.ds(0, PER)], sens, sems.at[1]),
    ]
    for copy in copies:
        copy.start()
    for copy in copies:
        copy.wait()

    def row(x, carry):
        g_re, g_im = combine(adjoint_row(table_ref, piece, x), sens, x, (None, None))
        out_ref[0, x] = g_re
        out_ref[1, x] = g_im
        return carry

    lax.fori_loop(0, KYD, row, 0)


def gradient_first(table, piece, sensitivity):
    return pl.pallas_call(
        gradient_first_kernel,
        out_shape=jax.ShapeDtypeStruct((2, KYD, N, Z), F32),
        in_specs=[VMEM, HBM, HBM],
        out_specs=VMEM,
        scratch_shapes=[
            pltpu.VMEM((TILES, PER, KYD, 16, Z), BF),
            pltpu.VMEM((PER, 2, KYD, N, Z), BF),
            DMA((2,)),
        ],
        compiler_params=pltpu.CompilerParams(vmem_limit_bytes=12 << 20),
        name="gradient_first",
    )(table, piece, sensitivity)


def gradient_last_kernel(position_ref, table_ref, piece_hbm, sens_hbm, before_ref, *rest):
    shares = rest[:NCOIL]
    piece, sens, out, arrive, sems = rest[NCOIL:]
    position = position_ref[0]
    span = KYD // 2

    def arrivals(stage):
        rows = pl.ds(stage * span, span)
        return (
            pltpu.make_async_copy(
                piece_hbm.at[:, :, rows], piece.at[:, :, rows], arrive.at[0, stage]
            ),
            pltpu.make_async_copy(
                sens_hbm.at[pl.ds(PER, PER), :, rows], sens.at[:, :, rows], arrive.at[1, stage]
            ),
        )

    def leave(k, stage):
        rows = pl.ds(stage * span, span)
        target = lax.rem(position + k, NCOIL)
        return pltpu.make_async_copy(
            out.at[target, :, rows], shares[k].at[:, rows], sems.at[k, stage]
        )

    for stage in range(2):
        for copy in arrivals(stage):
            copy.start()
    for stage in range(2):
        for copy in arrivals(stage):
            copy.wait()
        for x in range(stage * span, (stage + 1) * span):
            g_re, g_im = combine(
                adjoint_row(table_ref, piece, x), sens, x, (before_ref[0, x], before_ref[1, x])
            )
            out[:, 0, x] = g_re.astype(BF).reshape(NCOIL, N // NCOIL, Z)
            out[:, 1, x] = g_im.astype(BF).reshape(NCOIL, N // NCOIL, Z)
        for k in range(NCOIL):
            leave(k, stage).start()
    for stage in range(2):
        for k in range(NCOIL):
            leave(k, stage).wait()


def gradient_last(position, table, piece, sens, before):
    share = (2, KYD, N // NCOIL, Z)
    return pl.pallas_call(
        gradient_last_kernel,
        out_shape=(hbm(share, BF),) * NCOIL,
        in_specs=[SMEM, VMEM, HBM, HBM, VMEM],
        out_specs=(HBM,) * NCOIL,
        scratch_shapes=[
            pltpu.VMEM((TILES, PER, KYD, 16, Z), BF),
            pltpu.VMEM((PER, 2, KYD, N, Z), BF),
            pltpu.VMEM((NCOIL,) + share, BF),
            DMA((2, 2)),
            DMA((NCOIL, 2)),
        ],
        compiler_params=pltpu.CompilerParams(vmem_limit_bytes=12 << 20),
        name="gradient_last",
    )(position, table, piece, sens, before)


def haar_rows(top, low):
    add = (top + low) * 0.5
    sub = (top - low) * 0.5
    cols = top.shape[0]
    odd = lax.broadcasted_iota(jnp.int32, top.shape, 0) % 2 == 1

    def pairs(v):
        ahead = pltpu.roll(v, cols - 1, 0)
        behind = pltpu.roll(v, 1, 0)
        return jnp.where(odd, behind - v, v + ahead)

    return pairs(add), pairs(sub)


def target_kernel(position_ref, image_hbm, aux_ref, dual_ref, out_ref, image, sem):
    share = N // NCOIL
    columns = pl.ds(pl.multiple_of(position_ref[0] * share, share), share)
    copy = pltpu.make_async_copy(image_hbm.at[:, :, columns], image, sem)
    copy.start()
    copy.wait()
    for m in range(KYD // 2):
        for part in range(2):
            rows = haar_rows(
                *(aux_ref[part, 2 * m + i] - dual_ref[part, 2 * m + i] for i in range(2))
            )
            for i in range(2):
                current = image[part, 2 * m + i]
                out_ref[part, 2 * m + i] = current - step_size * penalty * (current - rows[i])


def target_step(position, image, auxiliary, scaled_dual):
    return pl.pallas_call(
        target_kernel,
        out_shape=jax.ShapeDtypeStruct(auxiliary.shape, F32),
        in_specs=[SMEM, HBM, VMEM, VMEM],
        out_specs=VMEM,
        scratch_shapes=[pltpu.VMEM(auxiliary.shape, F32), DMA],
        compiler_params=pltpu.CompilerParams(vmem_limit_bytes=6 << 20),
        name="target",
    )(position, image, auxiliary, scaled_dual)


def update_kernel(
    base_ref, s0, s1, s2, s3, dual_ref, image_hbm, aux_hbm, dual_hbm, image, aux, dual, sems
):
    leaving = []
    for m in range(KYD // 2):
        coeffs = []
        for part in range(2):
            rows = []
            for x in (2 * m, 2 * m + 1):
                gradient = s0[part, x].astype(F32)
                for share in (s1, s2, s3):
                    gradient = gradient + share[part, x].astype(F32)
                value = base_ref[part, x] - step_size * gradient
                image[part, x] = value
                rows.append(value)
            top, low = haar_rows(*rows)
            coeffs.append((top + dual_ref[part, 2 * m], low + dual_ref[part, 2 * m + 1]))
        for i in range(2):
            c_re = coeffs[0][i]
            c_im = coeffs[1][i]
            magnitude = jnp.sqrt(c_re * c_re + c_im * c_im)
            factor = jnp.maximum(1.0 - threshold / jnp.maximum(magnitude, threshold), 0.0)
            for part, value in enumerate((c_re, c_im)):
                kept = value * factor
                aux[part, 2 * m + i] = kept
                dual[part, 2 * m + i] = value - kept
        pair = pl.ds(2 * m, 2)
        for k, (near, far) in enumerate(((image, image_hbm), (aux, aux_hbm), (dual, dual_hbm))):
            copy = pltpu.make_async_copy(near.at[:, pair], far.at[:, pair], sems.at[k, m])
            copy.start()
            leaving.append(copy)
    for copy in leaving:
        copy.wait()


def update_step(base, shares, scaled_dual):
    shape = hbm(scaled_dual.shape, F32)
    return pl.pallas_call(
        update_kernel,
        out_shape=(shape, shape, shape),
        in_specs=[VMEM] * (NCOIL + 2),
        out_specs=(HBM, HBM, HBM),
        scratch_shapes=[pltpu.VMEM(scaled_dual.shape, F32)] * 3 + [DMA((3, KYD // 2))],
        compiler_params=pltpu.CompilerParams(vmem_limit_bytes=8 << 20),
        name="update",
    )(base, *shares, scaled_dual)


def body(image, sensitivity, blocks, samples, offsets, counts, auxiliary, scaled_dual):
    along_y, along_x = real_tables()
    y_forward, x_forward = jnp.asarray(along_y), jnp.asarray(along_x)
    y_kept, x_kept = lax.optimization_barrier((y_forward, x_forward))
    y_inverse = y_kept.T
    x_inverse = x_kept.T

    image, sensitivity = in_hbm(image), in_hbm(sensitivity)
    y_forward = in_hbm(y_forward)
    turned = jnp.swapaxes(blocks[0], 1, 2)
    by_coil = samples_by_coil(counts, in_hbm(samples.reshape(CH, P_SIZE, 2 * NCOIL, Z)))

    chunks = range(NCOIL // PER)
    pieces = []
    for chunk in chunks:
        half = coil_forward(chunk, y_forward, sensitivity, image)
        if chunk == 1:
            half, turned, by_coil, y_inverse, x_inverse = lax.optimization_barrier(
                (half, turned, by_coil, y_inverse, x_inverse)
            )
        piece = lax.all_to_all(half, "slab", 0, 0, tiled=True)
        pieces.append(piece)
    position = lax.axis_index("coil").reshape(1)
    base = target_step(position, image, auxiliary, scaled_dual)
    backs = []
    for chunk in chunks:
        back = grid_tile(
            chunk,
            offsets,
            counts,
            in_hbm(pieces[chunk]) if chunk == 0 else pieces[chunk],
            x_forward,
            x_inverse,
            in_hbm(blocks[0]),
            in_hbm(turned),
            in_hbm(by_coil),
        )
        backs.append(lax.all_to_all(back, "slab", 0, 0, tiled=True))
    first, last = backs
    before = gradient_first(y_inverse, in_hbm(first), sensitivity)
    own, *others = gradient_last(position, y_inverse, in_hbm(last), sensitivity, before)
    shares = [own]
    for k in (2, 1, 3):
        ring = [(i, (i + k) % NCOIL) for i in range(NCOIL)]
        shares.append(lax.ppermute(others[k - 1], "coil", ring))
    return update_step(base, shares, scaled_dual)


def solution(mesh):
    return jax.shard_map(
        body,
        mesh=mesh,
        in_specs=(
            P(None, "slab", None, None),
            P("coil", None, "slab", None, None),
            P("slab", None, None, None),
            P("slab", None, None, "coil", None, None),
            P("slab", None),
            P("slab"),
            P(None, "slab", "coil", None),
            P(None, "slab", "coil", None),
        ),
        out_specs=(
            P(None, "slab", "coil", None),
            P(None, "slab", "coil", None),
            P(None, "slab", "coil", None),
        ),
        check_vma=False,
    )
```

```python
import math

import jax
import jax.numpy as jnp
import numpy as np
import ml_dtypes
from jax import lax
from jax.experimental import pallas as pl
from jax.experimental.pallas import tpu as pltpu
from jax.sharding import PartitionSpec as P

N = 256
Z = 128
WIN = 64
P_SIZE = 128
CH = 24
KYD = 8
TILES = 32
CELLS = WIN * KYD
ROWS = N * KYD
NCOIL = 4
PER = 2

step_size = 0.5
penalty = 1.0
threshold = 0.3

BF = jnp.bfloat16
F32 = jnp.float32


def dft_parts():
    index = np.arange(N)
    angle = (index[:, None] * index[None, :] % N).astype(np.float32) * np.float32(2.0 * math.pi / N)
    factor = np.float32(1.0 / math.sqrt(N))
    re = (np.cos(angle) * factor).astype(ml_dtypes.bfloat16)
    im = (-np.sin(angle) * factor).astype(ml_dtypes.bfloat16)
    return re, im


def real_tables():
    re, im = dft_parts()
    along_y = np.stack(
        [np.concatenate([re, -im], 1), np.concatenate([im, re], 1)], 1
    ).reshape(2 * N, 2 * N)
    along_x = np.concatenate([np.concatenate([re, -im], 1), np.concatenate([im, re], 1)], 0)
    return along_y, along_x


def hbm(shape, dtype):
    return pltpu.HBM(shape, dtype)


def in_hbm(x):
    return pltpu.with_memory_space_constraint(x, pltpu.HBM)


VMEM = pl.BlockSpec(memory_space=pltpu.VMEM)
SMEM = pl.BlockSpec(memory_space=pltpu.SMEM)
HBM = pl.BlockSpec(memory_space=pltpu.HBM)
DMA = pltpu.SemaphoreType.DMA


def pack(even, odd, half):
    low = lax.broadcasted_iota(jnp.int32, even.shape, 1) < Z // 2
    if half == 0:
        return jnp.where(low, even, pltpu.roll(odd, Z // 2, 1))
    return jnp.where(low, pltpu.roll(even, Z // 2, 1), odd)


def coil_kernel(half, table_hbm, sens_hbm, image_hbm, out_hbm, table, sens, image, out, sems, leave):
    stages = 2
    span = KYD // stages

    def copies(stage):
        rows = pl.ds(stage * span, span)
        return (
            pltpu.make_async_copy(image_hbm.at[:, rows], image.at[:, rows], sems.at[0, stage]),
            pltpu.make_async_copy(sens_hbm.at[:, :, rows], sens.at[:, :, rows], sems.at[1, stage]),
        )

    def leave_copy(stage):
        rows = pl.ds(stage * span, span)
        return pltpu.make_async_copy(out.at[:, :, rows], out_hbm.at[:, :, rows], leave.at[stage])

    whole = pltpu.make_async_copy(table_hbm, table, sems.at[2, 0])
    whole.start()
    for stage in range(stages):
        for copy in copies(stage):
            copy.start()
    whole.wait()

    def row(x):
        m_re = pack(image[0, x], image[0, x], half)
        m_im = pack(image[1, x], image[1, x], half)
        parts = []
        for pair in range(PER):
            s_re, s_im = (
                pack(*(sens[2 * pair + k, part, x].astype(F32) for k in range(2)), half)
                for part in range(2)
            )
            c_re = (s_re * m_re - s_im * m_im).astype(BF)
            c_im = (s_re * m_im + s_im * m_re).astype(BF)
            parts.append(jnp.concatenate([c_re, c_im], 0))
        data = jnp.concatenate(parts, 1)
        result = jnp.dot(table[...], data, preferred_element_type=F32).astype(BF)
        for pair in range(PER):
            out[:, pair, x] = result[:, pair * Z : (pair + 1) * Z].reshape(TILES, 16, Z)

    for stage in range(stages):
        for copy in copies(stage):
            copy.wait()
        if half == 0:
            for x in range(stage * span, (stage + 1) * span):
                row(x)
        else:

            def rolled(x, carry):
                row(x)
                return carry

            lax.fori_loop(stage * span, (stage + 1) * span, rolled, 0)
        leave_copy(stage).start()
    for stage in range(stages):
        leave_copy(stage).wait()


def coil_forward(half, table, sensitivity, image):
    def kernel(*refs):
        coil_kernel(half, *refs)

    return pl.pallas_call(
        kernel,
        out_shape=hbm((TILES, PER, KYD, 16, Z), BF),
        in_specs=[HBM, HBM, HBM],
        out_specs=HBM,
        scratch_shapes=[
            pltpu.VMEM((2 * N, 2 * N), BF),
            pltpu.VMEM((NCOIL, 2, KYD, N, Z), BF),
            pltpu.VMEM((2, KYD, N, Z), F32),
            pltpu.VMEM((TILES, PER, KYD, 16, Z), BF),
            DMA((3, 2)),
            DMA((2,)),
        ],
        compiler_params=pltpu.CompilerParams(vmem_limit_bytes=16 << 20),
        name=f"coil_forward_{half}",
    )(table, sensitivity, image)


def samples_kernel(counts_ref, samples_hbm, out_hbm, samples, spread, out, arrive, leave):
    count = counts_ref[0]

    def into(j):
        return pltpu.make_async_copy(samples_hbm.at[j], samples.at[j], arrive.at[j])

    def back(j):
        return pltpu.make_async_copy(out.at[:, j], out_hbm.at[:, j], leave.at[j])

    def start(j, carry):
        into(j).start()
        return carry

    def group(j, carry):
        into(j).wait()
        slot = j % 2
        spread[slot] = samples[j].astype(F32).reshape(P_SIZE * 8, Z)
        for pair in range(PER):
            for part in range(2):
                even, odd = (
                    spread[slot, pl.ds(2 * (2 * pair + k) + part, P_SIZE, stride=8), :]
                    for k in range(2)
                )
                for half in range(2):
                    out[half * PER + pair, j, :, part * Z : (part + 1) * Z] = pack(
                        even, odd, half
                    ).astype(BF)
        back(j).start()
        return carry

    def finish(j, carry):
        back(j).wait()
        return carry

    lax.fori_loop(0, count, start, 0)
    lax.fori_loop(0, count, group, 0)
    lax.fori_loop(0, count, finish, 0)


def samples_by_coil(counts, samples):
    return pl.pallas_call(
        samples_kernel,
        out_shape=hbm((NCOIL, CH, P_SIZE, 2 * Z), BF),
        in_specs=[SMEM, HBM],
        out_specs=HBM,
        scratch_shapes=[
            pltpu.VMEM((CH, P_SIZE, 8, Z), BF),
            pltpu.VMEM((2, P_SIZE * 8, Z), F32),
            pltpu.VMEM((NCOIL, CH, P_SIZE, 2 * Z), BF),
            DMA((CH,)),
            DMA((CH,)),
        ],
        compiler_params=pltpu.CompilerParams(vmem_limit_bytes=18 << 20),
        name="samples_by_coil",
    )(counts, samples)


def conjugate(values, part):
    return values if part == 0 else -values


def grid_kernel(
    chunk,
    offsets_ref,
    counts_ref,
    piece_hbm,
    table_ref,
    blocks_hbm,
    turned_hbm,
    samples_hbm,
    out_hbm,
    piece,
    blocks,
    turned,
    samples,
    window,
    total,
    spread,
    out,
    sems,
    leave,
):
    count = counts_ref[0]
    if chunk == 0:
        arrival = pltpu.make_async_copy(piece_hbm, piece, leave.at[PER])
        arrival.start()
    else:
        piece = piece_hbm

    def copies(j):
        return [
            pltpu.make_async_copy(blocks_hbm.at[j], blocks.at[j], sems.at[0, j]),
            pltpu.make_async_copy(turned_hbm.at[j], turned.at[j], sems.at[1, j]),
        ] + [
            pltpu.make_async_copy(
                samples_hbm.at[chunk * PER + c, j],
                samples.at[j, :, pl.ds(2 * Z * c, 2 * Z)],
                sems.at[2 + c, j],
            )
            for c in range(PER)
        ]

    def start(j, carry):
        for copy in copies(j):
            copy.start()
        return carry

    lax.fori_loop(0, count, start, 0)

    if chunk == 0:
        arrival.wait()

    for c in range(PER):
        spread[c] = piece[:, c].astype(F32).reshape(ROWS * 2, Z)

    def forward_row(ky, carry):
        data = jnp.concatenate(
            [
                jnp.concatenate(
                    [
                        spread[c, pl.ds(2 * ky + part, N, stride=2 * KYD), :].astype(BF)
                        for part in range(2)
                    ],
                    0,
                )
                for c in range(PER)
            ],
            1,
        )
        result = jnp.dot(table_ref[...], data, preferred_element_type=F32)
        for c in range(PER):
            for part in range(2):
                total[2 * c + part, pl.ds(ky, N, stride=KYD), :] = result[
                    part * N : (part + 1) * N, c * Z : (c + 1) * Z
                ]
        return carry

    lax.fori_loop(0, KYD, forward_row, 0)
    for s in range(2 * PER):
        lanes = slice(s * Z, (s + 1) * Z)
        total[s, ROWS : ROWS + KYD, :] = jnp.zeros((KYD, Z), F32)
        window[0, :, lanes] = total[s, 0:ROWS, :].astype(BF)
        window[1, :, lanes] = total[s, KYD : ROWS + KYD, :].astype(BF)
    total[...] = jnp.zeros_like(total)

    def arrive(j):
        for copy in copies(j):
            copy.wait()

    def predict(j):
        first = offsets_ref[0, j]
        row = pl.multiple_of((first // 2) * (2 * KYD), 2 * KYD)
        view = window[first % 2, pl.ds(row, CELLS), :]
        predicted = jnp.dot(blocks[j], view, preferred_element_type=F32)
        return (predicted - samples[j].astype(F32)).astype(BF)

    def add_back(j, misfit):
        update = jnp.dot(turned[j], misfit, preferred_element_type=F32)
        spot = pl.ds(pl.multiple_of(offsets_ref[0, j] * KYD, KYD), CELLS)
        for s in range(2 * PER):
            total[s, spot, :] = total[s, spot, :] + update[:, s * Z : (s + 1) * Z]

    arrive(0)
    samples[0] = predict(0)

    def group(j, carry):
        arrive(j)
        before = samples[j - 1]
        misfit = predict(j)
        add_back(j - 1, before)
        samples[j] = misfit
        return carry

    lax.fori_loop(1, count, group, 0)
    add_back(count - 1, samples[count - 1])

    leaving = []
    for c in range(PER):

        def inverse_rows(pair, carry):
            data = jnp.concatenate(
                [
                    jnp.concatenate(
                        [
                            conjugate(
                                total[2 * c + part, pl.ds(2 * pair + i, N, stride=KYD), :], part
                            ).astype(BF)
                            for part in range(2)
                        ],
                        0,
                    )
                    for i in range(2)
                ],
                1,
            )
            result = jnp.dot(table_ref[...], data, preferred_element_type=F32)
            for i in range(2):
                for part in range(2):
                    spread[c, pl.ds(2 * (2 * pair + i) + part, N, stride=2 * KYD), :] = conjugate(
                        result[part * N : (part + 1) * N, i * Z : (i + 1) * Z], part
                    )
            return carry

        lax.fori_loop(0, KYD // 2, inverse_rows, 0)
        out[:, c] = spread[c].astype(BF).reshape(TILES, KYD, 16, Z)
        copy = pltpu.make_async_copy(out.at[:, c], out_hbm.at[:, c], leave.at[c])
        copy.start()
        leaving.append(copy)
    for copy in leaving:
        copy.wait()


def grid_tile(chunk, offsets, counts, piece, table, blocks, turned, samples):
    def kernel(*refs):
        grid_kernel(chunk, *refs)

    return pl.pallas_call(
        kernel,
        out_shape=hbm((TILES, PER, KYD, 16, Z), BF),
        in_specs=[SMEM, SMEM, HBM if chunk == 0 else VMEM, VMEM, HBM, HBM, HBM],
        out_specs=HBM,
        scratch_shapes=[
            pltpu.VMEM((TILES, PER, KYD, 16, Z) if chunk == 0 else (16, Z), BF),
            pltpu.VMEM((CH, P_SIZE, CELLS), BF),
            pltpu.VMEM((CH, CELLS, P_SIZE), BF),
            pltpu.VMEM((CH, P_SIZE, 2 * Z * PER), BF),
            pltpu.VMEM((2, ROWS, 2 * Z * PER), BF),
            pltpu.VMEM((2 * PER, ROWS + KYD, Z), F32),
            pltpu.VMEM((PER, 2 * ROWS, Z), F32),
            pltpu.VMEM((TILES, PER, KYD, 16, Z), BF),
            DMA((2 + PER, CH)),
            DMA((PER + 1,)),
        ],
        compiler_params=pltpu.CompilerParams(vmem_limit_bytes=34 << 20),
        name=f"grid_tile_{chunk}",
    )(offsets, counts, piece, table, blocks, turned, samples)


def combine(adjoint, packed):
    g_re = g_im = None
    for pair in range(PER):
        lanes = slice(pair * Z, (pair + 1) * Z)
        a_re = adjoint[:N, lanes]
        a_im = adjoint[N:, lanes]
        s_re, s_im = packed[pair]
        t_re = s_re * a_re + s_im * a_im
        t_im = s_re * a_im - s_im * a_re
        g_re = t_re if g_re is None else g_re + t_re
        g_im = t_im if g_im is None else g_im + t_im
    low = lax.broadcasted_iota(jnp.int32, g_re.shape, 1) < Z // 2
    return jnp.where(low, g_re + pltpu.roll(g_re, Z // 2, 1), g_im + pltpu.roll(g_im, Z // 2, 1))


def adjoint_row(table_ref, piece, x):
    data = jnp.concatenate([piece[:, pair, x].reshape(2 * N, Z) for pair in range(PER)], 1)
    return jnp.dot(table_ref[...], data, preferred_element_type=F32).astype(BF).astype(F32)


def share_copies(position, out, shares, rows, sems):
    return [
        pltpu.make_async_copy(
            out.at[lax.rem(position + k, NCOIL), rows], shares[k].at[rows], sems.at[k]
        )
        for k in range(NCOIL)
    ]


def gradient_first_kernel(position_ref, table_ref, piece_hbm, sens_hbm, *rest):
    shares = rest[:NCOIL]
    later_hbm, piece, sens, later, out, arrive, sems, last = rest[NCOIL:]
    copies = [
        pltpu.make_async_copy(piece_hbm, piece, arrive.at[0]),
        pltpu.make_async_copy(sens_hbm, sens, arrive.at[1]),
    ]
    for copy in copies:
        copy.start()
    for copy in copies:
        copy.wait()

    def row(x, carry):
        packed = []
        for pair in range(PER):
            both = []
            for part in range(2):
                even, odd = (sens[2 * pair + k, part, x].astype(F32) for k in range(2))
                both.append(pack(even, odd, 0))
                later[pair, part, x] = pack(even, odd, 1).astype(BF)
            packed.append(both)
        gradient = combine(adjoint_row(table_ref, piece, x), packed)
        out[:, x] = gradient.astype(BF).reshape(NCOIL, N // NCOIL, Z)
        return carry

    lax.fori_loop(0, KYD, row, 0)
    leaving = share_copies(position_ref[0], out, shares, pl.ds(0, KYD), sems)
    leaving.append(pltpu.make_async_copy(later, later_hbm, last.at[0]))
    for copy in leaving:
        copy.start()
    for copy in leaving:
        copy.wait()


def gradient_first(position, table, piece, sensitivity):
    share = (KYD, N // NCOIL, Z)
    packed = (PER, 2, KYD, N, Z)
    return pl.pallas_call(
        gradient_first_kernel,
        out_shape=(hbm(share, BF),) * NCOIL + (hbm(packed, BF),),
        in_specs=[SMEM, VMEM, HBM, HBM],
        out_specs=(HBM,) * (NCOIL + 1),
        scratch_shapes=[
            pltpu.VMEM((TILES, PER, KYD, 16, Z), BF),
            pltpu.VMEM((NCOIL, 2, KYD, N, Z), BF),
            pltpu.VMEM(packed, BF),
            pltpu.VMEM((NCOIL,) + share, BF),
            DMA((2,)),
            DMA((NCOIL,)),
            DMA((1,)),
        ],
        compiler_params=pltpu.CompilerParams(vmem_limit_bytes=14 << 20),
        name="gradient_first",
    )(position, table, piece, sensitivity)


def gradient_last_kernel(position_ref, table_ref, piece, sens_hbm, *rest):
    shares = rest[:NCOIL]
    sens, out, arrive, sems = rest[NCOIL:]
    span = KYD // 2

    def arrivals(stage):
        rows = pl.ds(stage * span, span)
        return pltpu.make_async_copy(
            sens_hbm.at[:, :, rows], sens.at[:, :, rows], arrive.at[stage]
        )

    for stage in range(2):
        arrivals(stage).start()
    leaving = []
    for stage in range(2):
        arrivals(stage).wait()
        for x in range(stage * span, (stage + 1) * span):
            packed = [
                [sens[pair, part, x].astype(F32) for part in range(2)] for pair in range(PER)
            ]
            gradient = combine(adjoint_row(table_ref, piece, x), packed)
            out[:, x] = gradient.astype(BF).reshape(NCOIL, N // NCOIL, Z)
        rows = pl.ds(stage * span, span)
        for copy in share_copies(position_ref[0], out, shares, rows, sems.at[stage]):
            copy.start()
            leaving.append(copy)
    for copy in leaving:
        copy.wait()


def gradient_last(position, table, piece, packed):
    share = (KYD, N // NCOIL, Z)
    return pl.pallas_call(
        gradient_last_kernel,
        out_shape=(hbm(share, BF),) * NCOIL,
        in_specs=[SMEM, VMEM, VMEM, HBM],
        out_specs=(HBM,) * NCOIL,
        scratch_shapes=[
            pltpu.VMEM((PER, 2, KYD, N, Z), BF),
            pltpu.VMEM((NCOIL,) + share, BF),
            DMA((2,)),
            DMA((2, NCOIL)),
        ],
        compiler_params=pltpu.CompilerParams(vmem_limit_bytes=8 << 20),
        name="gradient_last",
    )(position, table, piece, packed)


def haar_rows(top, low):
    add = (top + low) * 0.5
    sub = (top - low) * 0.5
    cols = top.shape[0]
    odd = lax.broadcasted_iota(jnp.int32, top.shape, 0) % 2 == 1

    def pairs(v):
        ahead = pltpu.roll(v, cols - 1, 0)
        behind = pltpu.roll(v, 1, 0)
        return jnp.where(odd, behind - v, v + ahead)

    return pairs(add), pairs(sub)


def target_kernel(position_ref, image_hbm, aux_ref, dual_ref, out_ref, image, sem):
    share = N // NCOIL
    columns = pl.ds(pl.multiple_of(position_ref[0] * share, share), share)
    copy = pltpu.make_async_copy(image_hbm.at[:, :, columns], image, sem)
    copy.start()
    copy.wait()
    for m in range(KYD // 2):
        for part in range(2):
            rows = haar_rows(
                *(aux_ref[part, 2 * m + i] - dual_ref[part, 2 * m + i] for i in range(2))
            )
            for i in range(2):
                current = image[part, 2 * m + i]
                out_ref[part, 2 * m + i] = current - step_size * penalty * (current - rows[i])


def target_step(position, image, auxiliary, scaled_dual):
    return pl.pallas_call(
        target_kernel,
        out_shape=jax.ShapeDtypeStruct(auxiliary.shape, F32),
        in_specs=[SMEM, HBM, VMEM, VMEM],
        out_specs=VMEM,
        scratch_shapes=[pltpu.VMEM(auxiliary.shape, F32), DMA],
        compiler_params=pltpu.CompilerParams(vmem_limit_bytes=6 << 20),
        name="target",
    )(position, image, auxiliary, scaled_dual)


def update_kernel(base_ref, *rest):
    halves = (rest[:NCOIL], rest[NCOIL : 2 * NCOIL])
    dual_ref, image_hbm, aux_hbm, dual_hbm, image, aux, dual, sems = rest[2 * NCOIL :]
    low = lax.broadcasted_iota(jnp.int32, (N // NCOIL, Z), 1) < Z // 2
    leaving = []
    for m in range(KYD // 2):
        rows = ([], [])
        for x in (2 * m, 2 * m + 1):
            sums = []
            for shares in halves:
                total = shares[0][x].astype(F32)
                for share in shares[1:]:
                    total = total + share[x].astype(F32)
                sums.append(total)
            gradient = (
                jnp.where(low, sums[0], pltpu.roll(sums[1], Z // 2, 1)),
                jnp.where(low, pltpu.roll(sums[0], Z // 2, 1), sums[1]),
            )
            for part in range(2):
                value = base_ref[part, x] - step_size * gradient[part]
                image[part, x] = value
                rows[part].append(value)
        coeffs = []
        for part in range(2):
            top, bottom = haar_rows(*rows[part])
            coeffs.append((top + dual_ref[part, 2 * m], bottom + dual_ref[part, 2 * m + 1]))
        for i in range(2):
            c_re = coeffs[0][i]
            c_im = coeffs[1][i]
            magnitude = jnp.sqrt(c_re * c_re + c_im * c_im)
            factor = jnp.maximum(1.0 - threshold / jnp.maximum(magnitude, threshold), 0.0)
            for part, value in enumerate((c_re, c_im)):
                kept = value * factor
                aux[part, 2 * m + i] = kept
                dual[part, 2 * m + i] = value - kept
        pair = pl.ds(2 * m, 2)
        for k, (held, place) in enumerate(((image, image_hbm), (aux, aux_hbm), (dual, dual_hbm))):
            copy = pltpu.make_async_copy(held.at[:, pair], place.at[:, pair], sems.at[k, m])
            copy.start()
            leaving.append(copy)
    for copy in leaving:
        copy.wait()


def update_step(base, shares, scaled_dual):
    shape = hbm(scaled_dual.shape, F32)
    return pl.pallas_call(
        update_kernel,
        out_shape=(shape, shape, shape),
        in_specs=[VMEM] * (2 * NCOIL + 2),
        out_specs=(HBM, HBM, HBM),
        scratch_shapes=[pltpu.VMEM(scaled_dual.shape, F32)] * 3 + [DMA((3, KYD // 2))],
        compiler_params=pltpu.CompilerParams(vmem_limit_bytes=8 << 20),
        name="update",
    )(base, *shares, scaled_dual)


def over_planes(shares):
    own, *others = shares
    got = [own]
    for k in (2, 1, 3):
        ring = [(i, (i + k) % NCOIL) for i in range(NCOIL)]
        got.append(lax.ppermute(others[k - 1], "coil", ring))
    return got


def body(image, sensitivity, blocks, samples, offsets, counts, auxiliary, scaled_dual):
    along_y, along_x = real_tables()
    y_forward, x_forward = jnp.asarray(along_y), jnp.asarray(along_x)
    y_inverse = lax.optimization_barrier(y_forward).T

    image, sensitivity = in_hbm(image), in_hbm(sensitivity)
    y_forward = in_hbm(y_forward)
    turned = jnp.swapaxes(blocks[0], 1, 2)
    by_coil = samples_by_coil(counts, in_hbm(samples.reshape(CH, P_SIZE, 2 * NCOIL, Z)))

    chunks = range(NCOIL // PER)
    pieces = []
    for chunk in chunks:
        half = coil_forward(chunk, y_forward, sensitivity, image)
        if chunk == 1:
            half, turned, by_coil, y_inverse = lax.optimization_barrier(
                (half, turned, by_coil, y_inverse)
            )
        piece = lax.all_to_all(half, "slab", 0, 0, tiled=True)
        pieces.append(piece)
    position = lax.axis_index("coil").reshape(1)
    base = target_step(position, image, auxiliary, scaled_dual)
    backs = []
    for chunk in chunks:
        back = grid_tile(
            chunk,
            offsets,
            counts,
            in_hbm(pieces[chunk]) if chunk == 0 else pieces[chunk],
            x_forward,
            in_hbm(blocks[0]),
            in_hbm(turned),
            in_hbm(by_coil),
        )
        backs.append(lax.all_to_all(back, "slab", 0, 0, tiled=True))
    *shares, packed = gradient_first(position, y_inverse, in_hbm(backs[0]), sensitivity)
    early = over_planes(shares)
    late = over_planes(gradient_last(position, y_inverse, backs[1], in_hbm(packed)))
    return update_step(base, early + late, scaled_dual)


def solution(mesh):
    return jax.shard_map(
        body,
        mesh=mesh,
        in_specs=(
            P(None, "slab", None, None),
            P("coil", None, "slab", None, None),
            P("slab", None, None, None),
            P("slab", None, None, "coil", None, None),
            P("slab", None),
            P("slab"),
            P(None, "slab", "coil", None),
            P(None, "slab", "coil", None),
        ),
        out_specs=(
            P(None, "slab", "coil", None),
            P(None, "slab", "coil", None),
            P(None, "slab", "coil", None),
        ),
        check_vma=False,
    )
```

```python
import math

import jax
import jax.numpy as jnp
import numpy as np
import ml_dtypes
from jax import lax
from jax.experimental import pallas as pl
from jax.experimental.pallas import tpu as pltpu
from jax.sharding import PartitionSpec as P

N = 256
Z = 128
WIN = 64
P_SIZE = 128
CH = 24
KYD = 8
TILES = 32
CELLS = WIN * KYD
ROWS = N * KYD
NCOIL = 4
PER = 2

step_size = 0.5
penalty = 1.0
threshold = 0.3

BF = jnp.bfloat16
F32 = jnp.float32


def dft_parts():
    index = np.arange(N)
    angle = (index[:, None] * index[None, :] % N).astype(np.float32) * np.float32(2.0 * math.pi / N)
    factor = np.float32(1.0 / math.sqrt(N))
    re = (np.cos(angle) * factor).astype(ml_dtypes.bfloat16)
    im = (-np.sin(angle) * factor).astype(ml_dtypes.bfloat16)
    return re, im


def real_tables():
    re, im = dft_parts()
    along_y = np.stack(
        [np.concatenate([re, -im], 1), np.concatenate([im, re], 1)], 1
    ).reshape(2 * N, 2 * N)
    along_x = np.concatenate([np.concatenate([re, -im], 1), np.concatenate([im, re], 1)], 0)
    return along_y, along_x


def hbm(shape, dtype):
    return pltpu.HBM(shape, dtype)


def in_hbm(x):
    return pltpu.with_memory_space_constraint(x, pltpu.HBM)


VMEM = pl.BlockSpec(memory_space=pltpu.VMEM)
SMEM = pl.BlockSpec(memory_space=pltpu.SMEM)
HBM = pl.BlockSpec(memory_space=pltpu.HBM)
DMA = pltpu.SemaphoreType.DMA


def pack(even, odd, half):
    low = lax.broadcasted_iota(jnp.int32, even.shape, 1) < Z // 2
    if half == 0:
        return jnp.where(low, even, pltpu.roll(odd, Z // 2, 1))
    return jnp.where(low, pltpu.roll(even, Z // 2, 1), odd)


def coil_kernel(half, table_hbm, sens_hbm, image_hbm, out_hbm, table, sens, image, out, sems, leave):
    stages = 2
    span = KYD // stages

    def copies(stage):
        rows = pl.ds(stage * span, span)
        return (
            pltpu.make_async_copy(image_hbm.at[:, rows], image.at[:, rows], sems.at[0, stage]),
            pltpu.make_async_copy(sens_hbm.at[:, :, rows], sens.at[:, :, rows], sems.at[1, stage]),
        )

    def leave_copy(stage):
        rows = pl.ds(stage * span, span)
        return pltpu.make_async_copy(out.at[:, :, rows], out_hbm.at[:, :, rows], leave.at[stage])

    whole = pltpu.make_async_copy(table_hbm, table, sems.at[2, 0])
    whole.start()
    for stage in range(stages):
        for copy in copies(stage):
            copy.start()
    whole.wait()

    def row(x):
        m_re = pack(image[0, x], image[0, x], half)
        m_im = pack(image[1, x], image[1, x], half)
        parts = []
        for pair in range(PER):
            s_re, s_im = (
                pack(*(sens[2 * pair + k, part, x] for k in range(2)), half).astype(F32)
                for part in range(2)
            )
            c_re = (s_re * m_re - s_im * m_im).astype(BF)
            c_im = (s_re * m_im + s_im * m_re).astype(BF)
            parts.append(jnp.concatenate([c_re, c_im], 0))
        data = jnp.concatenate(parts, 1)
        result = jnp.dot(table[...], data, preferred_element_type=F32).astype(BF)
        for pair in range(PER):
            out[:, pair, x] = result[:, pair * Z : (pair + 1) * Z].reshape(TILES, 16, Z)

    for stage in range(stages):
        for copy in copies(stage):
            copy.wait()
        if half == 0:
            for x in range(stage * span, (stage + 1) * span):
                row(x)
        else:

            def rolled(x, carry):
                row(x)
                return carry

            lax.fori_loop(stage * span, (stage + 1) * span, rolled, 0)
        leave_copy(stage).start()
    for stage in range(stages):
        leave_copy(stage).wait()


def coil_forward(half, table, sensitivity, image):
    def kernel(*refs):
        coil_kernel(half, *refs)

    return pl.pallas_call(
        kernel,
        out_shape=hbm((TILES, PER, KYD, 16, Z), BF),
        in_specs=[HBM, HBM, HBM],
        out_specs=HBM,
        scratch_shapes=[
            pltpu.VMEM((2 * N, 2 * N), BF),
            pltpu.VMEM((NCOIL, 2, KYD, N, Z), BF),
            pltpu.VMEM((2, KYD, N, Z), F32),
            pltpu.VMEM((TILES, PER, KYD, 16, Z), BF),
            DMA((3, 2)),
            DMA((2,)),
        ],
        compiler_params=pltpu.CompilerParams(vmem_limit_bytes=16 << 20),
        name=f"coil_forward_{half}",
    )(table, sensitivity, image)


def samples_kernel(counts_ref, samples_hbm, out_hbm, samples, spread, out, arrive, leave):
    count = counts_ref[0]

    def into(j):
        return pltpu.make_async_copy(samples_hbm.at[j], samples.at[j], arrive.at[j])

    def back(j):
        return pltpu.make_async_copy(out.at[:, j], out_hbm.at[:, j], leave.at[j])

    def start(j, carry):
        into(j).start()
        return carry

    def group(j, carry):
        into(j).wait()
        slot = j % 2
        spread[slot] = samples[j].astype(F32).reshape(P_SIZE * 8, Z)
        for pair in range(PER):
            for part in range(2):
                even, odd = (
                    spread[slot, pl.ds(2 * (2 * pair + k) + part, P_SIZE, stride=8), :]
                    for k in range(2)
                )
                for half in range(2):
                    out[half * PER + pair, j, :, part * Z : (part + 1) * Z] = pack(
                        even, odd, half
                    ).astype(BF)
        back(j).start()
        return carry

    def finish(j, carry):
        back(j).wait()
        return carry

    lax.fori_loop(0, count, start, 0)
    lax.fori_loop(0, count, group, 0)
    lax.fori_loop(0, count, finish, 0)


def samples_by_coil(counts, samples):
    return pl.pallas_call(
        samples_kernel,
        out_shape=hbm((NCOIL, CH, P_SIZE, 2 * Z), BF),
        in_specs=[SMEM, HBM],
        out_specs=HBM,
        scratch_shapes=[
            pltpu.VMEM((CH, P_SIZE, 8, Z), BF),
            pltpu.VMEM((2, P_SIZE * 8, Z), F32),
            pltpu.VMEM((NCOIL, CH, P_SIZE, 2 * Z), BF),
            DMA((CH,)),
            DMA((CH,)),
        ],
        compiler_params=pltpu.CompilerParams(vmem_limit_bytes=18 << 20),
        name="samples_by_coil",
    )(counts, samples)


def conjugate(values, part):
    return values if part == 0 else -values


def grid_kernel(
    chunk,
    offsets_ref,
    counts_ref,
    piece_hbm,
    table_ref,
    blocks_hbm,
    turned_hbm,
    samples_hbm,
    out_hbm,
    piece,
    blocks,
    turned,
    samples,
    window,
    total,
    spread,
    out,
    sems,
    leave,
):
    count = counts_ref[0]
    if chunk == 0:
        arrival = pltpu.make_async_copy(piece_hbm, piece, leave.at[PER])
        arrival.start()
    else:
        piece = piece_hbm

    def copies(j):
        return [
            pltpu.make_async_copy(blocks_hbm.at[j], blocks.at[j], sems.at[0, j]),
            pltpu.make_async_copy(turned_hbm.at[j], turned.at[j], sems.at[1, j]),
        ] + [
            pltpu.make_async_copy(
                samples_hbm.at[chunk * PER + c, j],
                samples.at[j, :, pl.ds(2 * Z * c, 2 * Z)],
                sems.at[2 + c, j],
            )
            for c in range(PER)
        ]

    def start(j, carry):
        for copy in copies(j):
            copy.start()
        return carry

    lax.fori_loop(0, count, start, 0)

    if chunk == 0:
        arrival.wait()

    for c in range(PER):
        spread[c] = piece[:, c].astype(F32).reshape(ROWS * 2, Z)

    def forward_row(ky, carry):
        data = jnp.concatenate(
            [
                jnp.concatenate(
                    [
                        spread[c, pl.ds(2 * ky + part, N, stride=2 * KYD), :].astype(BF)
                        for part in range(2)
                    ],
                    0,
                )
                for c in range(PER)
            ],
            1,
        )
        result = jnp.dot(table_ref[...], data, preferred_element_type=F32)
        for c in range(PER):
            for part in range(2):
                total[2 * c + part, pl.ds(ky, N, stride=KYD), :] = result[
                    part * N : (part + 1) * N, c * Z : (c + 1) * Z
                ]
        return carry

    lax.fori_loop(0, KYD, forward_row, 0)
    for s in range(2 * PER):
        lanes = slice(s * Z, (s + 1) * Z)
        total[s, ROWS : ROWS + KYD, :] = jnp.zeros((KYD, Z), F32)
        window[0, :, lanes] = total[s, 0:ROWS, :].astype(BF)
        window[1, :, lanes] = total[s, KYD : ROWS + KYD, :].astype(BF)
    total[...] = jnp.zeros_like(total)

    def arrive(j):
        for copy in copies(j):
            copy.wait()

    def predict(j):
        first = offsets_ref[0, j]
        row = pl.multiple_of((first // 2) * (2 * KYD), 2 * KYD)
        view = window[first % 2, pl.ds(row, CELLS), :]
        predicted = jnp.dot(blocks[j], view, preferred_element_type=F32)
        return (predicted - samples[j].astype(F32)).astype(BF)

    def add_back(j, misfit):
        update = jnp.dot(turned[j], misfit, preferred_element_type=F32)
        spot = pl.ds(pl.multiple_of(offsets_ref[0, j] * KYD, KYD), CELLS)
        for s in range(2 * PER):
            total[s, spot, :] = total[s, spot, :] + update[:, s * Z : (s + 1) * Z]

    arrive(0)
    samples[0] = predict(0)

    def group(j, carry):
        arrive(j)
        before = samples[j - 1]
        misfit = predict(j)
        add_back(j - 1, before)
        samples[j] = misfit
        return carry

    lax.fori_loop(1, count, group, 0)
    add_back(count - 1, samples[count - 1])

    leaving = []
    for c in range(PER):

        def inverse_rows(pair, carry):
            data = jnp.concatenate(
                [
                    jnp.concatenate(
                        [
                            conjugate(
                                total[2 * c + part, pl.ds(2 * pair + i, N, stride=KYD), :], part
                            ).astype(BF)
                            for part in range(2)
                        ],
                        0,
                    )
                    for i in range(2)
                ],
                1,
            )
            result = jnp.dot(table_ref[...], data, preferred_element_type=F32)
            for i in range(2):
                for part in range(2):
                    spread[c, pl.ds(2 * (2 * pair + i) + part, N, stride=2 * KYD), :] = conjugate(
                        result[part * N : (part + 1) * N, i * Z : (i + 1) * Z], part
                    )
            return carry

        lax.fori_loop(0, KYD // 2, inverse_rows, 0)
        out[:, c] = spread[c].astype(BF).reshape(TILES, KYD, 16, Z)
        copy = pltpu.make_async_copy(out.at[:, c], out_hbm.at[:, c], leave.at[c])
        copy.start()
        leaving.append(copy)
    for copy in leaving:
        copy.wait()


def grid_tile(chunk, offsets, counts, piece, table, blocks, turned, samples):
    def kernel(*refs):
        grid_kernel(chunk, *refs)

    return pl.pallas_call(
        kernel,
        out_shape=hbm((TILES, PER, KYD, 16, Z), BF),
        in_specs=[SMEM, SMEM, HBM if chunk == 0 else VMEM, VMEM, HBM, HBM, HBM],
        out_specs=HBM,
        scratch_shapes=[
            pltpu.VMEM((TILES, PER, KYD, 16, Z) if chunk == 0 else (16, Z), BF),
            pltpu.VMEM((CH, P_SIZE, CELLS), BF),
            pltpu.VMEM((CH, CELLS, P_SIZE), BF),
            pltpu.VMEM((CH, P_SIZE, 2 * Z * PER), BF),
            pltpu.VMEM((2, ROWS, 2 * Z * PER), BF),
            pltpu.VMEM((2 * PER, ROWS + KYD, Z), F32),
            pltpu.VMEM((PER, 2 * ROWS, Z), F32),
            pltpu.VMEM((TILES, PER, KYD, 16, Z), BF),
            DMA((2 + PER, CH)),
            DMA((PER + 1,)),
        ],
        compiler_params=pltpu.CompilerParams(vmem_limit_bytes=34 << 20),
        name=f"grid_tile_{chunk}",
    )(offsets, counts, piece, table, blocks, turned, samples)


def combine(adjoint, packed):
    g_re = g_im = None
    for pair in range(PER):
        lanes = slice(pair * Z, (pair + 1) * Z)
        a_re = adjoint[:N, lanes]
        a_im = adjoint[N:, lanes]
        s_re, s_im = packed[pair]
        t_re = s_re * a_re + s_im * a_im
        t_im = s_re * a_im - s_im * a_re
        g_re = t_re if g_re is None else g_re + t_re
        g_im = t_im if g_im is None else g_im + t_im
    low = lax.broadcasted_iota(jnp.int32, g_re.shape, 1) < Z // 2
    return jnp.where(low, g_re + pltpu.roll(g_re, Z // 2, 1), g_im + pltpu.roll(g_im, Z // 2, 1))


def adjoint_row(table_ref, piece, x):
    data = jnp.concatenate([piece[:, pair, x].reshape(2 * N, Z) for pair in range(PER)], 1)
    return jnp.dot(table_ref[...], data, preferred_element_type=F32).astype(BF)


def share_copies(position, out, shares, rows, sems):
    return [
        pltpu.make_async_copy(
            out.at[lax.rem(position + k, NCOIL), rows], shares[k].at[rows], sems.at[k]
        )
        for k in range(NCOIL)
    ]


def gradient_first_kernel(position_ref, table_ref, piece_hbm, sens_hbm, *rest):
    shares = rest[:NCOIL]
    later_hbm, piece, sens, later, out, arrive, sems, last = rest[NCOIL:]
    copies = [
        pltpu.make_async_copy(piece_hbm, piece, arrive.at[0]),
        pltpu.make_async_copy(sens_hbm, sens, arrive.at[1]),
    ]
    for copy in copies:
        copy.start()
    for copy in copies:
        copy.wait()

    def row(x, carry):
        packed = []
        for pair in range(PER):
            both = []
            for part in range(2):
                even, odd = (sens[2 * pair + k, part, x] for k in range(2))
                both.append(pack(even, odd, 0).astype(F32))
                later[pair, part, x] = pack(even, odd, 1)
            packed.append(both)
        gradient = combine(adjoint_row(table_ref, piece, x).astype(F32), packed)
        out[:, x] = gradient.astype(BF).reshape(NCOIL, N // NCOIL, Z)
        return carry

    lax.fori_loop(0, KYD, row, 0)
    leaving = share_copies(position_ref[0], out, shares, pl.ds(0, KYD), sems)
    leaving.append(pltpu.make_async_copy(later, later_hbm, last.at[0]))
    for copy in leaving:
        copy.start()
    for copy in leaving:
        copy.wait()


def gradient_first(position, table, piece, sensitivity):
    share = (KYD, N // NCOIL, Z)
    packed = (PER, 2, KYD, N, Z)
    return pl.pallas_call(
        gradient_first_kernel,
        out_shape=(hbm(share, BF),) * NCOIL + (hbm(packed, BF),),
        in_specs=[SMEM, VMEM, HBM, HBM],
        out_specs=(HBM,) * (NCOIL + 1),
        scratch_shapes=[
            pltpu.VMEM((TILES, PER, KYD, 16, Z), BF),
            pltpu.VMEM((NCOIL, 2, KYD, N, Z), BF),
            pltpu.VMEM(packed, BF),
            pltpu.VMEM((NCOIL,) + share, BF),
            DMA((2,)),
            DMA((NCOIL,)),
            DMA((1,)),
        ],
        compiler_params=pltpu.CompilerParams(vmem_limit_bytes=14 << 20),
        name="gradient_first",
    )(position, table, piece, sensitivity)


def gradient_last_kernel(position_ref, table_ref, piece, sens_hbm, *rest):
    shares = rest[:NCOIL]
    sens, adjoint, out, arrive, sems = rest[NCOIL:]
    span = KYD // 2

    def arrivals(stage):
        rows = pl.ds(stage * span, span)
        return pltpu.make_async_copy(
            sens_hbm.at[:, :, rows], sens.at[:, :, rows], arrive.at[stage]
        )

    for stage in range(2):
        arrivals(stage).start()
    leaving = []
    for stage in range(2):
        for x in range(stage * span, (stage + 1) * span):
            adjoint[x] = adjoint_row(table_ref, piece, x)
        arrivals(stage).wait()
        for x in range(stage * span, (stage + 1) * span):
            packed = [
                [sens[pair, part, x].astype(F32) for part in range(2)] for pair in range(PER)
            ]
            gradient = combine(adjoint[x].astype(F32), packed)
            out[:, x] = gradient.astype(BF).reshape(NCOIL, N // NCOIL, Z)
        rows = pl.ds(stage * span, span)
        for copy in share_copies(position_ref[0], out, shares, rows, sems.at[stage]):
            copy.start()
            leaving.append(copy)
    for copy in leaving:
        copy.wait()


def gradient_last(position, table, piece, packed):
    share = (KYD, N // NCOIL, Z)
    return pl.pallas_call(
        gradient_last_kernel,
        out_shape=(hbm(share, BF),) * NCOIL,
        in_specs=[SMEM, VMEM, VMEM, HBM],
        out_specs=(HBM,) * NCOIL,
        scratch_shapes=[
            pltpu.VMEM((PER, 2, KYD, N, Z), BF),
            pltpu.VMEM((KYD, 2 * N, 2 * Z), BF),
            pltpu.VMEM((NCOIL,) + share, BF),
            DMA((2,)),
            DMA((2, NCOIL)),
        ],
        compiler_params=pltpu.CompilerParams(vmem_limit_bytes=10 << 20),
        name="gradient_last",
    )(position, table, piece, packed)


def haar_rows(top, low):
    add = (top + low) * 0.5
    sub = (top - low) * 0.5
    cols = top.shape[0]
    odd = lax.broadcasted_iota(jnp.int32, top.shape, 0) % 2 == 1

    def pairs(v):
        ahead = pltpu.roll(v, cols - 1, 0)
        behind = pltpu.roll(v, 1, 0)
        return jnp.where(odd, behind - v, v + ahead)

    return pairs(add), pairs(sub)


def target_kernel(position_ref, image_hbm, aux_ref, dual_ref, out_ref, image, sem):
    share = N // NCOIL
    columns = pl.ds(pl.multiple_of(position_ref[0] * share, share), share)
    copy = pltpu.make_async_copy(image_hbm.at[:, :, columns], image, sem)
    copy.start()
    copy.wait()
    for m in range(KYD // 2):
        for part in range(2):
            rows = haar_rows(
                *(aux_ref[part, 2 * m + i] - dual_ref[part, 2 * m + i] for i in range(2))
            )
            for i in range(2):
                current = image[part, 2 * m + i]
                out_ref[part, 2 * m + i] = current - step_size * penalty * (current - rows[i])


def target_step(position, image, auxiliary, scaled_dual):
    return pl.pallas_call(
        target_kernel,
        out_shape=jax.ShapeDtypeStruct(auxiliary.shape, F32),
        in_specs=[SMEM, HBM, VMEM, VMEM],
        out_specs=VMEM,
        scratch_shapes=[pltpu.VMEM(auxiliary.shape, F32), DMA],
        compiler_params=pltpu.CompilerParams(vmem_limit_bytes=6 << 20),
        name="target",
    )(position, image, auxiliary, scaled_dual)


def update_kernel(base_ref, *rest):
    halves = (rest[:NCOIL], rest[NCOIL : 2 * NCOIL])
    dual_ref, image_hbm, aux_hbm, dual_hbm, image, aux, dual, sems = rest[2 * NCOIL :]
    low = lax.broadcasted_iota(jnp.int32, (N // NCOIL, Z), 1) < Z // 2
    leaving = []
    for m in range(KYD // 2):
        rows = ([], [])
        for x in (2 * m, 2 * m + 1):
            sums = []
            for shares in halves:
                total = shares[0][x].astype(F32)
                for share in shares[1:]:
                    total = total + share[x].astype(F32)
                sums.append(total)
            gradient = (
                jnp.where(low, sums[0], pltpu.roll(sums[1], Z // 2, 1)),
                jnp.where(low, pltpu.roll(sums[0], Z // 2, 1), sums[1]),
            )
            for part in range(2):
                value = base_ref[part, x] - step_size * gradient[part]
                image[part, x] = value
                rows[part].append(value)
        coeffs = []
        for part in range(2):
            top, bottom = haar_rows(*rows[part])
            coeffs.append((top + dual_ref[part, 2 * m], bottom + dual_ref[part, 2 * m + 1]))
        for i in range(2):
            c_re = coeffs[0][i]
            c_im = coeffs[1][i]
            magnitude = jnp.sqrt(c_re * c_re + c_im * c_im)
            factor = jnp.maximum(1.0 - threshold / jnp.maximum(magnitude, threshold), 0.0)
            for part, value in enumerate((c_re, c_im)):
                kept = value * factor
                aux[part, 2 * m + i] = kept
                dual[part, 2 * m + i] = value - kept
        pair = pl.ds(2 * m, 2)
        for k, (held, place) in enumerate(((image, image_hbm), (aux, aux_hbm), (dual, dual_hbm))):
            copy = pltpu.make_async_copy(held.at[:, pair], place.at[:, pair], sems.at[k, m])
            copy.start()
            leaving.append(copy)
    for copy in leaving:
        copy.wait()


def update_step(base, shares, scaled_dual):
    shape = hbm(scaled_dual.shape, F32)
    return pl.pallas_call(
        update_kernel,
        out_shape=(shape, shape, shape),
        in_specs=[VMEM] * (2 * NCOIL + 2),
        out_specs=(HBM, HBM, HBM),
        scratch_shapes=[pltpu.VMEM(scaled_dual.shape, F32)] * 3 + [DMA((3, KYD // 2))],
        compiler_params=pltpu.CompilerParams(vmem_limit_bytes=8 << 20),
        name="update",
    )(base, *shares, scaled_dual)


def over_planes(shares):
    own, *others = shares
    got = [own]
    for k in (2, 1, 3):
        ring = [(i, (i + k) % NCOIL) for i in range(NCOIL)]
        got.append(lax.ppermute(others[k - 1], "coil", ring))
    return got


def body(image, sensitivity, blocks, samples, offsets, counts, auxiliary, scaled_dual):
    along_y, along_x = real_tables()
    y_forward, x_forward = jnp.asarray(along_y), jnp.asarray(along_x)
    y_inverse = lax.optimization_barrier(y_forward).T

    image, sensitivity = in_hbm(image), in_hbm(sensitivity)
    y_forward = in_hbm(y_forward)
    turned = jnp.swapaxes(blocks[0], 1, 2)
    by_coil = samples_by_coil(counts, in_hbm(samples.reshape(CH, P_SIZE, 2 * NCOIL, Z)))

    chunks = range(NCOIL // PER)
    pieces = []
    for chunk in chunks:
        half = coil_forward(chunk, y_forward, sensitivity, image)
        if chunk == 1:
            half, turned, by_coil, y_inverse, pieces[0] = lax.optimization_barrier(
                (half, turned, by_coil, y_inverse, pieces[0])
            )
        piece = lax.all_to_all(half, "slab", 0, 0, tiled=True)
        pieces.append(piece)
    position = lax.axis_index("coil").reshape(1)
    base = target_step(position, image, auxiliary, scaled_dual)
    backs = []
    for chunk in chunks:
        back = grid_tile(
            chunk,
            offsets,
            counts,
            in_hbm(pieces[chunk]) if chunk == 0 else pieces[chunk],
            x_forward,
            in_hbm(blocks[0]),
            in_hbm(turned),
            in_hbm(by_coil),
        )
        backs.append(lax.all_to_all(back, "slab", 0, 0, tiled=True))
    *shares, packed = gradient_first(position, y_inverse, in_hbm(backs[0]), sensitivity)
    early = over_planes(shares)
    late = over_planes(gradient_last(position, y_inverse, backs[1], in_hbm(packed)))
    return update_step(base, early + late, scaled_dual)


def solution(mesh):
    return jax.shard_map(
        body,
        mesh=mesh,
        in_specs=(
            P(None, "slab", None, None),
            P("coil", None, "slab", None, None),
            P("slab", None, None, None),
            P("slab", None, None, "coil", None, None),
            P("slab", None),
            P("slab"),
            P(None, "slab", "coil", None),
            P(None, "slab", "coil", None),
        ),
        out_specs=(
            P(None, "slab", "coil", None),
            P(None, "slab", "coil", None),
            P(None, "slab", "coil", None),
        ),
        check_vma=False,
    )
```

```python
import math

import jax
import jax.numpy as jnp
import numpy as np
import ml_dtypes
from jax import lax
from jax.experimental import pallas as pl
from jax.experimental.pallas import tpu as pltpu
from jax.sharding import PartitionSpec as P

N = 256
Z = 128
WIN = 64
P_SIZE = 128
CH = 24
KYD = 8
TILES = 32
CELLS = WIN * KYD
ROWS = N * KYD
NCOIL = 4
PER = 2

step_size = 0.5
penalty = 1.0
threshold = 0.3

BF = jnp.bfloat16
F32 = jnp.float32


def dft_parts():
    index = np.arange(N)
    angle = (index[:, None] * index[None, :] % N).astype(np.float32) * np.float32(2.0 * math.pi / N)
    factor = np.float32(1.0 / math.sqrt(N))
    re = (np.cos(angle) * factor).astype(ml_dtypes.bfloat16)
    im = (-np.sin(angle) * factor).astype(ml_dtypes.bfloat16)
    return re, im


def real_tables():
    re, im = dft_parts()
    along_y = np.stack(
        [np.concatenate([re, -im], 1), np.concatenate([im, re], 1)], 1
    ).reshape(2 * N, 2 * N)
    along_x = np.concatenate([np.concatenate([re, -im], 1), np.concatenate([im, re], 1)], 0)
    return along_y, along_x


def hbm(shape, dtype):
    return pltpu.HBM(shape, dtype)


def in_hbm(x):
    return pltpu.with_memory_space_constraint(x, pltpu.HBM)


VMEM = pl.BlockSpec(memory_space=pltpu.VMEM)
SMEM = pl.BlockSpec(memory_space=pltpu.SMEM)
HBM = pl.BlockSpec(memory_space=pltpu.HBM)
DMA = pltpu.SemaphoreType.DMA


def pack(even, odd, half):
    low = lax.broadcasted_iota(jnp.int32, even.shape, 1) < Z // 2
    if half == 0:
        return jnp.where(low, even, pltpu.roll(odd, Z // 2, 1))
    return jnp.where(low, pltpu.roll(even, Z // 2, 1), odd)


def coil_kernel(half, table_hbm, sens_hbm, image_hbm, out_hbm, table, sens, image, out, sems, leave):
    stages = 2
    span = KYD // stages

    def copies(stage):
        rows = pl.ds(stage * span, span)
        return (
            pltpu.make_async_copy(image_hbm.at[:, rows], image.at[:, rows], sems.at[0, stage]),
            pltpu.make_async_copy(sens_hbm.at[:, :, rows], sens.at[:, :, rows], sems.at[1, stage]),
        )

    def leave_copy(stage):
        rows = pl.ds(stage * span, span)
        return pltpu.make_async_copy(out.at[:, :, rows], out_hbm.at[:, :, rows], leave.at[stage])

    whole = pltpu.make_async_copy(table_hbm, table, sems.at[2, 0])
    whole.start()
    for stage in range(stages):
        for copy in copies(stage):
            copy.start()
    whole.wait()

    def row(x):
        m_re = pack(image[0, x], image[0, x], half)
        m_im = pack(image[1, x], image[1, x], half)
        parts = []
        for pair in range(PER):
            s_re, s_im = (
                pack(*(sens[2 * pair + k, part, x] for k in range(2)), half).astype(F32)
                for part in range(2)
            )
            c_re = (s_re * m_re - s_im * m_im).astype(BF)
            c_im = (s_re * m_im + s_im * m_re).astype(BF)
            parts.append(jnp.concatenate([c_re, c_im], 0))
        data = jnp.concatenate(parts, 1)
        result = jnp.dot(table[...], data, preferred_element_type=F32).astype(BF)
        for pair in range(PER):
            out[:, pair, x] = result[:, pair * Z : (pair + 1) * Z].reshape(TILES, 16, Z)

    for stage in range(stages):
        for copy in copies(stage):
            copy.wait()
        if half == 0:
            for x in range(stage * span, (stage + 1) * span):
                row(x)
        else:

            def rolled(x, carry):
                row(x)
                return carry

            lax.fori_loop(stage * span, (stage + 1) * span, rolled, 0)
        leave_copy(stage).start()
    for stage in range(stages):
        leave_copy(stage).wait()


def coil_forward(half, table, sensitivity, image):
    def kernel(*refs):
        coil_kernel(half, *refs)

    return pl.pallas_call(
        kernel,
        out_shape=hbm((TILES, PER, KYD, 16, Z), BF),
        in_specs=[HBM, HBM, HBM],
        out_specs=HBM,
        scratch_shapes=[
            pltpu.VMEM((2 * N, 2 * N), BF),
            pltpu.VMEM((NCOIL, 2, KYD, N, Z), BF),
            pltpu.VMEM((2, KYD, N, Z), F32),
            pltpu.VMEM((TILES, PER, KYD, 16, Z), BF),
            DMA((3, 2)),
            DMA((2,)),
        ],
        compiler_params=pltpu.CompilerParams(vmem_limit_bytes=16 << 20),
        name=f"coil_forward_{half}",
    )(table, sensitivity, image)


def samples_kernel(counts_ref, samples_hbm, out_hbm, samples, spread, out, arrive, leave):
    count = counts_ref[0]

    def into(j):
        return pltpu.make_async_copy(samples_hbm.at[j], samples.at[j], arrive.at[j])

    def back(j):
        return pltpu.make_async_copy(out.at[:, j], out_hbm.at[:, j], leave.at[j])

    def start(j, carry):
        into(j).start()
        return carry

    def group(j, carry):
        into(j).wait()
        slot = j % 2
        spread[slot] = samples[j].astype(F32).reshape(P_SIZE * 8, Z)
        for pair in range(PER):
            for part in range(2):
                even, odd = (
                    spread[slot, pl.ds(2 * (2 * pair + k) + part, P_SIZE, stride=8), :]
                    for k in range(2)
                )
                for half in range(2):
                    out[half * PER + pair, j, :, part * Z : (part + 1) * Z] = pack(
                        even, odd, half
                    ).astype(BF)
        back(j).start()
        return carry

    def finish(j, carry):
        back(j).wait()
        return carry

    lax.fori_loop(0, count, start, 0)
    lax.fori_loop(0, count, group, 0)
    lax.fori_loop(0, count, finish, 0)


def samples_by_coil(counts, samples):
    return pl.pallas_call(
        samples_kernel,
        out_shape=hbm((NCOIL, CH, P_SIZE, 2 * Z), BF),
        in_specs=[SMEM, HBM],
        out_specs=HBM,
        scratch_shapes=[
            pltpu.VMEM((CH, P_SIZE, 8, Z), BF),
            pltpu.VMEM((2, P_SIZE * 8, Z), F32),
            pltpu.VMEM((NCOIL, CH, P_SIZE, 2 * Z), BF),
            DMA((CH,)),
            DMA((CH,)),
        ],
        compiler_params=pltpu.CompilerParams(vmem_limit_bytes=18 << 20),
        name="samples_by_coil",
    )(counts, samples)


def conjugate(values, part):
    return values if part == 0 else -values


def grid_kernel(
    chunk,
    offsets_ref,
    counts_ref,
    piece_hbm,
    table_ref,
    blocks_hbm,
    turned_hbm,
    samples_hbm,
    out_hbm,
    piece,
    blocks,
    turned,
    samples,
    window,
    total,
    spread,
    out,
    sems,
    leave,
):
    count = counts_ref[0]
    if chunk == 0:
        arrival = pltpu.make_async_copy(piece_hbm, piece, leave.at[PER])
        arrival.start()
    else:
        piece = piece_hbm

    def copies(j):
        return [
            pltpu.make_async_copy(blocks_hbm.at[j], blocks.at[j], sems.at[0, j]),
            pltpu.make_async_copy(turned_hbm.at[j], turned.at[j], sems.at[1, j]),
        ] + [
            pltpu.make_async_copy(
                samples_hbm.at[chunk * PER + c, j],
                samples.at[j, :, pl.ds(2 * Z * c, 2 * Z)],
                sems.at[2 + c, j],
            )
            for c in range(PER)
        ]

    def start(j, carry):
        for copy in copies(j):
            copy.start()
        return carry

    lax.fori_loop(0, count, start, 0)

    if chunk == 0:
        arrival.wait()

    for c in range(PER):
        spread[c] = piece[:, c].astype(F32).reshape(ROWS * 2, Z)

    def forward_row(ky, carry):
        data = jnp.concatenate(
            [
                jnp.concatenate(
                    [
                        spread[c, pl.ds(2 * ky + part, N, stride=2 * KYD), :].astype(BF)
                        for part in range(2)
                    ],
                    0,
                )
                for c in range(PER)
            ],
            1,
        )
        result = jnp.dot(table_ref[...], data, preferred_element_type=F32)
        for c in range(PER):
            for part in range(2):
                total[2 * c + part, pl.ds(ky, N, stride=KYD), :] = result[
                    part * N : (part + 1) * N, c * Z : (c + 1) * Z
                ]
        return carry

    lax.fori_loop(0, KYD, forward_row, 0)
    for s in range(2 * PER):
        lanes = slice(s * Z, (s + 1) * Z)
        total[s, ROWS : ROWS + KYD, :] = jnp.zeros((KYD, Z), F32)
        window[0, :, lanes] = total[s, 0:ROWS, :].astype(BF)
        window[1, :, lanes] = total[s, KYD : ROWS + KYD, :].astype(BF)
    total[...] = jnp.zeros_like(total)

    def arrive(j):
        for copy in copies(j):
            copy.wait()

    def predict(j):
        first = offsets_ref[0, j]
        row = pl.multiple_of((first // 2) * (2 * KYD), 2 * KYD)
        view = window[first % 2, pl.ds(row, CELLS), :]
        predicted = jnp.dot(blocks[j], view, preferred_element_type=F32)
        return (predicted - samples[j].astype(F32)).astype(BF)

    def add_back(j, misfit):
        update = jnp.dot(turned[j], misfit, preferred_element_type=F32)
        spot = pl.ds(pl.multiple_of(offsets_ref[0, j] * KYD, KYD), CELLS)
        for s in range(2 * PER):
            total[s, spot, :] = total[s, spot, :] + update[:, s * Z : (s + 1) * Z]

    arrive(0)
    samples[0] = predict(0)

    def group(j, carry):
        arrive(j)
        before = samples[j - 1]
        misfit = predict(j)
        add_back(j - 1, before)
        samples[j] = misfit
        return carry

    lax.fori_loop(1, count, group, 0)
    add_back(count - 1, samples[count - 1])

    leaving = []
    for c in range(PER):

        def inverse_rows(pair, carry):
            data = jnp.concatenate(
                [
                    jnp.concatenate(
                        [
                            conjugate(
                                total[2 * c + part, pl.ds(2 * pair + i, N, stride=KYD), :], part
                            ).astype(BF)
                            for part in range(2)
                        ],
                        0,
                    )
                    for i in range(2)
                ],
                1,
            )
            result = jnp.dot(table_ref[...], data, preferred_element_type=F32)
            for i in range(2):
                for part in range(2):
                    spread[c, pl.ds(2 * (2 * pair + i) + part, N, stride=2 * KYD), :] = conjugate(
                        result[part * N : (part + 1) * N, i * Z : (i + 1) * Z], part
                    )
            return carry

        lax.fori_loop(0, KYD // 2, inverse_rows, 0)
        out[:, c] = spread[c].astype(BF).reshape(TILES, KYD, 16, Z)
        copy = pltpu.make_async_copy(out.at[:, c], out_hbm.at[:, c], leave.at[c])
        copy.start()
        leaving.append(copy)
    for copy in leaving:
        copy.wait()


def grid_tile(chunk, offsets, counts, piece, table, blocks, turned, samples):
    def kernel(*refs):
        grid_kernel(chunk, *refs)

    return pl.pallas_call(
        kernel,
        out_shape=hbm((TILES, PER, KYD, 16, Z), BF),
        in_specs=[SMEM, SMEM, HBM if chunk == 0 else VMEM, VMEM, HBM, HBM, HBM],
        out_specs=HBM,
        scratch_shapes=[
            pltpu.VMEM((TILES, PER, KYD, 16, Z) if chunk == 0 else (16, Z), BF),
            pltpu.VMEM((CH, P_SIZE, CELLS), BF),
            pltpu.VMEM((CH, CELLS, P_SIZE), BF),
            pltpu.VMEM((CH, P_SIZE, 2 * Z * PER), BF),
            pltpu.VMEM((2, ROWS, 2 * Z * PER), BF),
            pltpu.VMEM((2 * PER, ROWS + KYD, Z), F32),
            pltpu.VMEM((PER, 2 * ROWS, Z), F32),
            pltpu.VMEM((TILES, PER, KYD, 16, Z), BF),
            DMA((2 + PER, CH)),
            DMA((PER + 1,)),
        ],
        compiler_params=pltpu.CompilerParams(vmem_limit_bytes=34 << 20),
        name=f"grid_tile_{chunk}",
    )(offsets, counts, piece, table, blocks, turned, samples)


def combine(adjoint, packed):
    g_re = g_im = None
    for pair in range(PER):
        lanes = slice(pair * Z, (pair + 1) * Z)
        a_re = adjoint[:N, lanes]
        a_im = adjoint[N:, lanes]
        s_re, s_im = packed[pair]
        t_re = s_re * a_re + s_im * a_im
        t_im = s_re * a_im - s_im * a_re
        g_re = t_re if g_re is None else g_re + t_re
        g_im = t_im if g_im is None else g_im + t_im
    low = lax.broadcasted_iota(jnp.int32, g_re.shape, 1) < Z // 2
    return jnp.where(low, g_re + pltpu.roll(g_re, Z // 2, 1), g_im + pltpu.roll(g_im, Z // 2, 1))


def adjoint_row(table_ref, piece, x):
    data = jnp.concatenate([piece[:, pair, x].reshape(2 * N, Z) for pair in range(PER)], 1)
    return jnp.dot(table_ref[...], data, preferred_element_type=F32).astype(BF)


def share_copies(position, out, shares, rows, sems):
    return [
        pltpu.make_async_copy(
            out.at[lax.rem(position + k, NCOIL), rows], shares[k].at[rows], sems.at[k]
        )
        for k in range(NCOIL)
    ]


def gradient_first_kernel(position_ref, table_ref, piece_hbm, sens_hbm, *rest):
    shares = rest[:NCOIL]
    later_hbm, piece, sens, later, out, arrive, sems, last = rest[NCOIL:]
    copies = [
        pltpu.make_async_copy(piece_hbm, piece, arrive.at[0]),
        pltpu.make_async_copy(sens_hbm, sens, arrive.at[1]),
    ]
    for copy in copies:
        copy.start()
    for copy in copies:
        copy.wait()

    def row(x, carry):
        packed = []
        for pair in range(PER):
            both = []
            for part in range(2):
                even, odd = (sens[2 * pair + k, part, x] for k in range(2))
                both.append(pack(even, odd, 0).astype(F32))
                later[pair, part, x] = pack(even, odd, 1)
            packed.append(both)
        gradient = combine(adjoint_row(table_ref, piece, x).astype(F32), packed)
        out[:, x] = gradient.astype(BF).reshape(NCOIL, N // NCOIL, Z)
        return carry

    lax.fori_loop(0, KYD, row, 0)
    leaving = share_copies(position_ref[0], out, shares, pl.ds(0, KYD), sems)
    leaving.append(pltpu.make_async_copy(later, later_hbm, last.at[0]))
    for copy in leaving:
        copy.start()
    for copy in leaving:
        copy.wait()


def gradient_first(position, table, piece, sensitivity):
    share = (KYD, N // NCOIL, Z)
    packed = (PER, 2, KYD, N, Z)
    return pl.pallas_call(
        gradient_first_kernel,
        out_shape=(hbm(share, BF),) * NCOIL + (hbm(packed, BF),),
        in_specs=[SMEM, VMEM, HBM, HBM],
        out_specs=(HBM,) * (NCOIL + 1),
        scratch_shapes=[
            pltpu.VMEM((TILES, PER, KYD, 16, Z), BF),
            pltpu.VMEM((NCOIL, 2, KYD, N, Z), BF),
            pltpu.VMEM(packed, BF),
            pltpu.VMEM((NCOIL,) + share, BF),
            DMA((2,)),
            DMA((NCOIL,)),
            DMA((1,)),
        ],
        compiler_params=pltpu.CompilerParams(vmem_limit_bytes=14 << 20),
        name="gradient_first",
    )(position, table, piece, sensitivity)


def gradient_last_kernel(position_ref, table_ref, piece, sens_hbm, *rest):
    shares = rest[:NCOIL]
    sens, adjoint, out, arrive, sems = rest[NCOIL:]
    span = KYD // 2

    def arrivals(stage):
        rows = pl.ds(stage * span, span)
        return pltpu.make_async_copy(
            sens_hbm.at[:, :, rows], sens.at[:, :, rows], arrive.at[stage]
        )

    for stage in range(2):
        arrivals(stage).start()
    leaving = []
    for stage in range(2):
        for x in range(stage * span, (stage + 1) * span):
            adjoint[x] = adjoint_row(table_ref, piece, x)
        arrivals(stage).wait()
        for x in range(stage * span, (stage + 1) * span):
            packed = [
                [sens[pair, part, x].astype(F32) for part in range(2)] for pair in range(PER)
            ]
            gradient = combine(adjoint[x].astype(F32), packed)
            out[:, x] = gradient.astype(BF).reshape(NCOIL, N // NCOIL, Z)
        rows = pl.ds(stage * span, span)
        for copy in share_copies(position_ref[0], out, shares, rows, sems.at[stage]):
            copy.start()
            leaving.append(copy)
    for copy in leaving:
        copy.wait()


def gradient_last(position, table, piece, packed):
    share = (KYD, N // NCOIL, Z)
    return pl.pallas_call(
        gradient_last_kernel,
        out_shape=(hbm(share, BF),) * NCOIL,
        in_specs=[SMEM, VMEM, VMEM, HBM],
        out_specs=(HBM,) * NCOIL,
        scratch_shapes=[
            pltpu.VMEM((PER, 2, KYD, N, Z), BF),
            pltpu.VMEM((KYD, 2 * N, 2 * Z), BF),
            pltpu.VMEM((NCOIL,) + share, BF),
            DMA((2,)),
            DMA((2, NCOIL)),
        ],
        compiler_params=pltpu.CompilerParams(vmem_limit_bytes=10 << 20),
        name="gradient_last",
    )(position, table, piece, packed)


def haar_rows(top, low):
    add = (top + low) * 0.5
    sub = (top - low) * 0.5
    cols = top.shape[0]
    odd = lax.broadcasted_iota(jnp.int32, top.shape, 0) % 2 == 1

    def pairs(v):
        ahead = pltpu.roll(v, cols - 1, 0)
        behind = pltpu.roll(v, 1, 0)
        return jnp.where(odd, behind - v, v + ahead)

    return pairs(add), pairs(sub)


def spread_halves(first, second):
    low = lax.broadcasted_iota(jnp.int32, first.shape, 1) < Z // 2
    return (
        jnp.where(low, first, pltpu.roll(second, Z // 2, 1)),
        jnp.where(low, pltpu.roll(first, Z // 2, 1), second),
    )


def target_kernel(position_ref, image_hbm, aux_ref, dual_ref, *rest):
    early = rest[:NCOIL]
    own_ref, out_ref, image, sem = rest[NCOIL:]
    share = N // NCOIL
    columns = pl.ds(pl.multiple_of(position_ref[0] * share, share), share)
    copy = pltpu.make_async_copy(image_hbm.at[:, :, columns], image, sem)
    copy.start()
    copy.wait()
    for m in range(KYD // 2):
        known = []
        for x in (2 * m, 2 * m + 1):
            total = early[0][x].astype(F32)
            for other in early[1:]:
                total = total + other[x].astype(F32)
            known.append(spread_halves(total, own_ref[x].astype(F32)))
        for part in range(2):
            rows = haar_rows(
                *(aux_ref[part, 2 * m + i] - dual_ref[part, 2 * m + i] for i in range(2))
            )
            for i in range(2):
                current = image[part, 2 * m + i]
                out_ref[part, 2 * m + i] = current - step_size * (
                    known[i][part] + penalty * (current - rows[i])
                )


def target_step(position, image, auxiliary, scaled_dual, early, own):
    return pl.pallas_call(
        target_kernel,
        out_shape=jax.ShapeDtypeStruct(auxiliary.shape, F32),
        in_specs=[SMEM, HBM] + [VMEM] * (NCOIL + 3),
        out_specs=VMEM,
        scratch_shapes=[pltpu.VMEM(auxiliary.shape, F32), DMA],
        compiler_params=pltpu.CompilerParams(vmem_limit_bytes=7 << 20),
        name="target",
    )(position, image, auxiliary, scaled_dual, *early, own)


def update_kernel(base_ref, *rest):
    late = rest[: NCOIL - 1]
    dual_ref, image_hbm, aux_hbm, dual_hbm, image, aux, dual, sems = rest[NCOIL - 1 :]
    low = lax.broadcasted_iota(jnp.int32, (N // NCOIL, Z), 1) < Z // 2
    leaving = []
    for m in range(KYD // 2):
        rows = ([], [])
        for x in (2 * m, 2 * m + 1):
            total = late[0][x].astype(F32)
            for other in late[1:]:
                total = total + other[x].astype(F32)
            zero = jnp.zeros_like(total)
            gradient = (
                jnp.where(low, zero, pltpu.roll(total, Z // 2, 1)),
                jnp.where(low, zero, total),
            )
            for part in range(2):
                value = base_ref[part, x] - step_size * gradient[part]
                image[part, x] = value
                rows[part].append(value)
        coeffs = []
        for part in range(2):
            top, bottom = haar_rows(*rows[part])
            coeffs.append((top + dual_ref[part, 2 * m], bottom + dual_ref[part, 2 * m + 1]))
        for i in range(2):
            c_re = coeffs[0][i]
            c_im = coeffs[1][i]
            magnitude = jnp.sqrt(c_re * c_re + c_im * c_im)
            factor = jnp.maximum(1.0 - threshold / jnp.maximum(magnitude, threshold), 0.0)
            for part, value in enumerate((c_re, c_im)):
                kept = value * factor
                aux[part, 2 * m + i] = kept
                dual[part, 2 * m + i] = value - kept
        pair = pl.ds(2 * m, 2)
        for k, (held, place) in enumerate(((image, image_hbm), (aux, aux_hbm), (dual, dual_hbm))):
            copy = pltpu.make_async_copy(held.at[:, pair], place.at[:, pair], sems.at[k, m])
            copy.start()
            leaving.append(copy)
    for copy in leaving:
        copy.wait()


def update_step(base, late, scaled_dual):
    shape = hbm(scaled_dual.shape, F32)
    return pl.pallas_call(
        update_kernel,
        out_shape=(shape, shape, shape),
        in_specs=[VMEM] * (NCOIL + 1),
        out_specs=(HBM, HBM, HBM),
        scratch_shapes=[pltpu.VMEM(scaled_dual.shape, F32)] * 3 + [DMA((3, KYD // 2))],
        compiler_params=pltpu.CompilerParams(vmem_limit_bytes=8 << 20),
        name="update",
    )(base, *late, scaled_dual)


def over_planes(shares):
    own, *others = shares
    got = [own]
    for k in (2, 1, 3):
        ring = [(i, (i + k) % NCOIL) for i in range(NCOIL)]
        got.append(lax.ppermute(others[k - 1], "coil", ring))
    return got


def body(image, sensitivity, blocks, samples, offsets, counts, auxiliary, scaled_dual):
    along_y, along_x = real_tables()
    y_forward, x_forward = jnp.asarray(along_y), jnp.asarray(along_x)
    y_inverse = lax.optimization_barrier(y_forward).T

    image, sensitivity = in_hbm(image), in_hbm(sensitivity)
    y_forward = in_hbm(y_forward)
    turned = jnp.swapaxes(blocks[0], 1, 2)
    by_coil = samples_by_coil(counts, in_hbm(samples.reshape(CH, P_SIZE, 2 * NCOIL, Z)))

    chunks = range(NCOIL // PER)
    pieces = []
    for chunk in chunks:
        half = coil_forward(chunk, y_forward, sensitivity, image)
        if chunk == 1:
            half, turned, by_coil, y_inverse, pieces[0] = lax.optimization_barrier(
                (half, turned, by_coil, y_inverse, pieces[0])
            )
        piece = lax.all_to_all(half, "slab", 0, 0, tiled=True)
        pieces.append(piece)
    position = lax.axis_index("coil").reshape(1)
    backs = []
    for chunk in chunks:
        back = grid_tile(
            chunk,
            offsets,
            counts,
            in_hbm(pieces[chunk]) if chunk == 0 else pieces[chunk],
            x_forward,
            in_hbm(blocks[0]),
            in_hbm(turned),
            in_hbm(by_coil),
        )
        backs.append(lax.all_to_all(back, "slab", 0, 0, tiled=True))
    *shares, packed = gradient_first(position, y_inverse, in_hbm(backs[0]), sensitivity)
    early = over_planes(shares)
    late = over_planes(gradient_last(position, y_inverse, backs[1], in_hbm(packed)))
    base = target_step(position, image, auxiliary, scaled_dual, early, late[0])
    return update_step(base, late[1:], scaled_dual)


def solution(mesh):
    return jax.shard_map(
        body,
        mesh=mesh,
        in_specs=(
            P(None, "slab", None, None),
            P("coil", None, "slab", None, None),
            P("slab", None, None, None),
            P("slab", None, None, "coil", None, None),
            P("slab", None),
            P("slab"),
            P(None, "slab", "coil", None),
            P(None, "slab", "coil", None),
        ),
        out_specs=(
            P(None, "slab", "coil", None),
            P(None, "slab", "coil", None),
            P(None, "slab", "coil", None),
        ),
        check_vma=False,
    )
```

```python
import math

import jax
import jax.numpy as jnp
import numpy as np
import ml_dtypes
from jax import lax
from jax.experimental import pallas as pl
from jax.experimental.pallas import tpu as pltpu
from jax.sharding import PartitionSpec as P

N = 256
Z = 128
WIN = 64
P_SIZE = 128
CH = 24
KYD = 8
TILES = 32
CELLS = WIN * KYD
ROWS = N * KYD
NCOIL = 4
PER = 2

step_size = 0.5
penalty = 1.0
threshold = 0.3

BF = jnp.bfloat16
F32 = jnp.float32


def dft_parts():
    index = np.arange(N)
    angle = (index[:, None] * index[None, :] % N).astype(np.float32) * np.float32(2.0 * math.pi / N)
    factor = np.float32(1.0 / math.sqrt(N))
    re = (np.cos(angle) * factor).astype(ml_dtypes.bfloat16)
    im = (-np.sin(angle) * factor).astype(ml_dtypes.bfloat16)
    return re, im


def real_tables():
    re, im = dft_parts()
    along_y = np.stack(
        [np.concatenate([re, -im], 1), np.concatenate([im, re], 1)], 1
    ).reshape(2 * N, 2 * N)
    along_x = np.concatenate([np.concatenate([re, -im], 1), np.concatenate([im, re], 1)], 0)
    return along_y, along_x


def hbm(shape, dtype):
    return pltpu.HBM(shape, dtype)


def in_hbm(x):
    return pltpu.with_memory_space_constraint(x, pltpu.HBM)


VMEM = pl.BlockSpec(memory_space=pltpu.VMEM)
SMEM = pl.BlockSpec(memory_space=pltpu.SMEM)
HBM = pl.BlockSpec(memory_space=pltpu.HBM)
DMA = pltpu.SemaphoreType.DMA


def pack(even, odd, half):
    low = lax.broadcasted_iota(jnp.int32, even.shape, 1) < Z // 2
    if half == 0:
        return jnp.where(low, even, pltpu.roll(odd, Z // 2, 1))
    return jnp.where(low, pltpu.roll(even, Z // 2, 1), odd)


def coil_kernel(half, table_hbm, sens_hbm, image_hbm, out_hbm, table, sens, image, out, sems, leave):
    stages = 2
    span = KYD // stages

    def copies(stage):
        rows = pl.ds(stage * span, span)
        return (
            pltpu.make_async_copy(image_hbm.at[:, rows], image.at[:, rows], sems.at[0, stage]),
            pltpu.make_async_copy(sens_hbm.at[:, :, rows], sens.at[:, :, rows], sems.at[1, stage]),
        )

    def leave_copy(stage):
        rows = pl.ds(stage * span, span)
        return pltpu.make_async_copy(out.at[:, :, rows], out_hbm.at[:, :, rows], leave.at[stage])

    whole = pltpu.make_async_copy(table_hbm, table, sems.at[2, 0])
    whole.start()
    for stage in range(stages):
        for copy in copies(stage):
            copy.start()
    whole.wait()

    def row(x):
        m_re = pack(image[0, x], image[0, x], half)
        m_im = pack(image[1, x], image[1, x], half)
        parts = []
        for pair in range(PER):
            s_re, s_im = (
                pack(*(sens[2 * pair + k, part, x] for k in range(2)), half).astype(F32)
                for part in range(2)
            )
            c_re = (s_re * m_re - s_im * m_im).astype(BF)
            c_im = (s_re * m_im + s_im * m_re).astype(BF)
            parts.append(jnp.concatenate([c_re, c_im], 0))
        data = jnp.concatenate(parts, 1)
        result = jnp.dot(table[...], data, preferred_element_type=F32).astype(BF)
        for pair in range(PER):
            out[:, pair, x] = result[:, pair * Z : (pair + 1) * Z].reshape(TILES, 16, Z)

    for stage in range(stages):
        for copy in copies(stage):
            copy.wait()
        if half == 0:
            for x in range(stage * span, (stage + 1) * span):
                row(x)
        else:

            def rolled(x, carry):
                row(x)
                return carry

            lax.fori_loop(stage * span, (stage + 1) * span, rolled, 0)
        leave_copy(stage).start()
    for stage in range(stages):
        leave_copy(stage).wait()


def coil_forward(half, table, sensitivity, image):
    def kernel(*refs):
        coil_kernel(half, *refs)

    return pl.pallas_call(
        kernel,
        out_shape=hbm((TILES, PER, KYD, 16, Z), BF),
        in_specs=[HBM, HBM, HBM],
        out_specs=HBM,
        scratch_shapes=[
            pltpu.VMEM((2 * N, 2 * N), BF),
            pltpu.VMEM((NCOIL, 2, KYD, N, Z), BF),
            pltpu.VMEM((2, KYD, N, Z), F32),
            pltpu.VMEM((TILES, PER, KYD, 16, Z), BF),
            DMA((3, 2)),
            DMA((2,)),
        ],
        compiler_params=pltpu.CompilerParams(vmem_limit_bytes=16 << 20),
        name=f"coil_forward_{half}",
    )(table, sensitivity, image)


def samples_kernel(counts_ref, samples_hbm, out_hbm, samples, spread, out, arrive, leave):
    count = counts_ref[0]

    def into(j):
        return pltpu.make_async_copy(samples_hbm.at[j], samples.at[j], arrive.at[j])

    def back(j):
        return pltpu.make_async_copy(out.at[:, j], out_hbm.at[:, j], leave.at[j])

    def start(j, carry):
        into(j).start()
        return carry

    def group(j, carry):
        into(j).wait()
        slot = j % 2
        spread[slot] = samples[j].astype(F32).reshape(P_SIZE * 8, Z)
        for pair in range(PER):
            for part in range(2):
                even, odd = (
                    spread[slot, pl.ds(2 * (2 * pair + k) + part, P_SIZE, stride=8), :]
                    for k in range(2)
                )
                for half in range(2):
                    out[half * PER + pair, j, :, part * Z : (part + 1) * Z] = pack(
                        even, odd, half
                    ).astype(BF)
        back(j).start()
        return carry

    def finish(j, carry):
        back(j).wait()
        return carry

    lax.fori_loop(0, count, start, 0)
    lax.fori_loop(0, count, group, 0)
    lax.fori_loop(0, count, finish, 0)


def samples_by_coil(counts, samples):
    return pl.pallas_call(
        samples_kernel,
        out_shape=hbm((NCOIL, CH, P_SIZE, 2 * Z), BF),
        in_specs=[SMEM, HBM],
        out_specs=HBM,
        scratch_shapes=[
            pltpu.VMEM((CH, P_SIZE, 8, Z), BF),
            pltpu.VMEM((2, P_SIZE * 8, Z), F32),
            pltpu.VMEM((NCOIL, CH, P_SIZE, 2 * Z), BF),
            DMA((CH,)),
            DMA((CH,)),
        ],
        compiler_params=pltpu.CompilerParams(vmem_limit_bytes=18 << 20),
        name="samples_by_coil",
    )(counts, samples)


def conjugate(values, part):
    return values if part == 0 else -values


def grid_kernel(
    chunk,
    offsets_ref,
    counts_ref,
    piece_hbm,
    table_ref,
    blocks_hbm,
    turned_hbm,
    samples_hbm,
    out_hbm,
    piece,
    blocks,
    turned,
    samples,
    window,
    total,
    spread,
    out,
    sems,
    leave,
):
    count = counts_ref[0]
    if chunk == 0:
        arrival = pltpu.make_async_copy(piece_hbm, piece, leave.at[PER])
        arrival.start()
    else:
        piece = piece_hbm

    def copies(j):
        return [
            pltpu.make_async_copy(blocks_hbm.at[j], blocks.at[j], sems.at[0, j]),
            pltpu.make_async_copy(turned_hbm.at[j], turned.at[j], sems.at[1, j]),
        ] + [
            pltpu.make_async_copy(
                samples_hbm.at[chunk * PER + c, j],
                samples.at[j, :, pl.ds(2 * Z * c, 2 * Z)],
                sems.at[2 + c, j],
            )
            for c in range(PER)
        ]

    def start(j, carry):
        for copy in copies(j):
            copy.start()
        return carry

    lax.fori_loop(0, count, start, 0)

    if chunk == 0:
        arrival.wait()

    for c in range(PER):
        spread[c] = piece[:, c].astype(F32).reshape(ROWS * 2, Z)

    def forward_row(ky, carry):
        data = jnp.concatenate(
            [
                jnp.concatenate(
                    [
                        spread[c, pl.ds(2 * ky + part, N, stride=2 * KYD), :].astype(BF)
                        for part in range(2)
                    ],
                    0,
                )
                for c in range(PER)
            ],
            1,
        )
        result = jnp.dot(table_ref[...], data, preferred_element_type=F32)
        for c in range(PER):
            for part in range(2):
                total[2 * c + part, pl.ds(ky, N, stride=KYD), :] = result[
                    part * N : (part + 1) * N, c * Z : (c + 1) * Z
                ]
        return carry

    lax.fori_loop(0, KYD, forward_row, 0)
    for s in range(2 * PER):
        lanes = slice(s * Z, (s + 1) * Z)
        total[s, ROWS : ROWS + KYD, :] = jnp.zeros((KYD, Z), F32)
        window[0, :, lanes] = total[s, 0:ROWS, :].astype(BF)
        window[1, :, lanes] = total[s, KYD : ROWS + KYD, :].astype(BF)
    total[...] = jnp.zeros_like(total)

    def arrive(j):
        for copy in copies(j):
            copy.wait()

    def predict(j):
        first = offsets_ref[0, j]
        row = pl.multiple_of((first // 2) * (2 * KYD), 2 * KYD)
        view = window[first % 2, pl.ds(row, CELLS), :]
        predicted = jnp.dot(blocks[j], view, preferred_element_type=F32)
        return (predicted - samples[j].astype(F32)).astype(BF)

    def add_back(j, misfit):
        update = jnp.dot(turned[j], misfit, preferred_element_type=F32)
        spot = pl.ds(pl.multiple_of(offsets_ref[0, j] * KYD, KYD), CELLS)
        for s in range(2 * PER):
            total[s, spot, :] = total[s, spot, :] + update[:, s * Z : (s + 1) * Z]

    arrive(0)
    samples[0] = predict(0)

    def group(j, carry):
        arrive(j)
        before = samples[j - 1]
        misfit = predict(j)
        add_back(j - 1, before)
        samples[j] = misfit
        return carry

    lax.fori_loop(1, count, group, 0)
    add_back(count - 1, samples[count - 1])

    leaving = []
    for c in range(PER):

        def inverse_rows(pair, carry):
            data = jnp.concatenate(
                [
                    jnp.concatenate(
                        [
                            conjugate(
                                total[2 * c + part, pl.ds(2 * pair + i, N, stride=KYD), :], part
                            ).astype(BF)
                            for part in range(2)
                        ],
                        0,
                    )
                    for i in range(2)
                ],
                1,
            )
            result = jnp.dot(table_ref[...], data, preferred_element_type=F32)
            for i in range(2):
                for part in range(2):
                    spread[c, pl.ds(2 * (2 * pair + i) + part, N, stride=2 * KYD), :] = conjugate(
                        result[part * N : (part + 1) * N, i * Z : (i + 1) * Z], part
                    )
            return carry

        lax.fori_loop(0, KYD // 2, inverse_rows, 0)
        out[:, c] = spread[c].astype(BF).reshape(TILES, KYD, 16, Z)
        copy = pltpu.make_async_copy(out.at[:, c], out_hbm.at[:, c], leave.at[c])
        copy.start()
        leaving.append(copy)
    for copy in leaving:
        copy.wait()


def grid_tile(chunk, offsets, counts, piece, table, blocks, turned, samples):
    def kernel(*refs):
        grid_kernel(chunk, *refs)

    return pl.pallas_call(
        kernel,
        out_shape=hbm((TILES, PER, KYD, 16, Z), BF),
        in_specs=[SMEM, SMEM, HBM if chunk == 0 else VMEM, VMEM, HBM, HBM, HBM],
        out_specs=HBM,
        scratch_shapes=[
            pltpu.VMEM((TILES, PER, KYD, 16, Z) if chunk == 0 else (16, Z), BF),
            pltpu.VMEM((CH, P_SIZE, CELLS), BF),
            pltpu.VMEM((CH, CELLS, P_SIZE), BF),
            pltpu.VMEM((CH, P_SIZE, 2 * Z * PER), BF),
            pltpu.VMEM((2, ROWS, 2 * Z * PER), BF),
            pltpu.VMEM((2 * PER, ROWS + KYD, Z), F32),
            pltpu.VMEM((PER, 2 * ROWS, Z), F32),
            pltpu.VMEM((TILES, PER, KYD, 16, Z), BF),
            DMA((2 + PER, CH)),
            DMA((PER + 1,)),
        ],
        compiler_params=pltpu.CompilerParams(vmem_limit_bytes=34 << 20),
        name=f"grid_tile_{chunk}",
    )(offsets, counts, piece, table, blocks, turned, samples)


def combine(adjoint, packed):
    g_re = g_im = None
    for pair in range(PER):
        lanes = slice(pair * Z, (pair + 1) * Z)
        a_re = adjoint[:N, lanes]
        a_im = adjoint[N:, lanes]
        s_re, s_im = packed[pair]
        t_re = s_re * a_re + s_im * a_im
        t_im = s_re * a_im - s_im * a_re
        g_re = t_re if g_re is None else g_re + t_re
        g_im = t_im if g_im is None else g_im + t_im
    low = lax.broadcasted_iota(jnp.int32, g_re.shape, 1) < Z // 2
    return jnp.where(low, g_re + pltpu.roll(g_re, Z // 2, 1), g_im + pltpu.roll(g_im, Z // 2, 1))


def adjoint_row(table_ref, piece, x):
    data = jnp.concatenate([piece[:, pair, x].reshape(2 * N, Z) for pair in range(PER)], 1)
    return jnp.dot(table_ref[...], data, preferred_element_type=F32).astype(BF)


def share_copies(position, out, shares, rows, sems):
    return [
        pltpu.make_async_copy(
            out.at[lax.rem(position + k, NCOIL), rows], shares[k].at[rows], sems.at[k]
        )
        for k in range(NCOIL)
    ]


def gradient_first_kernel(position_ref, table_ref, piece_hbm, sens_hbm, *rest):
    shares = rest[:NCOIL]
    later_hbm, piece, sens, later, out, arrive, sems, last = rest[NCOIL:]
    copies = [
        pltpu.make_async_copy(piece_hbm, piece, arrive.at[0]),
        pltpu.make_async_copy(sens_hbm, sens, arrive.at[1]),
    ]
    for copy in copies:
        copy.start()
    for copy in copies:
        copy.wait()

    def row(x, carry):
        packed = []
        for pair in range(PER):
            both = []
            for part in range(2):
                even, odd = (sens[2 * pair + k, part, x] for k in range(2))
                both.append(pack(even, odd, 0).astype(F32))
                later[pair, part, x] = pack(even, odd, 1)
            packed.append(both)
        gradient = combine(adjoint_row(table_ref, piece, x).astype(F32), packed)
        out[:, x] = gradient.astype(BF).reshape(NCOIL, N // NCOIL, Z)
        return carry

    lax.fori_loop(0, KYD, row, 0)
    leaving = share_copies(position_ref[0], out, shares, pl.ds(0, KYD), sems)
    leaving.append(pltpu.make_async_copy(later, later_hbm, last.at[0]))
    for copy in leaving:
        copy.start()
    for copy in leaving:
        copy.wait()


def gradient_first(position, table, piece, sensitivity):
    share = (KYD, N // NCOIL, Z)
    packed = (PER, 2, KYD, N, Z)
    return pl.pallas_call(
        gradient_first_kernel,
        out_shape=(hbm(share, BF),) * NCOIL + (hbm(packed, BF),),
        in_specs=[SMEM, VMEM, HBM, HBM],
        out_specs=(HBM,) * (NCOIL + 1),
        scratch_shapes=[
            pltpu.VMEM((TILES, PER, KYD, 16, Z), BF),
            pltpu.VMEM((NCOIL, 2, KYD, N, Z), BF),
            pltpu.VMEM(packed, BF),
            pltpu.VMEM((NCOIL,) + share, BF),
            DMA((2,)),
            DMA((NCOIL,)),
            DMA((1,)),
        ],
        compiler_params=pltpu.CompilerParams(vmem_limit_bytes=14 << 20),
        name="gradient_first",
    )(position, table, piece, sensitivity)


def gradient_last_kernel(position_ref, table_ref, piece, sens_hbm, *rest):
    shares = rest[:NCOIL]
    sens, adjoint, out, arrive, sems = rest[NCOIL:]
    span = KYD // 2

    def arrivals(stage):
        rows = pl.ds(stage * span, span)
        return pltpu.make_async_copy(
            sens_hbm.at[:, :, rows], sens.at[:, :, rows], arrive.at[stage]
        )

    for stage in range(2):
        arrivals(stage).start()
    leaving = []
    for stage in range(2):
        for x in range(stage * span, (stage + 1) * span):
            adjoint[x] = adjoint_row(table_ref, piece, x)
        arrivals(stage).wait()
        for x in range(stage * span, (stage + 1) * span):
            packed = [
                [sens[pair, part, x].astype(F32) for part in range(2)] for pair in range(PER)
            ]
            gradient = combine(adjoint[x].astype(F32), packed)
            out[:, x] = gradient.astype(BF).reshape(NCOIL, N // NCOIL, Z)
        rows = pl.ds(stage * span, span)
        for copy in share_copies(position_ref[0], out, shares, rows, sems.at[stage]):
            copy.start()
            leaving.append(copy)
    for copy in leaving:
        copy.wait()


def gradient_last(position, table, piece, packed):
    share = (KYD, N // NCOIL, Z)
    return pl.pallas_call(
        gradient_last_kernel,
        out_shape=(hbm(share, BF),) * NCOIL,
        in_specs=[SMEM, VMEM, VMEM, HBM],
        out_specs=(HBM,) * NCOIL,
        scratch_shapes=[
            pltpu.VMEM((PER, 2, KYD, N, Z), BF),
            pltpu.VMEM((KYD, 2 * N, 2 * Z), BF),
            pltpu.VMEM((NCOIL,) + share, BF),
            DMA((2,)),
            DMA((2, NCOIL)),
        ],
        compiler_params=pltpu.CompilerParams(vmem_limit_bytes=10 << 20),
        name="gradient_last",
    )(position, table, piece, packed)


def haar_rows(top, low):
    add = (top + low) * 0.5
    sub = (top - low) * 0.5
    cols = top.shape[0]
    odd = lax.broadcasted_iota(jnp.int32, top.shape, 0) % 2 == 1

    def pairs(v):
        ahead = pltpu.roll(v, cols - 1, 0)
        behind = pltpu.roll(v, 1, 0)
        return jnp.where(odd, behind - v, v + ahead)

    return pairs(add), pairs(sub)


def spread_halves(first, second):
    low = lax.broadcasted_iota(jnp.int32, first.shape, 1) < Z // 2
    return (
        jnp.where(low, first, pltpu.roll(second, Z // 2, 1)),
        jnp.where(low, pltpu.roll(first, Z // 2, 1), second),
    )


def target_kernel(position_ref, image_hbm, aux_ref, dual_ref, *rest):
    early = rest[:NCOIL]
    own_ref, out_ref, image, sem = rest[NCOIL:]
    share = N // NCOIL
    columns = pl.ds(pl.multiple_of(position_ref[0] * share, share), share)
    copy = pltpu.make_async_copy(image_hbm.at[:, :, columns], image, sem)
    copy.start()
    copy.wait()
    for m in range(KYD // 2):
        known = []
        for x in (2 * m, 2 * m + 1):
            total = early[0][x].astype(F32)
            for other in early[1:]:
                total = total + other[x].astype(F32)
            known.append(spread_halves(total, own_ref[x].astype(F32)))
        for part in range(2):
            rows = haar_rows(
                *(aux_ref[part, 2 * m + i] - dual_ref[part, 2 * m + i] for i in range(2))
            )
            for i in range(2):
                current = image[part, 2 * m + i]
                out_ref[part, 2 * m + i] = current - step_size * (
                    known[i][part] + penalty * (current - rows[i])
                )


def target_step(position, image, auxiliary, scaled_dual, early, own):
    return pl.pallas_call(
        target_kernel,
        out_shape=jax.ShapeDtypeStruct(auxiliary.shape, F32),
        in_specs=[SMEM, HBM] + [VMEM] * (NCOIL + 3),
        out_specs=VMEM,
        scratch_shapes=[pltpu.VMEM(auxiliary.shape, F32), DMA],
        compiler_params=pltpu.CompilerParams(vmem_limit_bytes=7 << 20),
        name="target",
    )(position, image, auxiliary, scaled_dual, *early, own)


def update_kernel(base_ref, *rest):
    late = rest[: NCOIL - 1]
    dual_ref, image_hbm, aux_hbm, dual_hbm, image, aux, dual, sems = rest[NCOIL - 1 :]
    low = lax.broadcasted_iota(jnp.int32, (N // NCOIL, Z), 1) < Z // 2
    leaving = []
    for m in range(KYD // 2):
        rows = ([], [])
        for x in (2 * m, 2 * m + 1):
            total = late[0][x].astype(F32)
            for other in late[1:]:
                total = total + other[x].astype(F32)
            zero = jnp.zeros_like(total)
            gradient = (
                jnp.where(low, zero, pltpu.roll(total, Z // 2, 1)),
                jnp.where(low, zero, total),
            )
            for part in range(2):
                value = base_ref[part, x] - step_size * gradient[part]
                image[part, x] = value
                rows[part].append(value)
        pair = pl.ds(2 * m, 2)
        copy = pltpu.make_async_copy(image.at[:, pair], image_hbm.at[:, pair], sems.at[0, m])
        copy.start()
        leaving.append(copy)
        coeffs = []
        for part in range(2):
            top, bottom = haar_rows(*rows[part])
            coeffs.append((top + dual_ref[part, 2 * m], bottom + dual_ref[part, 2 * m + 1]))
        for i in range(2):
            c_re = coeffs[0][i]
            c_im = coeffs[1][i]
            magnitude = jnp.sqrt(c_re * c_re + c_im * c_im)
            factor = jnp.maximum(1.0 - threshold / jnp.maximum(magnitude, threshold), 0.0)
            for part, value in enumerate((c_re, c_im)):
                kept = value * factor
                aux[part, 2 * m + i] = kept
                dual[part, 2 * m + i] = value - kept
        for k, (held, place) in ((1, (aux, aux_hbm)), (2, (dual, dual_hbm))):
            copy = pltpu.make_async_copy(held.at[:, pair], place.at[:, pair], sems.at[k, m])
            copy.start()
            leaving.append(copy)
    for copy in leaving:
        copy.wait()


def update_step(base, late, scaled_dual):
    shape = hbm(scaled_dual.shape, F32)
    return pl.pallas_call(
        update_kernel,
        out_shape=(shape, shape, shape),
        in_specs=[VMEM] * (NCOIL + 1),
        out_specs=(HBM, HBM, HBM),
        scratch_shapes=[pltpu.VMEM(scaled_dual.shape, F32)] * 3 + [DMA((3, KYD // 2))],
        compiler_params=pltpu.CompilerParams(vmem_limit_bytes=8 << 20),
        name="update",
    )(base, *late, scaled_dual)


def over_planes(shares):
    own, *others = shares
    got = [own]
    for k in (2, 1, 3):
        ring = [(i, (i + k) % NCOIL) for i in range(NCOIL)]
        got.append(lax.ppermute(others[k - 1], "coil", ring))
    return got


def body(image, sensitivity, blocks, samples, offsets, counts, auxiliary, scaled_dual):
    along_y, along_x = real_tables()
    y_forward, x_forward = jnp.asarray(along_y), jnp.asarray(along_x)
    y_inverse = lax.optimization_barrier(y_forward).T

    image, sensitivity = in_hbm(image), in_hbm(sensitivity)
    y_forward = in_hbm(y_forward)
    turned = jnp.swapaxes(blocks[0], 1, 2)
    by_coil = samples_by_coil(counts, in_hbm(samples.reshape(CH, P_SIZE, 2 * NCOIL, Z)))

    chunks = range(NCOIL // PER)
    pieces = []
    for chunk in chunks:
        half = coil_forward(chunk, y_forward, sensitivity, image)
        if chunk == 1:
            half, turned, by_coil, y_inverse, pieces[0] = lax.optimization_barrier(
                (half, turned, by_coil, y_inverse, pieces[0])
            )
        piece = lax.all_to_all(half, "slab", 0, 0, tiled=True)
        pieces.append(piece)
    position = lax.axis_index("coil").reshape(1)
    backs = []
    for chunk in chunks:
        back = grid_tile(
            chunk,
            offsets,
            counts,
            in_hbm(pieces[chunk]) if chunk == 0 else pieces[chunk],
            x_forward,
            in_hbm(blocks[0]),
            in_hbm(turned),
            in_hbm(by_coil),
        )
        backs.append(lax.all_to_all(back, "slab", 0, 0, tiled=True))
    *shares, packed = gradient_first(position, y_inverse, in_hbm(backs[0]), sensitivity)
    early = over_planes(shares)
    late = over_planes(gradient_last(position, y_inverse, backs[1], in_hbm(packed)))
    base = target_step(position, image, auxiliary, scaled_dual, early, late[0])
    return update_step(base, late[1:], scaled_dual)


def solution(mesh):
    return jax.shard_map(
        body,
        mesh=mesh,
        in_specs=(
            P(None, "slab", None, None),
            P("coil", None, "slab", None, None),
            P("slab", None, None, None),
            P("slab", None, None, "coil", None, None),
            P("slab", None),
            P("slab"),
            P(None, "slab", "coil", None),
            P(None, "slab", "coil", None),
        ),
        out_specs=(
            P(None, "slab", "coil", None),
            P(None, "slab", "coil", None),
            P(None, "slab", "coil", None),
        ),
        check_vma=False,
    )
```
